32 devices in a mesh: dp: 8 (over y, x, core), ctx: 4 (over z).
Axes of the slice: x: 2, y: 2, z: 4, core: 2. Of those that a mesh axis runs over, the one named last changes fastest.
Arguments:
- inputs: bfloat16 [8, 1024, 1152], P('dp', 'ctx'), may hold values from -6 to 6
- counts: int32 [8], P('dp'), may hold values from 512 to 1024
- params: float32 [1, 15241216], P(None, ('dp', 'ctx')), as said below
- first_moment: float32 [1, 15241216], P(None, ('dp', 'ctx')), may hold values from -60 to 60
- second_moment: float32 [1, 15241216], P(None, ('dp', 'ctx')), may hold values from 10 to 10000
- out_cotangent: float32 [8, 1024, 1152], P('dp', 'ctx'), may hold values from -6 to 6
Outputs:
- output: bfloat16 [8, 1024, 1152], P('dp', 'ctx')
- input_grad: float32 [8, 1024, 1152], P('dp', 'ctx')
- param_grads: float32 [1, 15241216], P(None, ('dp', 'ctx'))
- new_params: float32 [1, 15241216], P(None, ('dp', 'ctx'))
- new_first: float32 [1, 15241216], P(None, ('dp', 'ctx'))
- new_second: float32 [1, 15241216], P(None, ('dp', 'ctx'))
The draws below stay inside these ranges and needn't reach their ends.
Inputs may be any that keep to these rules, and one draw needn't show every extreme that they name: `counts`: valid patch tokens of each image; slots from this count up to 1024 are padding. `params`: laid out as the first step says, zeros in each row's tail.
All inputs are finite; a program needn't handle non-finite values.
Results may differ from the reference program's by a relative error of at most 0.014.
The reference program's roundings to bfloat16 on the way count: a program that leaves them out, or rounds other values in their place, can miss the bound.
Values may be sent and summed in bfloat16 or wider, within the bound.
No kernel may reach another device: no remote copies, remote signals or barrier semaphores. Data moves between devices by JAX's collectives and lax.ppermute only.
A program may use at most 320 MiB of HBM per device.

```python
import functools
import math
import jax
import jax.numpy as jnp
from jax import lax

D = 1152
H = 16
HD = 72
FF = 4304
SEQ = 1024
LAYERS = 1
IMAGES = 8
PFLAT = 15241216


def draw_params(key, part):
    base = jax.random.normal(key, (LAYERS, PFLAT), jnp.float32)
    boost = 1.0
    column = jnp.arange(3 * D)
    qkv_scale = jnp.where(column < 2 * D, boost, 1.0) * D ** (-0.5)
    qkv_part = jnp.broadcast_to(qkv_scale[None, :], (D, 3 * D)).reshape(-1)
    used = 4 * D * D + 2 * D * FF + 8 * D + FF
    vector_scales = [0.2, 0.3, 0.3, 0.3, 0.3, 0.2, 0.3, 0.3]
    scale = jnp.concatenate([qkv_part, jnp.full((D * D,), 6.0 * D ** (-0.5), jnp.float32), jnp.full((D * FF,), D ** (-0.5), jnp.float32), jnp.full((FF * D,), FF ** (-0.5), jnp.float32)] + [jnp.full((D,), value, jnp.float32) for value in vector_scales] + [jnp.full((FF,), 0.3, jnp.float32), jnp.zeros((PFLAT - used,), jnp.float32)])
    gains = [0.0, 0.0, 0.0, 0.0, 0.0, 0.0, 0.0, 0.0]
    gains[0] = 1.0
    gains[5] = 1.0
    offset = jnp.concatenate([jnp.zeros((4 * D * D + 2 * D * FF,), jnp.float32)] + [jnp.full((D,), value, jnp.float32) for value in gains] + [jnp.zeros((FF + PFLAT - used,), jnp.float32)])
    return base * scale[None, :] + offset[None, :]


def with_ends(entries, own_key, smallest, largest):
    longest = entries.shape.index(max(entries.shape))
    spots = []
    for shift in (0, 1):
        where = [jax.random.randint(jax.random.fold_in(own_key, axis), (), 0, length) for axis, length in enumerate(entries.shape)]
        where[longest] = (where[longest] + shift) % entries.shape[longest]
        spots.append(tuple(where))
    return entries.at[spots[0]].set(smallest).at[spots[1]].set(largest)


def block_levels(key, dims, shards, smallest, largest):
    loudness = 1.0
    for position, blocks in shards:
        steps = jax.random.uniform(jax.random.fold_in(jax.random.fold_in(key, 6), position), (blocks,), jnp.float32, smallest / len(shards), largest / len(shards))
        loudness = loudness * jnp.repeat(jnp.exp(steps), dims[position] // blocks).reshape((-1,) + (1,) * (len(dims) - 1 - position))
    return loudness


def centred(key, extent, deviation, bound, cuts=(), held_as=jnp.bfloat16):
    level = block_levels(key, extent, cuts, -0.22, 0.18) if cuts else 1.0
    entries = jax.random.normal(key, extent, jnp.float32) * deviation * level
    return jnp.minimum(jnp.maximum(entries, -bound), bound).astype(held_as)


def setup_inputs(seed: int = 0) -> dict:
    splits = jax.random.split(jax.random.key(seed), 7)
    return {
        "inputs": centred(splits[0], (IMAGES, SEQ, D), 1.0, 6.0, ((0, 8), (1, 4))),
        "counts": with_ends(jax.random.randint(splits[1], (IMAGES,), SEQ // 2, SEQ + 1), jax.random.fold_in(splits[1], 1), SEQ // 2, SEQ).astype(jnp.int32),
        "params": draw_params(jax.random.fold_in(splits[6], 71), 0),
        "first_moment": centred(splits[3], (LAYERS, PFLAT), 10.0, 60.0, ((1, 32),), jnp.float32),
        "second_moment": jnp.clip(jnp.exp(math.log(10000.0) - 6.9077553 * jax.random.uniform(splits[4], (LAYERS, PFLAT), jnp.float32) ** block_levels(splits[4], (LAYERS, PFLAT), ((1, 32),), -0.2, 0.2)), 10.0, 10000.0),
        "out_cotangent": centred(splits[5], (IMAGES, SEQ, D), 1.0, 6.0, ((0, 8), (1, 4)), jnp.float32),
    }


norm_epsilon = 1e-06
beta_one = 0.9
beta_two = 0.95
adam_epsilon = 1e-08
adam_step = 3
rate_matrix = 0.005
rate_vector = 0.1
weight_decay = 0.1
masked_score = -1e+30

def unpack(flat_params):
    lengths = [3 * D * D, D * D, D * FF, FF * D] + [D] * 8 + [FF]
    pieces = []
    offset = 0
    for length in lengths:
        pieces.append(flat_params[offset:offset + length])
        offset = offset + length
    shapes = [(D, 3 * D), (D, D), (D, FF), (FF, D)]
    return [pieces[index].reshape(shapes[index]) for index in range(4)] + pieces[4:]

def pack(parts, total):
    flat_grads = jnp.concatenate([piece.reshape(-1) for piece in parts])
    return jnp.concatenate([flat_grads, jnp.zeros((total - flat_grads.shape[0],), jnp.float32)])

def norm_forward(residual, gain, shift):
    centre = residual - lax.optimization_barrier(jnp.mean(residual, -1, keepdims=True))
    inverse = lax.rsqrt(lax.optimization_barrier(jnp.mean(centre * centre, -1, keepdims=True)) + norm_epsilon)
    unit = centre * inverse
    return (unit * gain + shift, unit, inverse)

def norm_back(grad_normed, unit, inverse, gain):
    scaled = grad_normed * gain
    return inverse * (scaled - lax.optimization_barrier(jnp.mean(scaled, -1, keepdims=True)) - unit * lax.optimization_barrier(jnp.mean(scaled * unit, -1, keepdims=True)))

def split_heads(array):
    return array.reshape(array.shape[0], array.shape[1], H, HD).astype(jnp.float32)

def scores_of(queries, keys, key_valid):
    scores = jnp.einsum('bqhd,bkhd->bhqk', split_heads(queries), split_heads(keys))
    return jnp.where(key_valid[:, None, None, :], scores, masked_score)

def attend(queries, keys, values, key_valid):
    scores = scores_of(queries, keys, key_valid)
    top = lax.optimization_barrier(jnp.max(scores, -1, keepdims=True))
    exponent = jnp.exp(scores - top)
    total = lax.optimization_barrier(jnp.sum(exponent, -1, keepdims=True))
    probs = (exponent / total).astype(jnp.bfloat16)
    log_total = (top + jnp.log(total))[..., 0]
    mixed = jnp.einsum('bhqk,bkhd->bqhd', probs.astype(jnp.float32), split_heads(values))
    return (mixed.reshape(queries.shape[0], queries.shape[1], D).astype(jnp.bfloat16), log_total)

def attend_back(queries, keys, values, key_valid, log_total, grad_mixed):
    probs = jnp.exp(scores_of(queries, keys, key_valid) - log_total[..., None])
    grad_heads = split_heads(grad_mixed)
    grad_probs = jnp.einsum('bqhd,bkhd->bhqk', grad_heads, split_heads(values))
    delta = lax.optimization_barrier(jnp.sum(probs * grad_probs, -1, keepdims=True))
    grad_scores = (probs * (grad_probs - delta)).astype(jnp.bfloat16).astype(jnp.float32)
    grad_query = jnp.einsum('bhqk,bkhd->bqhd', grad_scores, split_heads(keys))
    grad_key = jnp.einsum('bhqk,bqhd->bkhd', grad_scores, split_heads(queries))
    probs_round = probs.astype(jnp.bfloat16).astype(jnp.float32)
    grad_value = jnp.einsum('bhqk,bqhd->bkhd', probs_round, grad_heads)
    batch = queries.shape[0]
    return (grad_query.reshape(batch, queries.shape[1], D), grad_key.reshape(batch, keys.shape[1], D), grad_value.reshape(batch, keys.shape[1], D))

def dense(left, right):
    return jnp.dot(left, right, preferred_element_type=jnp.float32)

def forward_layer(residual, weights, key_valid):
    qkv_weight, out_weight, up_weight, down_weight, gain_one, shift_one, bias_query, bias_value, bias_out, gain_two, shift_two, bias_down, bias_up = [piece.astype(jnp.float32) if piece.ndim == 1 else piece for piece in weights]
    batch, rows = (residual.shape[0], residual.shape[1])
    score_scale = HD ** (-0.5)
    normed, unit_one, inverse_one = norm_forward(residual, gain_one, shift_one)
    normed_round = normed.astype(jnp.bfloat16)
    projected = dense(normed_round.reshape(-1, D), qkv_weight).reshape(batch, rows, 3 * D)
    queries = ((projected[..., :D] + bias_query) * score_scale).astype(jnp.bfloat16)
    keys = projected[..., D:2 * D].astype(jnp.bfloat16)
    values = (projected[..., 2 * D:] + bias_value).astype(jnp.bfloat16)
    mixed, log_total = attend(queries, keys, values, key_valid)
    middle = residual + dense(mixed.reshape(-1, D), out_weight).reshape(batch, rows, D) + bias_out
    normed_two, unit_two, inverse_two = norm_forward(middle, gain_two, shift_two)
    normed_two_round = normed_two.astype(jnp.bfloat16)
    pre_gelu = dense(normed_two_round.reshape(-1, D), up_weight) + bias_up
    activated = jax.nn.gelu(pre_gelu, approximate=True).astype(jnp.bfloat16)
    result = middle + dense(activated, down_weight).reshape(batch, rows, D) + bias_down
    saved = (normed_round, unit_one, inverse_one, queries, keys, values, mixed, log_total, normed_two_round, unit_two, inverse_two, pre_gelu, activated)
    return (result, saved)

def backward_layer(grad_next, weights, saved, key_valid):
    qkv_weight, out_weight, up_weight, down_weight, gain_one, shift_one, bias_query, bias_value, bias_out, gain_two, shift_two, bias_down, bias_up = weights
    normed_round, unit_one, inverse_one, queries, keys, values, mixed, log_total, normed_two_round, unit_two, inverse_two, pre_gelu, activated = saved
    batch, rows = (grad_next.shape[0], grad_next.shape[1])
    score_scale = HD ** (-0.5)
    grad_rows = grad_next.reshape(-1, D)
    grad_bias_down = lax.optimization_barrier(jnp.sum(grad_rows, 0))
    grad_round = grad_rows.astype(jnp.bfloat16)
    grad_down = dense(activated.T, grad_round)
    grad_act = dense(grad_round, down_weight.T)
    gelu_back = jax.vjp(functools.partial(jax.nn.gelu, approximate=True), pre_gelu)[1]
    grad_pre = gelu_back(grad_act)[0]
    grad_bias_up = lax.optimization_barrier(jnp.sum(grad_pre, 0))
    grad_pre_round = grad_pre.astype(jnp.bfloat16)
    grad_up = dense(normed_two_round.reshape(-1, D).T, grad_pre_round)
    grad_normed_two = dense(grad_pre_round, up_weight.T).reshape(batch, rows, D)
    grad_gain_two = lax.optimization_barrier(jnp.sum(grad_normed_two * unit_two, (0, 1)))
    grad_shift_two = lax.optimization_barrier(jnp.sum(grad_normed_two, (0, 1)))
    grad_middle = grad_next + norm_back(grad_normed_two, unit_two, inverse_two, gain_two.astype(jnp.float32))
    grad_bias_out = lax.optimization_barrier(jnp.sum(grad_middle, (0, 1)))
    middle_round = grad_middle.reshape(-1, D).astype(jnp.bfloat16)
    grad_out = dense(mixed.reshape(-1, D).T, middle_round)
    grad_mixed = dense(middle_round, out_weight.T).astype(jnp.bfloat16).reshape(batch, rows, D)
    grad_query, grad_key, grad_value = attend_back(queries, keys, values, key_valid, log_total, grad_mixed)
    grad_query = grad_query * score_scale
    grad_bias_query = lax.optimization_barrier(jnp.sum(grad_query, (0, 1)))
    grad_bias_value = lax.optimization_barrier(jnp.sum(grad_value, (0, 1)))
    grad_projected = jnp.concatenate([grad_query, grad_key, grad_value], -1).reshape(-1, 3 * D).astype(jnp.bfloat16)
    grad_qkv = dense(normed_round.reshape(-1, D).T, grad_projected)
    grad_normed_one = dense(grad_projected, qkv_weight.T).reshape(batch, rows, D)
    grad_gain_one = lax.optimization_barrier(jnp.sum(grad_normed_one * unit_one, (0, 1)))
    grad_shift_one = lax.optimization_barrier(jnp.sum(grad_normed_one, (0, 1)))
    grad_input = grad_middle + norm_back(grad_normed_one, unit_one, inverse_one, gain_one.astype(jnp.float32))
    flat_grads = pack([grad_qkv, grad_out, grad_up, grad_down, grad_gain_one, grad_shift_one, grad_bias_query, grad_bias_value, grad_bias_out, grad_gain_two, grad_shift_two, grad_bias_down, grad_bias_up], PFLAT)
    return (grad_input, flat_grads)

def adam_update(master, grads, first, second, index):
    matrix_part = index < 4 * D * D + 2 * D * FF
    first_new = beta_one * first + (1.0 - beta_one) * grads
    second_new = beta_two * second + (1.0 - beta_two) * grads * grads
    first_hat = first_new / (1.0 - beta_one ** adam_step)
    second_hat = second_new / (1.0 - beta_two ** adam_step)
    rate = jnp.where(matrix_part, rate_matrix, rate_vector)
    decay = jnp.where(matrix_part, weight_decay, 0.0)
    updated = master - rate * (first_hat / (jnp.sqrt(second_hat) + adam_epsilon) + decay * master)
    return (updated, first_new, second_new)

def reference(inputs, counts, params, first_moment, second_moment, out_cotangent):
    weights_all = [unpack(params[layer_index].astype(jnp.bfloat16)) for layer_index in range(LAYERS)]
    group = math.gcd(IMAGES, max(1, 4096 // SEQ))
    rounds = IMAGES // group

    def per_group(carry, batch):
        inputs_group, counts_group, cotangent_group = batch
        positions = jnp.arange(SEQ, dtype=jnp.int32)
        valid = positions[None, :] < counts_group[:, None]
        residual = inputs_group.astype(jnp.float32)
        saved_list = []
        for layer_index in range(LAYERS):
            residual, saved = forward_layer(residual, weights_all[layer_index], valid)
            saved_list.append(saved)
        output = residual.astype(jnp.bfloat16)
        grad = cotangent_group * valid[..., None].astype(jnp.float32)
        flat_list = []
        for layer_index in reversed(range(LAYERS)):
            grad, flat_grads = backward_layer(grad, weights_all[layer_index], saved_list[layer_index], valid)
            flat_list.append(flat_grads)
        flat_list = flat_list[::-1]
        return (carry + jnp.stack(flat_list), (output, grad))
    totals, (outputs, grads) = lax.scan(per_group, jnp.zeros((LAYERS, PFLAT), jnp.float32), (inputs.reshape(rounds, group, SEQ, D), counts.reshape(rounds, group), out_cotangent.reshape(rounds, group, SEQ, D)))
    index = jnp.arange(PFLAT, dtype=jnp.int32)[None, :]
    new_params, new_first, new_second = adam_update(params, totals, first_moment, second_moment, index)
    return (outputs.reshape(IMAGES, SEQ, D), grads.reshape(IMAGES, SEQ, D), totals, new_params, new_first, new_second)
```

```python
import functools
import math

import jax
import jax.numpy as jnp
from jax import lax
from jax.experimental import pallas as pl
from jax.experimental.pallas import tpu as pltpu
from jax.sharding import PartitionSpec as P

D = 1152
H = 16
HD = 72
FF = 4304
LANES = 128
TILE = 16

norm_epsilon = 1e-06
beta_one = 0.9
beta_two = 0.95
adam_epsilon = 1e-08
adam_step = 3
rate_matrix = 0.005
rate_vector = 0.1
weight_decay = 0.1
masked_score = -1e30

BF = jnp.bfloat16
F32 = jnp.float32

QKV_BLOCKS = 3 * D // LANES
D_BLOCKS = D // LANES
ROW_QKV = 0
ROW_OUT = D * QKV_BLOCKS
ROW_UP = ROW_OUT + D * D_BLOCKS
ROW_DOWN = ROW_UP + D * FF // LANES
ROW_VEC = ROW_DOWN + FF * D_BLOCKS
VEC_ROWS = 128
VEC_LENGTHS = [D] * 8 + [FF]

UP_GROUP = LANES // math.gcd(FF, LANES)
UP_STRIDE = UP_GROUP * FF // LANES
UP_BLOCKS = -(-FF // LANES)
UP_TAIL = FF - (UP_BLOCKS - 1) * LANES
STEPS = 9
BLOCK = D // STEPS
DOWN_BLOCK = -(-FF // (STEPS * TILE)) * TILE
VMEM_LIMIT = 60 * 1024 * 1024


class Layout:
    def __init__(self, dp, ctx, shard_length):
        self.dp, self.ctx = dp, ctx
        self.devices = dp * ctx
        self.columns = dp // 2
        self.half = self.columns // 2
        self.rows = shard_length // LANES
        longest = (self.rows + TILE - 1) // TILE
        self.piece = -(-longest // self.columns) * TILE
        self.total = self.rows * self.devices

    def start(self, shard):
        return shard * self.rows // TILE * TILE

    def pieces(self, shard):
        group, within = divmod(shard, 2 * self.ctx)
        found = []
        for column in range(self.columns):
            device = column * 2 * self.ctx + within
            first = self.start(shard) + column * self.piece
            rows = min(self.piece, self.start(shard + 1) - first)
            source = (device * self.half + group % self.half) * self.piece
            if rows > 0:
                found.append((group // self.half, source, first, rows))
        return found

    def covering(self, low, high):
        return [
            shard
            for shard in range(self.devices)
            if self.start(shard) < high and self.start(shard + 1) > low
        ]


def lane_index(rows):
    return lax.broadcasted_iota(jnp.int32, (rows, LANES), 1)


def rows_to_matrix(flat, base, rows, blocks, wide, out):
    wide[pl.ds(0, rows * blocks), :] = flat[pl.ds(base, rows * blocks), :].astype(F32)
    for block in range(blocks):
        part = wide[pl.ds(block, rows, stride=blocks), :]
        out[:, block * LANES : (block + 1) * LANES] = part.astype(BF)


def matrix_to_rows(matrix, rows, blocks, wide, flat, base):
    for block in range(blocks):
        part = matrix[:, block * LANES : (block + 1) * LANES].astype(F32)
        wide[pl.ds(block, rows, stride=blocks), :] = part
    flat[pl.ds(base, rows * blocks), :] = wide[pl.ds(0, rows * blocks), :].astype(BF)


def rows_to_up(flat, base, wide, square, out):
    groups = BLOCK // UP_GROUP
    length = groups * UP_STRIDE
    wide[pl.ds(0, length), :] = flat[pl.ds(base, length), :].astype(F32)
    lanes = lane_index(groups)
    for row in range(UP_GROUP):
        first, shift = divmod(row * FF, LANES)
        held = None
        for block in range(UP_BLOCKS + 1):
            if block == UP_BLOCKS and shift + UP_TAIL <= LANES:
                piece = held
            else:
                piece = wide[pl.ds(first + block, groups, stride=UP_STRIDE), :]
                if shift:
                    piece = pltpu.roll(piece, LANES - shift, 1)
            if block:
                value = jnp.where(lanes < LANES - shift, held, piece) if shift else held
                square[block - 1, pl.ds(row, groups, stride=UP_GROUP), :] = value
            held = piece
    for block in range(UP_BLOCKS):
        first, last = (block * LANES, min(FF, (block + 1) * LANES))
        out[:, first:last] = square[block, :, : last - first].astype(BF)


def up_to_rows(matrix, square, wide, flat, base):
    groups = BLOCK // UP_GROUP
    length = groups * UP_STRIDE
    for block in range(UP_BLOCKS):
        first, last = (block * LANES, min(FF, (block + 1) * LANES))
        square[block, :, : last - first] = matrix[:, first:last].astype(F32)
    lanes = lane_index(groups)
    held = None
    for row in range(UP_GROUP):
        first, shift = divmod(row * FF, LANES)
        for block in range(UP_BLOCKS):
            piece = square[block, pl.ds(row, groups, stride=UP_GROUP), :]
            if shift:
                piece = pltpu.roll(piece, shift, 1)
                value = jnp.where(lanes < shift, held, piece)
            else:
                value = piece
            if block == UP_BLOCKS - 1 and shift + UP_TAIL < LANES:
                held = value
            else:
                wide[pl.ds(first + block, groups, stride=UP_STRIDE), :] = value
                held = piece
    flat[pl.ds(base, length), :] = wide[pl.ds(0, length), :].astype(BF)


def fetch(layout, shards, sources, flat, sem):
    origin = layout.start(shards[0])
    for shard in shards:
        for half, source, first, rows in layout.pieces(shard):
            pltpu.make_async_copy(
                sources[half].at[pl.ds(source, rows), :],
                flat.at[pl.ds(first - origin, rows), :],
                sem,
            ).start()
    whole = flat.at[pl.ds(0, layout.start(shards[-1] + 1) - origin), :]
    pltpu.make_async_copy(whole, whole, sem).wait()


def first_weights(layout, gathered):
    shards = layout.covering(ROW_QKV, ROW_OUT)
    origin = layout.start(shards[0])
    length = layout.start(shards[-1] + 1) - origin

    def kernel(source, qkv, flat, wide, sem):
        step = pl.program_id(0)

        @pl.when(step == 0)
        def _():
            fetch(layout, shards, (source,), flat, sem)

        base = pl.multiple_of(ROW_QKV - origin + step * (BLOCK * QKV_BLOCKS), TILE)
        rows_to_matrix(flat, base, BLOCK, QKV_BLOCKS, wide, qkv)

    return pl.pallas_call(
        kernel,
        name="first_weights",
        grid=(STEPS,),
        in_specs=[pl.BlockSpec(memory_space=pl.ANY)],
        out_specs=pl.BlockSpec((BLOCK, 3 * D), lambda i: (i, 0)),
        out_shape=jax.ShapeDtypeStruct((D, 3 * D), BF),
        scratch_shapes=[
            pltpu.VMEM((length, LANES), BF),
            pltpu.VMEM((BLOCK * QKV_BLOCKS, LANES), F32),
            pltpu.SemaphoreType.DMA,
        ],
        compiler_params=pltpu.CompilerParams(vmem_limit_bytes=VMEM_LIMIT),
    )(gathered)


def other_weights(layout, first_half, second_half):
    shards = layout.covering(ROW_OUT, ROW_VEC)
    origin = layout.start(shards[0])
    length = layout.start(shards[-1] + 1) - origin
    padded = max(length, ROW_DOWN - origin + STEPS * DOWN_BLOCK * D_BLOCKS)
    up_length = BLOCK // UP_GROUP * UP_STRIDE

    def kernel(first, second, out_w, up_w, down_w, flat, wide, square, sem):
        step = pl.program_id(0)

        @pl.when(step == 0)
        def _():
            fetch(layout, shards, (first, second), flat, sem)

        base = pl.multiple_of(ROW_OUT - origin + step * (BLOCK * D_BLOCKS), TILE)
        rows_to_matrix(flat, base, BLOCK, D_BLOCKS, wide, out_w)
        base = pl.multiple_of(ROW_UP - origin + step * up_length, TILE)
        rows_to_up(flat, base, wide, square, up_w)
        base = pl.multiple_of(ROW_DOWN - origin + step * (DOWN_BLOCK * D_BLOCKS), TILE)
        rows_to_matrix(flat, base, DOWN_BLOCK, D_BLOCKS, wide, down_w)

    return pl.pallas_call(
        kernel,
        name="other_weights",
        grid=(STEPS,),
        in_specs=[pl.BlockSpec(memory_space=pl.ANY)] * 2,
        out_specs=[
            pl.BlockSpec((BLOCK, D), lambda i: (i, 0)),
            pl.BlockSpec((BLOCK, FF), lambda i: (i, 0)),
            pl.BlockSpec((DOWN_BLOCK, D), lambda i: (i, 0)),
        ],
        out_shape=[
            jax.ShapeDtypeStruct((D, D), BF),
            jax.ShapeDtypeStruct((D, FF), BF),
            jax.ShapeDtypeStruct((FF, D), BF),
        ],
        scratch_shapes=[
            pltpu.VMEM((padded, LANES), BF),
            pltpu.VMEM((max(up_length + 8, DOWN_BLOCK * D_BLOCKS), LANES), F32),
            pltpu.VMEM((UP_BLOCKS, BLOCK, LANES), F32),
            pltpu.SemaphoreType.DMA,
        ],
        compiler_params=pltpu.CompilerParams(vmem_limit_bytes=VMEM_LIMIT),
    )(first_half, second_half)


def send_pieces(layout, half, origin, flat, out, sem):
    for device in range(layout.devices):
        column, within = divmod(device, 2 * layout.ctx)
        for slot in range(layout.half):
            shard = (half * layout.half + slot) * 2 * layout.ctx + within
            first = layout.start(shard) + column * layout.piece - origin
            target = (device * layout.half + slot) * layout.piece
            pltpu.make_async_copy(
                flat.at[pl.ds(first, layout.piece), :], out.at[pl.ds(target, layout.piece), :], sem
            ).start()
    pltpu.make_async_copy(out, out, sem).wait()


def late_gradients(layout, grad_qkv, grad_out, grad_up):
    count = layout.half * 2 * layout.ctx
    end = layout.start(count - 1) + layout.columns * layout.piece
    up_length = BLOCK // UP_GROUP * UP_STRIDE
    ups = -(-(end - ROW_UP) // up_length)
    padded = ROW_UP + ups * up_length
    rows = layout.devices * layout.half * layout.piece

    def kernel(qkv, out_w, up_w, pieces, flat, wide, square, sem):
        step = pl.program_id(0)
        base = pl.multiple_of(ROW_QKV + step * (BLOCK * QKV_BLOCKS), TILE)
        matrix_to_rows(qkv, BLOCK, QKV_BLOCKS, wide, flat, base)
        base = pl.multiple_of(ROW_OUT + step * (BLOCK * D_BLOCKS), TILE)
        matrix_to_rows(out_w, BLOCK, D_BLOCKS, wide, flat, base)

        @pl.when(step < ups)
        def _():
            base = pl.multiple_of(ROW_UP + step * up_length, TILE)
            up_to_rows(up_w, square, wide, flat, base)

        @pl.when(step == STEPS - 1)
        def _():
            send_pieces(layout, 0, 0, flat, pieces, sem)

    return pl.pallas_call(
        kernel,
        name="late_gradients",
        grid=(STEPS,),
        in_specs=[
            pl.BlockSpec((BLOCK, 3 * D), lambda i: (i, 0)),
            pl.BlockSpec((BLOCK, D), lambda i: (i, 0)),
            pl.BlockSpec((BLOCK, FF), lambda i: (jnp.minimum(i, ups - 1), 0)),
        ],
        out_specs=pl.BlockSpec(memory_space=pl.ANY),
        out_shape=jax.ShapeDtypeStruct((rows, LANES), BF),
        scratch_shapes=[
            pltpu.VMEM((padded, LANES), BF),
            pltpu.VMEM((max(up_length, BLOCK * QKV_BLOCKS), LANES), F32),
            pltpu.VMEM((UP_BLOCKS, BLOCK, LANES), F32),
            pltpu.SemaphoreType.DMA,
        ],
        compiler_params=pltpu.CompilerParams(vmem_limit_bytes=VMEM_LIMIT),
    )(grad_qkv, grad_out, grad_up)


def early_gradients(layout, grad_up, grad_down):
    start = layout.start(layout.half * 2 * layout.ctx)
    end = layout.start(layout.devices - 1) + layout.columns * layout.piece
    up_length = BLOCK // UP_GROUP * UP_STRIDE
    skipped = (start - ROW_UP) // up_length
    origin = ROW_UP + skipped * up_length
    padded = max(end, ROW_DOWN + STEPS * DOWN_BLOCK * D_BLOCKS) - origin
    rows = layout.devices * layout.half * layout.piece

    def kernel(up_w, down_w, pieces, flat, wide, square, sem):
        step = pl.program_id(0)

        @pl.when(step < STEPS - skipped)
        def _():
            base = pl.multiple_of(step * up_length, TILE)
            up_to_rows(up_w, square, wide, flat, base)

        base = pl.multiple_of(ROW_DOWN - origin + step * (DOWN_BLOCK * D_BLOCKS), TILE)
        matrix_to_rows(down_w, DOWN_BLOCK, D_BLOCKS, wide, flat, base)

        @pl.when(step == STEPS - 1)
        def _():
            tail = padded - (ROW_VEC - origin)
            flat[pl.ds(ROW_VEC - origin, tail), :] = jnp.zeros((tail, LANES), BF)
            send_pieces(layout, 1, origin, flat, pieces, sem)

    return pl.pallas_call(
        kernel,
        name="early_gradients",
        grid=(STEPS,),
        in_specs=[
            pl.BlockSpec((BLOCK, FF), lambda i: (jnp.minimum(i + skipped, STEPS - 1), 0)),
            pl.BlockSpec((DOWN_BLOCK, D), lambda i: (i, 0)),
        ],
        out_specs=pl.BlockSpec(memory_space=pl.ANY),
        out_shape=jax.ShapeDtypeStruct((rows, LANES), BF),
        scratch_shapes=[
            pltpu.VMEM((padded, LANES), BF),
            pltpu.VMEM((max(up_length, DOWN_BLOCK * D_BLOCKS), LANES), F32),
            pltpu.VMEM((UP_BLOCKS, BLOCK, LANES), F32),
            pltpu.SemaphoreType.DMA,
        ],
        compiler_params=pltpu.CompilerParams(vmem_limit_bytes=VMEM_LIMIT),
    )(grad_up, grad_down)


def dot_t(left, right):
    return lax.dot_general(left, right, (((1,), (1,)), ((), ())), preferred_element_type=F32)


def t_dot(left, right):
    return lax.dot_general(left, right, (((0,), (0,)), ((), ())), preferred_element_type=F32)


def dense(left, right):
    return jnp.dot(left, right, preferred_element_type=F32)


def masked(scores, count):
    columns = lax.broadcasted_iota(jnp.int32, scores.shape, 1)
    return jnp.where(columns < count, scores, masked_score)


def attend(counts, queries, keys, values, chunk):
    heads, length, _ = queries.shape

    def kernel(count, q, k, v, mixed, log_total):
        for first in range(0, length, chunk):
            scores = masked(dot_t(q[0, first : first + chunk, :], k[0]), count[0])
            top = jnp.max(scores, -1, keepdims=True)
            exponent = jnp.exp(scores - top)
            total = jnp.sum(exponent, -1, keepdims=True)
            probs = (exponent / total).astype(BF)
            mixed[0, first : first + chunk, :] = dense(probs, v[0]).astype(BF)
            log_total[0, first : first + chunk, :] = top + jnp.log(total)

    spec = pl.BlockSpec((1, length, HD), lambda h: (h, 0, 0))
    return pl.pallas_call(
        kernel,
        name="attend",
        grid=(heads,),
        in_specs=[pl.BlockSpec(memory_space=pltpu.SMEM), spec, spec, spec],
        out_specs=[spec, pl.BlockSpec((1, length, 1), lambda h: (h, 0, 0))],
        out_shape=[
            jax.ShapeDtypeStruct((heads, length, HD), BF),
            jax.ShapeDtypeStruct((heads, length, 1), F32),
        ],
        compiler_params=pltpu.CompilerParams(vmem_limit_bytes=VMEM_LIMIT),
    )(counts, queries, keys, values)


def attend_back(counts, queries, keys, values, log_total, grad_mixed, chunk):
    heads, length, _ = queries.shape
    scale = HD ** (-0.5)

    def kernel(count, q, k, v, logs, grad, dq, dk, dv, sum_q, sum_v, acc_k, acc_v):
        acc_k[...] = jnp.zeros_like(acc_k)
        acc_v[...] = jnp.zeros_like(acc_v)
        total_q = jnp.zeros((1, HD), F32)
        for first in range(0, length, chunk):
            part = slice(first, first + chunk)
            scores = masked(dot_t(q[0, part, :], k[0]), count[0])
            probs = jnp.exp(scores - logs[0, part, :])
            grad_probs = dot_t(grad[0, part, :], v[0])
            delta = jnp.sum(probs * grad_probs, -1, keepdims=True)
            grad_scores = (probs * (grad_probs - delta)).astype(BF)
            grad_query = dense(grad_scores, k[0]) * scale
            total_q = total_q + jnp.sum(grad_query, 0, keepdims=True)
            dq[0, part, :] = grad_query.astype(BF)
            acc_k[...] += t_dot(grad_scores, q[0, part, :])
            acc_v[...] += t_dot(probs.astype(BF), grad[0, part, :])
        dk[0] = acc_k[...].astype(BF)
        dv[0] = acc_v[...].astype(BF)
        sum_q[0] = total_q
        sum_v[0] = jnp.sum(acc_v[...], 0, keepdims=True)

    spec = pl.BlockSpec((1, length, HD), lambda h: (h, 0, 0))
    row = pl.BlockSpec((1, 1, HD), lambda h: (h, 0, 0))
    return pl.pallas_call(
        kernel,
        name="attend_back",
        grid=(heads,),
        in_specs=[
            pl.BlockSpec(memory_space=pltpu.SMEM),
            spec,
            spec,
            spec,
            pl.BlockSpec((1, length, 1), lambda h: (h, 0, 0)),
            spec,
        ],
        out_specs=[spec, spec, spec, row, row],
        out_shape=[jax.ShapeDtypeStruct((heads, length, HD), BF)] * 3
        + [jax.ShapeDtypeStruct((heads, 1, HD), F32)] * 2,
        scratch_shapes=[pltpu.VMEM((length, HD), F32)] * 2,
        compiler_params=pltpu.CompilerParams(vmem_limit_bytes=VMEM_LIMIT),
    )(counts, queries, keys, values, log_total, grad_mixed)


def norm_forward(residual):
    centre = residual - jnp.mean(residual, -1, keepdims=True)
    inverse = lax.rsqrt(jnp.mean(centre * centre, -1, keepdims=True) + norm_epsilon)
    return (centre * inverse, inverse)


def norm_back(grad_normed, unit, inverse, gain):
    scaled = grad_normed * gain
    return inverse * (
        scaled
        - jnp.mean(scaled, -1, keepdims=True)
        - unit * jnp.mean(scaled * unit, -1, keepdims=True)
    )


def adam_update(master, grads, first, second, index):
    matrix_part = index < 4 * D * D + 2 * D * FF
    first_new = beta_one * first + (1.0 - beta_one) * grads
    second_new = beta_two * second + (1.0 - beta_two) * grads * grads
    first_hat = first_new / (1.0 - beta_one**adam_step)
    second_hat = second_new / (1.0 - beta_two**adam_step)
    rate = jnp.where(matrix_part, rate_matrix, rate_vector)
    decay = jnp.where(matrix_part, weight_decay, 0.0)
    updated = master - rate * (first_hat / (jnp.sqrt(second_hat) + adam_epsilon) + decay * master)
    return (updated, first_new, second_new)


def to_heads(array, parts):
    ctx = lax.axis_size("ctx")
    rows = array.shape[0]
    split = array.reshape(rows, parts, ctx, D // ctx).transpose(2, 0, 1, 3)
    held = lax.all_to_all(split, "ctx", split_axis=0, concat_axis=0, tiled=True)
    held = held.reshape(rows * ctx, parts, H // ctx, HD).transpose(1, 2, 0, 3)
    return [held[part] for part in range(parts)]


def from_heads(arrays):
    ctx = lax.axis_size("ctx")
    parts, (heads, length, _) = (len(arrays), arrays[0].shape)
    stacked = jnp.stack(arrays).reshape(parts, heads, ctx, length // ctx, HD)
    split = stacked.transpose(2, 3, 0, 1, 4).reshape(ctx, length // ctx, parts, heads * HD)
    held = lax.all_to_all(split, "ctx", split_axis=0, concat_axis=0, tiled=True)
    return held.transpose(1, 2, 0, 3).reshape(length // ctx, parts * D)


def column_groups(layout):
    return [[column * 2 + core for column in range(layout.columns)] for core in range(2)]


def spread_weights(layout, flat, shard, everyone):
    last = layout.devices - 1
    before = lax.ppermute(
        flat[-TILE:], ("dp", "ctx"), [(index, index + 1) for index in range(last)]
    )
    length = layout.columns * layout.piece
    padded = jnp.concatenate([before, flat, jnp.zeros((length - layout.rows, LANES), BF)])
    offset = (shard * layout.rows) % TILE
    chunk = lax.dynamic_slice(padded, (TILE - offset, 0), (length, LANES))
    pieces = chunk.reshape(layout.columns, layout.piece, LANES)
    held = lax.all_to_all(
        pieces, "dp", split_axis=0, concat_axis=0, tiled=True, axis_index_groups=everyone
    )
    halves = held.reshape(2, layout.half * layout.piece, LANES)
    return (halves[0], halves[1])


def broadcast_vectors(layout, flat):
    first = ROW_VEC - (layout.devices - 1) * layout.rows
    assert 0 <= first and first + VEC_ROWS <= layout.rows
    held = flat[first : first + VEC_ROWS]
    for axis, size in (("dp", layout.dp), ("ctx", layout.ctx)):
        bit = 1
        while bit < size:
            other = lax.ppermute(held, axis, [(index, index ^ bit) for index in range(size)])
            mine = (lax.axis_index(axis) & bit) != 0
            held = jnp.where(mine, held, other)
            bit *= 2
    flat_vectors = held.reshape(-1).astype(F32)
    vectors = []
    offset = 0
    for length in VEC_LENGTHS:
        vectors.append(flat_vectors[offset : offset + length])
        offset += length
    return vectors


def scatter_half(pieces):
    partial = lax.psum_scatter(pieces, "dp", scatter_dimension=0, tiled=True)
    return lax.psum_scatter(partial, "ctx", scatter_dimension=0, tiled=True)


def shards(layout, inputs, counts, params, first_moment, second_moment, out_cotangent):
    local_rows = inputs.shape[1]
    shard = lax.axis_index(("dp", "ctx"))
    score_scale = HD ** (-0.5)
    everyone = column_groups(layout)
    chunk = 256

    flat = params.reshape(layout.rows, LANES).astype(BF)
    share_one, share_two = spread_weights(layout, flat, shard, everyone)
    half_one = lax.all_gather(share_one, ("dp", "ctx"), axis=0, tiled=True)
    half_two = lax.all_gather(share_two, ("dp", "ctx"), axis=0, tiled=True)
    (
        gain_one,
        shift_one,
        bias_query,
        bias_value,
        bias_out,
        gain_two,
        shift_two,
        bias_down,
        bias_up,
    ) = broadcast_vectors(layout, flat)

    residual = inputs[0].astype(F32)
    unit_one, inverse_one = norm_forward(residual)
    normed_round = (unit_one * gain_one + shift_one).astype(BF)
    qkv_weight = first_weights(layout, half_one)
    projected = dense(normed_round, qkv_weight)
    queries = ((projected[:, :D] + bias_query) * score_scale).astype(BF)
    keys = projected[:, D : 2 * D].astype(BF)
    values = (projected[:, 2 * D :] + bias_value).astype(BF)
    queries, keys, values = to_heads(jnp.concatenate([queries, keys, values], -1), 3)
    out_weight, up_weight, down_weight = other_weights(layout, half_one, half_two)
    mixed_heads, log_total = attend(counts, queries, keys, values, chunk)
    mixed = from_heads([mixed_heads])
    middle = residual + dense(mixed, out_weight) + bias_out
    unit_two, inverse_two = norm_forward(middle)
    normed_two_round = (unit_two * gain_two + shift_two).astype(BF)
    pre_gelu = dense(normed_two_round, up_weight) + bias_up
    activated = jax.nn.gelu(pre_gelu, approximate=True).astype(BF)
    output = (middle + dense(activated, down_weight) + bias_down).astype(BF)

    positions = lax.axis_index("ctx") * local_rows + jnp.arange(local_rows, dtype=jnp.int32)
    row_valid = (positions < counts[0])[:, None].astype(F32)
    grad_next = out_cotangent[0] * row_valid
    grad_bias_down = jnp.sum(grad_next, 0)
    grad_round = grad_next.astype(BF)
    grad_down = t_dot(activated, grad_round).astype(BF)
    grad_act = dot_t(grad_round, down_weight)
    gelu_back = jax.vjp(functools.partial(jax.nn.gelu, approximate=True), pre_gelu)[1]
    grad_pre = gelu_back(grad_act)[0]
    grad_bias_up = jnp.sum(grad_pre, 0)
    grad_pre_round = grad_pre.astype(BF)
    grad_up = t_dot(normed_two_round, grad_pre_round).astype(BF)
    half_two_sum = scatter_half(early_gradients(layout, grad_up, grad_down))
    grad_normed_two = dot_t(grad_pre_round, up_weight)
    grad_gain_two = jnp.sum(grad_normed_two * unit_two, 0)
    grad_shift_two = jnp.sum(grad_normed_two, 0)
    grad_middle = grad_next + norm_back(grad_normed_two, unit_two, inverse_two, gain_two)
    grad_bias_out = jnp.sum(grad_middle, 0)
    middle_round = grad_middle.astype(BF)
    grad_out = t_dot(mixed, middle_round).astype(BF)
    grad_mixed = dot_t(middle_round, out_weight).astype(BF)
    (grad_mixed_heads,) = to_heads(grad_mixed, 1)
    grad_q, grad_k, grad_v, sum_q, sum_v = attend_back(
        counts, queries, keys, values, log_total, grad_mixed_heads, chunk
    )
    grad_projected = from_heads([grad_q, grad_k, grad_v])
    grad_qkv = t_dot(normed_round, grad_projected).astype(BF)
    half_one_sum = scatter_half(late_gradients(layout, grad_qkv, grad_out, grad_up))
    grad_normed_one = dot_t(grad_projected, qkv_weight)
    grad_gain_one = jnp.sum(grad_normed_one * unit_one, 0)
    grad_shift_one = jnp.sum(grad_normed_one, 0)
    input_grad = grad_middle + norm_back(grad_normed_one, unit_one, inverse_one, gain_one)

    share = D // layout.ctx
    place = (lax.axis_index("ctx") * share,)
    grad_bias_query = lax.dynamic_update_slice(jnp.zeros((D,), F32), sum_q.reshape(-1), place)
    grad_bias_value = lax.dynamic_update_slice(jnp.zeros((D,), F32), sum_v.reshape(-1), place)
    vector_terms = [
        grad_gain_one,
        grad_shift_one,
        grad_bias_query,
        grad_bias_value,
        grad_bias_out,
        grad_gain_two,
        grad_shift_two,
        grad_bias_down,
        grad_bias_up,
    ]
    padding = jnp.zeros((VEC_ROWS * LANES - sum(VEC_LENGTHS),), F32)
    vector_grads = lax.psum(jnp.concatenate(vector_terms + [padding]), ("dp", "ctx"))

    summed = jnp.concatenate([half_one_sum, half_two_sum])
    held = lax.all_to_all(
        summed.reshape(layout.columns, layout.piece, LANES),
        "dp",
        split_axis=0,
        concat_axis=0,
        tiled=True,
        axis_index_groups=everyone,
    )
    offset = (shard * layout.rows) % TILE
    rows = lax.dynamic_slice(
        held.reshape(-1, LANES).astype(F32), (offset, 0), (layout.rows, LANES)
    )
    first = ROW_VEC - (layout.devices - 1) * layout.rows
    with_vectors = lax.dynamic_update_slice(
        rows, vector_grads.reshape(VEC_ROWS, LANES), (first, 0)
    )
    rows = jnp.where(shard == layout.devices - 1, with_vectors, rows)
    param_grads = rows.reshape(params.shape)
    index = (shard * params.shape[1] + jnp.arange(params.shape[1], dtype=jnp.int32))[None, :]
    new_params, new_first, new_second = adam_update(
        params, param_grads, first_moment, second_moment, index
    )
    return (output[None], input_grad[None], param_grads, new_params, new_first, new_second)


def solution(mesh):
    placed = (
        P("dp", "ctx", None),
        P("dp"),
        P(None, ("dp", "ctx")),
        P(None, ("dp", "ctx")),
        P(None, ("dp", "ctx")),
        P("dp", "ctx", None),
    )
    dp, ctx = (mesh.shape["dp"], mesh.shape["ctx"])

    def program(inputs, counts, params, first_moment, second_moment, out_cotangent):
        layout = Layout(dp, ctx, params.shape[1] // (dp * ctx))
        return jax.shard_map(
            functools.partial(shards, layout),
            mesh=mesh,
            in_specs=placed,
            out_specs=(
                P("dp", "ctx", None),
                P("dp", "ctx", None),
                P(None, ("dp", "ctx")),
                P(None, ("dp", "ctx")),
                P(None, ("dp", "ctx")),
                P(None, ("dp", "ctx")),
            ),
            check_vma=False,
        )(inputs, counts, params, first_moment, second_moment, out_cotangent)

    return program
```

```python
import functools
import math

import jax
import jax.numpy as jnp
from jax import lax
from jax.experimental import pallas as pl
from jax.experimental.pallas import tpu as pltpu
from jax.sharding import PartitionSpec as P

D = 1152
H = 16
HD = 72
FF = 4304
LANES = 128
TILE = 16

norm_epsilon = 1e-06
beta_one = 0.9
beta_two = 0.95
adam_epsilon = 1e-08
adam_step = 3
rate_matrix = 0.005
rate_vector = 0.1
weight_decay = 0.1
masked_score = -1e30

BF = jnp.bfloat16
F32 = jnp.float32

QKV_BLOCKS = 3 * D // LANES
D_BLOCKS = D // LANES
ROW_QKV = 0
ROW_OUT = D * QKV_BLOCKS
ROW_UP = ROW_OUT + D * D_BLOCKS
ROW_DOWN = ROW_UP + D * FF // LANES
ROW_VEC = ROW_DOWN + FF * D_BLOCKS
VEC_ROWS = 128
VEC_LENGTHS = [D] * 8 + [FF]

UP_GROUP = LANES // math.gcd(FF, LANES)
UP_STRIDE = UP_GROUP * FF // LANES
UP_BLOCKS = -(-FF // LANES)
UP_TAIL = FF - (UP_BLOCKS - 1) * LANES
STEPS = 9
BLOCK = D // STEPS
DOWN_BLOCK = -(-FF // (STEPS * TILE)) * TILE
VMEM_LIMIT = 60 * 1024 * 1024


class Layout:
    def __init__(self, dp, ctx, shard_length):
        self.dp, self.ctx = dp, ctx
        self.devices = dp * ctx
        self.columns = dp // 2
        self.rows = shard_length // LANES
        longest = (self.rows + TILE - 1) // TILE
        self.piece = -(-longest // self.columns) * TILE
        self.group_shards = 2 * ctx
        self.first = ROW_OUT // (self.group_shards * self.rows)
        self.last_piece = self.rows // TILE * TILE - (self.columns - 1) * self.piece
        assert self.first > 0 and self.last_piece > 0

    def start(self, shard):
        return shard * self.rows // TILE * TILE

    def group_start(self, group):
        return self.start(group * self.group_shards)

    def group_end(self, group):
        return self.start(group * self.group_shards - 1) + self.columns * self.piece

    def leftover(self):
        shard = self.first * self.group_shards
        found = []
        while self.start(shard) < ROW_OUT:
            found.append((shard, min(ROW_OUT, self.start(shard + 1)) - self.start(shard)))
            shard += 1
        return found


def lane_index(rows):
    return lax.broadcasted_iota(jnp.int32, (rows, LANES), 1)


def rows_to_matrix(flat, base, rows, blocks, wide, out):
    wide[pl.ds(0, rows * blocks), :] = flat[pl.ds(base, rows * blocks), :].astype(F32)
    for block in range(blocks):
        part = wide[pl.ds(block, rows, stride=blocks), :]
        out[:, block * LANES : (block + 1) * LANES] = part.astype(BF)


def matrix_to_rows(matrix, rows, blocks, wide, flat, base):
    for block in range(blocks):
        part = matrix[:, block * LANES : (block + 1) * LANES].astype(F32)
        wide[pl.ds(block, rows, stride=blocks), :] = part
    flat[pl.ds(base, rows * blocks), :] = wide[pl.ds(0, rows * blocks), :].astype(BF)


def rows_to_up(flat, base, wide, square, out):
    groups = BLOCK // UP_GROUP
    length = groups * UP_STRIDE
    wide[pl.ds(0, length), :] = flat[pl.ds(base, length), :].astype(F32)
    lanes = lane_index(groups)
    for row in range(UP_GROUP):
        first, shift = divmod(row * FF, LANES)
        held = None
        for block in range(UP_BLOCKS + 1):
            if block == UP_BLOCKS and shift + UP_TAIL <= LANES:
                piece = held
            else:
                piece = wide[pl.ds(first + block, groups, stride=UP_STRIDE), :]
                if shift:
                    piece = pltpu.roll(piece, LANES - shift, 1)
            if block:
                value = jnp.where(lanes < LANES - shift, held, piece) if shift else held
                square[block - 1, pl.ds(row, groups, stride=UP_GROUP), :] = value
            held = piece
    for block in range(UP_BLOCKS):
        first, last = (block * LANES, min(FF, (block + 1) * LANES))
        out[:, first:last] = square[block, :, : last - first].astype(BF)


def up_to_rows(matrix, square, wide, flat, base):
    groups = BLOCK // UP_GROUP
    length = groups * UP_STRIDE
    for block in range(UP_BLOCKS):
        first, last = (block * LANES, min(FF, (block + 1) * LANES))
        square[block, :, : last - first] = matrix[:, first:last].astype(F32)
    lanes = lane_index(groups)
    held = None
    for row in range(UP_GROUP):
        first, shift = divmod(row * FF, LANES)
        for block in range(UP_BLOCKS):
            piece = square[block, pl.ds(row, groups, stride=UP_GROUP), :]
            if shift:
                piece = pltpu.roll(piece, shift, 1)
                value = jnp.where(lanes < shift, held, piece)
            else:
                value = piece
            if block == UP_BLOCKS - 1 and shift + UP_TAIL < LANES:
                held = value
            else:
                wide[pl.ds(first + block, groups, stride=UP_STRIDE), :] = value
                held = piece
    flat[pl.ds(base, length), :] = wide[pl.ds(0, length), :].astype(BF)


def fetch(layout, place, groups, origin, sources, flat, sem):
    low, high = groups
    count = high - low
    for ref, (column, core, first_row, members) in sources:
        device_column = jnp.bitwise_xor(place[0], column)
        device_core = jnp.bitwise_xor(place[1], core)

        def body(index, _, ref=ref, first_row=first_row):
            row = jnp.bitwise_xor(place[2], first_row + index // count)
            group = low + index % count
            shard = group * layout.group_shards + device_core * layout.ctx + row
            start = shard * layout.rows // TILE * TILE
            target = pl.multiple_of(start + device_column * layout.piece - origin, TILE)
            source = pl.multiple_of(index * layout.piece, TILE)

            def copy(offset, rows):
                pltpu.make_async_copy(
                    ref.at[pl.ds(source + offset, rows), :],
                    flat.at[pl.ds(target + offset, rows), :],
                    sem,
                ).start()

            is_last = device_column == layout.columns - 1
            longer = shard * layout.rows % TILE + layout.rows % TILE >= TILE

            @pl.when(jnp.logical_not(is_last))
            def _():
                copy(0, layout.piece)

            @pl.when(is_last)
            def _():
                copy(0, layout.last_piece)

            @pl.when(jnp.logical_and(is_last, longer))
            def _():
                copy(layout.last_piece, TILE)

            return 0

        lax.fori_loop(0, members * count, body, 0)


def flat_of(gathered):
    return [array for array, _ in gathered]


def first_weights(layout, place, gathered, leftover):
    inside = layout.group_start(layout.first)
    length = inside + leftover.shape[0]
    assert length == ROW_OUT
    arrays = flat_of(gathered)

    def kernel(place_ref, *refs):
        sources, (extra, qkv, flat, wide, sem) = (refs[: len(arrays)], refs[len(arrays) :])
        step = pl.program_id(0)

        @pl.when(step == 0)
        def _():
            named = [(ref, entry) for ref, (_, entry) in zip(sources, gathered)]
            fetch(layout, place_ref, (0, layout.first), 0, named, flat, sem)
            pltpu.make_async_copy(
                extra, flat.at[pl.ds(inside, leftover.shape[0]), :], sem
            ).start()
            pltpu.make_async_copy(flat, flat, sem).wait()

        base = pl.multiple_of(step * (BLOCK * QKV_BLOCKS), TILE)
        rows_to_matrix(flat, base, BLOCK, QKV_BLOCKS, wide, qkv)

    return pl.pallas_call(
        kernel,
        name="first_weights",
        grid=(STEPS,),
        in_specs=[pl.BlockSpec(memory_space=pltpu.SMEM)]
        + [pl.BlockSpec(memory_space=pl.ANY)] * (len(arrays) + 1),
        out_specs=pl.BlockSpec((BLOCK, 3 * D), lambda i: (i, 0)),
        out_shape=jax.ShapeDtypeStruct((D, 3 * D), BF),
        scratch_shapes=[
            pltpu.VMEM((length, LANES), BF),
            pltpu.VMEM((BLOCK * QKV_BLOCKS, LANES), F32),
            pltpu.SemaphoreType.DMA,
        ],
        compiler_params=pltpu.CompilerParams(vmem_limit_bytes=VMEM_LIMIT),
    )(place, *arrays, leftover)


def other_weights(layout, place, gathered):
    origin = layout.group_start(layout.first)
    length = layout.start(layout.devices) - origin
    padded = max(length, ROW_DOWN - origin + STEPS * DOWN_BLOCK * D_BLOCKS)
    up_length = BLOCK // UP_GROUP * UP_STRIDE
    arrays = flat_of(gathered)

    def kernel(place_ref, *refs):
        sources = refs[: len(arrays)]
        out_w, up_w, down_w, flat, wide, square, sem = refs[len(arrays) :]
        step = pl.program_id(0)

        @pl.when(step == 0)
        def _():
            named = [(ref, entry) for ref, (_, entry) in zip(sources, gathered)]
            fetch(layout, place_ref, (layout.first, layout.columns), origin, named, flat, sem)
            whole = flat.at[pl.ds(0, length), :]
            pltpu.make_async_copy(whole, whole, sem).wait()

        base = pl.multiple_of(ROW_OUT - origin + step * (BLOCK * D_BLOCKS), TILE)
        rows_to_matrix(flat, base, BLOCK, D_BLOCKS, wide, out_w)
        base = pl.multiple_of(ROW_UP - origin + step * up_length, TILE)
        rows_to_up(flat, base, wide, square, up_w)
        base = pl.multiple_of(ROW_DOWN - origin + step * (DOWN_BLOCK * D_BLOCKS), TILE)
        rows_to_matrix(flat, base, DOWN_BLOCK, D_BLOCKS, wide, down_w)

    return pl.pallas_call(
        kernel,
        name="other_weights",
        grid=(STEPS,),
        in_specs=[pl.BlockSpec(memory_space=pltpu.SMEM)]
        + [pl.BlockSpec(memory_space=pl.ANY)] * len(arrays),
        out_specs=[
            pl.BlockSpec((BLOCK, D), lambda i: (i, 0)),
            pl.BlockSpec((BLOCK, FF), lambda i: (i, 0)),
            pl.BlockSpec((DOWN_BLOCK, D), lambda i: (i, 0)),
        ],
        out_shape=[
            jax.ShapeDtypeStruct((D, D), BF),
            jax.ShapeDtypeStruct((D, FF), BF),
            jax.ShapeDtypeStruct((FF, D), BF),
        ],
        scratch_shapes=[
            pltpu.VMEM((padded, LANES), BF),
            pltpu.VMEM((max(up_length + 8, DOWN_BLOCK * D_BLOCKS), LANES), F32),
            pltpu.VMEM((UP_BLOCKS, BLOCK, LANES), F32),
            pltpu.SemaphoreType.DMA,
        ],
        compiler_params=pltpu.CompilerParams(vmem_limit_bytes=VMEM_LIMIT),
    )(place, *arrays)


MATRICES = {
    "qkv": (ROW_QKV, BLOCK, BLOCK * QKV_BLOCKS, 3 * D),
    "out": (ROW_OUT, BLOCK, BLOCK * D_BLOCKS, D),
    "up": (ROW_UP, BLOCK, BLOCK // UP_GROUP * UP_STRIDE, FF),
    "down": (ROW_DOWN, DOWN_BLOCK, DOWN_BLOCK * D_BLOCKS, D),
}


def gradient_pieces(layout, place, groups, matrices, leftover=False):
    low, high = layout.group_start(groups[0]), layout.group_end(groups[1])
    count = groups[1] - groups[0]
    names = list(matrices)
    plan = {}
    for name in names:
        first, _, stride, _ = MATRICES[name]
        blocks = [
            block
            for block in range(STEPS)
            if leftover
            or (first + block * stride < high and first + (block + 1) * stride > low)
        ]
        plan[name] = (first, blocks[0], len(blocks), stride)
    origin = min([low] + [first + b * stride for first, b, _, stride in plan.values()])
    end = max([high] + [first + (b + n) * stride for first, b, n, stride in plan.values()])
    steps = max(n for _, _, n, _ in plan.values())
    covered = min(first + b * stride for first, b, _, stride in plan.values())
    rows = layout.devices * count * layout.piece
    extra = ROW_OUT - layout.group_start(layout.first)

    def kernel(place_ref, *refs):
        inputs, refs = (refs[: len(names)], refs[len(names) :])
        outputs, (flat, wide, square, sem) = (refs[:-4], refs[-4:])
        step = pl.program_id(0)
        if covered > low:

            @pl.when(step == 0)
            def _():
                flat[pl.ds(low - origin, covered - low), :] = jnp.zeros((covered - low, LANES), BF)

        for ref, name in zip(inputs, names):
            first, block, number, stride = plan[name]

            def convert(ref=ref, name=name, first=first, block=block, stride=stride):
                base = pl.multiple_of(first - origin + (block + step) * stride, TILE)
                if name == "up":
                    up_to_rows(ref, square, wide, flat, base)
                else:
                    blocks = QKV_BLOCKS if name == "qkv" else D_BLOCKS
                    matrix_to_rows(ref, stride // blocks, blocks, wide, flat, base)

            if number == steps:
                convert()
            else:
                pl.when(step < number)(convert)

        @pl.when(step == steps - 1)
        def _():
            if "down" in names:
                tail = end - ROW_VEC
                flat[pl.ds(ROW_VEC - origin, tail), :] = jnp.zeros((tail, LANES), BF)

            def body(index, _):
                group = groups[0] + index % count
                key = index // count
                row = jnp.bitwise_xor(place_ref[2], key % layout.ctx)
                key = key // layout.ctx
                column = jnp.bitwise_xor(place_ref[0], key % layout.columns)
                core = jnp.bitwise_xor(place_ref[1], key // layout.columns)
                shard = group * layout.group_shards + core * layout.ctx + row
                start = shard * layout.rows // TILE * TILE
                source = pl.multiple_of(start + column * layout.piece - origin, TILE)
                target = pl.multiple_of(index * layout.piece, TILE)
                pltpu.make_async_copy(
                    flat.at[pl.ds(source, layout.piece), :],
                    outputs[0].at[pl.ds(target, layout.piece), :],
                    sem,
                ).start()
                return 0

            lax.fori_loop(0, layout.devices * count, body, 0)
            pltpu.make_async_copy(outputs[0], outputs[0], sem).wait()
            if leftover:
                copy = pltpu.make_async_copy(
                    flat.at[pl.ds(ROW_OUT - extra - origin, extra), :], outputs[1], sem
                )
                copy.start()
                copy.wait()

    def spec(name):
        _, block, number, _ = plan[name]
        _, height, _, width = MATRICES[name]
        return pl.BlockSpec(
            (height, width), lambda i: (block + jnp.minimum(i, number - 1), 0)
        )

    shapes = [jax.ShapeDtypeStruct((rows, LANES), BF)]
    if leftover:
        shapes.append(jax.ShapeDtypeStruct((extra, LANES), BF))
    wide_rows = max(stride for _, _, _, stride in plan.values())
    return pl.pallas_call(
        kernel,
        name="pieces_" + "_".join(names),
        grid=(steps,),
        in_specs=[pl.BlockSpec(memory_space=pltpu.SMEM)] + [spec(name) for name in names],
        out_specs=[pl.BlockSpec(memory_space=pl.ANY)] * len(shapes),
        out_shape=shapes,
        scratch_shapes=[
            pltpu.VMEM((end - origin, LANES), BF),
            pltpu.VMEM((wide_rows, LANES), F32),
            pltpu.VMEM((UP_BLOCKS if "up" in names else 1, BLOCK, LANES), F32),
            pltpu.SemaphoreType.DMA,
        ],
        compiler_params=pltpu.CompilerParams(vmem_limit_bytes=VMEM_LIMIT),
    )(place, *[matrices[name] for name in names])


def dot_t(left, right):
    return lax.dot_general(left, right, (((1,), (1,)), ((), ())), preferred_element_type=F32)


def t_dot(left, right):
    return lax.dot_general(left, right, (((0,), (0,)), ((), ())), preferred_element_type=F32)


def dense(left, right):
    return jnp.dot(left, right, preferred_element_type=F32)


def masked(scores, count):
    columns = lax.broadcasted_iota(jnp.int32, scores.shape, 1)
    return jnp.where(columns < count, scores, masked_score)


def unpack_heads(source, parts, heads, held):
    for part in range(parts):
        for head in range(heads):
            first = (part * heads + head) * HD
            held[part, head] = source[:, first : first + HD]


def attend(counts, packed, chunk):
    length, width = packed.shape
    heads = width // (3 * HD)

    def kernel(count, source, mixed, log_total, held, made):
        head = pl.program_id(0)

        @pl.when(head == 0)
        def _():
            unpack_heads(source, 3, heads, held)

        for first in range(0, length, chunk):
            queries = held[0, head, pl.ds(first, chunk), :]
            scores = masked(dot_t(queries, held[1, head]), count[0])
            top = jnp.max(scores, -1, keepdims=True)
            exponent = jnp.exp(scores - top)
            total = jnp.sum(exponent, -1, keepdims=True)
            probs = (exponent / total).astype(BF)
            made[head, pl.ds(first, chunk), :] = dense(probs, held[2, head]).astype(BF)
            log_total[0, first : first + chunk, :] = top + jnp.log(total)

        @pl.when(head == heads - 1)
        def _():
            mixed[...] = jnp.concatenate([made[index] for index in range(heads)], -1)

    return pl.pallas_call(
        kernel,
        name="attend",
        grid=(heads,),
        in_specs=[
            pl.BlockSpec(memory_space=pltpu.SMEM),
            pl.BlockSpec((length, width), lambda h: (0, 0)),
        ],
        out_specs=[
            pl.BlockSpec((length, heads * HD), lambda h: (0, 0)),
            pl.BlockSpec((1, length, 1), lambda h: (h, 0, 0)),
        ],
        out_shape=[
            jax.ShapeDtypeStruct((length, heads * HD), BF),
            jax.ShapeDtypeStruct((heads, length, 1), F32),
        ],
        scratch_shapes=[
            pltpu.VMEM((3, heads, length, HD), BF),
            pltpu.VMEM((heads, length, HD), BF),
        ],
        compiler_params=pltpu.CompilerParams(vmem_limit_bytes=VMEM_LIMIT),
    )(counts, packed)


def attend_back(counts, packed, log_total, grad_mixed, chunk):
    length, width = packed.shape
    heads = width // (3 * HD)
    scale = HD ** (-0.5)

    def kernel(count, source, logs, grad_source, made, sums, held, grad, results, acc_k, acc_v):
        head = pl.program_id(0)

        @pl.when(head == 0)
        def _():
            unpack_heads(source, 3, heads, held)
            unpack_heads(grad_source, 1, heads, grad)

        acc_k[...] = jnp.zeros_like(acc_k)
        acc_v[...] = jnp.zeros_like(acc_v)
        total_q = jnp.zeros((1, HD), F32)
        for first in range(0, length, chunk):
            part = pl.ds(first, chunk)
            queries = held[0, head, part, :]
            scores = masked(dot_t(queries, held[1, head]), count[0])
            probs = jnp.exp(scores - logs[0, part, :])
            grad_heads = grad[0, head, part, :]
            grad_probs = dot_t(grad_heads, held[2, head])
            delta = jnp.sum(probs * grad_probs, -1, keepdims=True)
            grad_scores = (probs * (grad_probs - delta)).astype(BF)
            grad_query = dense(grad_scores, held[1, head]) * scale
            total_q = total_q + jnp.sum(grad_query, 0, keepdims=True)
            results[0, head, part, :] = grad_query.astype(BF)
            acc_k[...] += t_dot(grad_scores, queries)
            acc_v[...] += t_dot(probs.astype(BF), grad_heads)
        results[1, head] = acc_k[...].astype(BF)
        results[2, head] = acc_v[...].astype(BF)
        sums[0, 0:1, :] = total_q
        sums[0, 1:2, :] = jnp.sum(acc_v[...], 0, keepdims=True)

        @pl.when(head == heads - 1)
        def _():
            made[...] = jnp.concatenate(
                [results[part, index] for part in range(3) for index in range(heads)], -1
            )

    return pl.pallas_call(
        kernel,
        name="attend_back",
        grid=(heads,),
        in_specs=[
            pl.BlockSpec(memory_space=pltpu.SMEM),
            pl.BlockSpec((length, width), lambda h: (0, 0)),
            pl.BlockSpec((1, length, 1), lambda h: (h, 0, 0)),
            pl.BlockSpec((length, heads * HD), lambda h: (0, 0)),
        ],
        out_specs=[
            pl.BlockSpec((length, width), lambda h: (0, 0)),
            pl.BlockSpec((1, 2, HD), lambda h: (h, 0, 0)),
        ],
        out_shape=[
            jax.ShapeDtypeStruct((length, width), BF),
            jax.ShapeDtypeStruct((heads, 2, HD), F32),
        ],
        scratch_shapes=[
            pltpu.VMEM((3, heads, length, HD), BF),
            pltpu.VMEM((1, heads, length, HD), BF),
            pltpu.VMEM((3, heads, length, HD), BF),
            pltpu.VMEM((length, HD), F32),
            pltpu.VMEM((length, HD), F32),
        ],
        compiler_params=pltpu.CompilerParams(vmem_limit_bytes=VMEM_LIMIT),
    )(counts, packed, log_total, grad_mixed)


def norm_forward(residual):
    centre = residual - jnp.mean(residual, -1, keepdims=True)
    inverse = lax.rsqrt(jnp.mean(centre * centre, -1, keepdims=True) + norm_epsilon)
    return (centre * inverse, inverse)


def norm_back(grad_normed, unit, inverse, gain):
    scaled = grad_normed * gain
    return inverse * (
        scaled
        - jnp.mean(scaled, -1, keepdims=True)
        - unit * jnp.mean(scaled * unit, -1, keepdims=True)
    )


def adam_update(master, grads, first, second, index):
    matrix_part = index < 4 * D * D + 2 * D * FF
    first_new = beta_one * first + (1.0 - beta_one) * grads
    second_new = beta_two * second + (1.0 - beta_two) * grads * grads
    first_hat = first_new / (1.0 - beta_one**adam_step)
    second_hat = second_new / (1.0 - beta_two**adam_step)
    rate = jnp.where(matrix_part, rate_matrix, rate_vector)
    decay = jnp.where(matrix_part, weight_decay, 0.0)
    updated = master - rate * (first_hat / (jnp.sqrt(second_hat) + adam_epsilon) + decay * master)
    return (updated, first_new, second_new)


def to_heads(array, parts):
    ctx = lax.axis_size("ctx")
    rows = array.shape[0]
    split = array.reshape(rows, parts, ctx, D // ctx).transpose(2, 0, 1, 3)
    split = split.reshape(ctx, rows, parts * D // ctx)
    held = lax.all_to_all(split, "ctx", split_axis=0, concat_axis=0, tiled=True)
    return held.reshape(rows * ctx, parts * D // ctx)


def from_heads(array, parts):
    ctx = lax.axis_size("ctx")
    length = array.shape[0]
    split = array.reshape(ctx, length // ctx, parts * D // ctx)
    held = lax.all_to_all(split, "ctx", split_axis=0, concat_axis=0, tiled=True)
    held = held.reshape(ctx, length // ctx, parts, D // ctx)
    return held.transpose(1, 2, 0, 3).reshape(length // ctx, parts * D)


def exchange(array, axis, bit):
    size = lax.axis_size(axis)
    return lax.ppermute(array, axis, [(index, index ^ bit) for index in range(size)])


def add(*arrays):
    return functools.reduce(jnp.add, [array.astype(F32) for array in arrays]).astype(BF)


def gather(layout, share):
    held = {0: share}
    bit = layout.ctx // 2
    while bit:
        held.update({key ^ bit: exchange(held[key], "ctx", bit) for key in list(held)})
        bit //= 2
    stack = jnp.concatenate([held[key] for key in range(layout.ctx)])
    arrays = [(stack, (0, 0, 0, layout.ctx))]
    if layout.columns == 4:
        middle, half = (stack.shape[0] // 2, layout.ctx // 2)
        by_x, by_y = (exchange(stack, "dp", 2), exchange(stack, "dp", 4))
        arrays += [(by_x, (1, 0, 0, layout.ctx)), (by_y, (2, 0, 0, layout.ctx))]
        arrays.append((exchange(by_x[:middle], "dp", 4), (3, 0, 0, half)))
        arrays.append((exchange(by_y[middle:], "dp", 2), (3, 0, half, half)))
    else:
        bit = 1
        while bit < layout.columns:
            arrays += [
                (exchange(array, "dp", 2 * bit), (place[0] ^ bit,) + place[1:])
                for array, place in arrays
            ]
            bit *= 2
    arrays += [
        (exchange(array, "dp", 1), (place[0], 1) + place[2:]) for array, place in arrays
    ]
    return arrays, stack


def scatter(layout, pieces):
    middle = pieces.shape[0] // 2
    kept = add(pieces[:middle], exchange(pieces[middle:], "dp", 1))
    size = middle // layout.columns
    parts = [kept[index * size : (index + 1) * size] for index in range(layout.columns)]
    if layout.columns == 4:
        half = size // 2
        low = add(parts[1][:half], exchange(parts[3][:half], "dp", 4))
        high = add(parts[2][half:], exchange(parts[3][half:], "dp", 2))
        halves = [
            add(parts[0][:half], exchange(low, "dp", 2), exchange(parts[2][:half], "dp", 4)),
            add(parts[0][half:], exchange(parts[1][half:], "dp", 2), exchange(high, "dp", 4)),
        ]
        summed = halves
    else:
        bit = layout.columns // 2
        while bit:
            parts = [
                add(parts[index], exchange(parts[index ^ bit], "dp", 2 * bit))
                for index in range(bit)
            ]
            bit //= 2
        half = size // 2
        summed = [parts[0][:half], parts[0][half:]]
    each = layout.ctx // 2
    length = size // layout.ctx
    held = {
        key: summed[key // each][(key % each) * length : (key % each + 1) * length]
        for key in range(layout.ctx)
    }
    bit = 1
    while bit < layout.ctx:
        for key in [key for key in held if key & bit]:
            held[key ^ bit] = add(held[key ^ bit], exchange(held.pop(key), "ctx", bit))
        bit *= 2
    return held[0]


def bits(layout):
    found = []
    for axis, size, unit in (("ctx", layout.ctx, 1), ("dp", layout.dp, layout.ctx)):
        bit = 1
        while bit < size:
            found.append((axis, bit, bit * unit))
            bit *= 2
    return found


def column_groups(layout):
    return [[column * 2 + core for column in range(layout.columns)] for core in range(2)]


def spread_weights(layout, flat, shard, everyone):
    last = layout.devices - 1
    before = lax.ppermute(
        flat[-TILE:], ("dp", "ctx"), [(index, index + 1) for index in range(last)]
    )
    length = layout.columns * layout.piece
    padded = jnp.concatenate([before, flat, jnp.zeros((length - layout.rows, LANES), BF)])
    offset = (shard * layout.rows) % TILE
    chunk = lax.dynamic_slice(padded, (TILE - offset, 0), (length, LANES))
    pieces = chunk.reshape(layout.columns, layout.piece, LANES)
    held = lax.all_to_all(
        pieces, "dp", split_axis=0, concat_axis=0, tiled=True, axis_index_groups=everyone
    )
    return chunk, held


def broadcast(layout, shard, sources):
    held = jnp.concatenate([rows for _, rows in sources])
    owner = jnp.concatenate(
        [jnp.full((rows.shape[0], 1), source, jnp.int32) for source, rows in sources]
    )
    for axis, bit, unit in bits(layout):
        other = exchange(held, axis, bit)
        held = jnp.where(((owner ^ shard) & unit) == 0, held, other)
    return held


def shards(layout, inputs, counts, params, first_moment, second_moment, out_cotangent):
    local_rows = inputs.shape[1]
    shard = lax.axis_index(("dp", "ctx"))
    score_scale = HD ** (-0.5)
    everyone = column_groups(layout)
    chunk = 256

    place = jnp.stack(
        [lax.axis_index("dp") // 2, lax.axis_index("dp") % 2, lax.axis_index("ctx")]
    ).astype(jnp.int32)
    padding = -layout.rows % 8 * LANES
    flat = jnp.pad(params[0].astype(BF), (0, padding)).reshape(-1, LANES)[: layout.rows]
    chunk_rows, pieces = spread_weights(layout, flat, shard, everyone)
    shared_first = pieces[: layout.first].reshape(-1, LANES)
    gathered_first, stack = gather(layout, shared_first)
    shared_rest = pieces[layout.first :].reshape(-1, LANES)
    shared_rest = lax.optimization_barrier((shared_rest, stack))[0]
    gathered_rest, _ = gather(layout, shared_rest)
    vector_first = ROW_VEC - layout.start(layout.devices - 1)
    assert 0 <= vector_first and vector_first + VEC_ROWS <= layout.columns * layout.piece
    sources = [(owner, chunk_rows[:rows]) for owner, rows in layout.leftover()]
    sources.append((layout.devices - 1, chunk_rows[vector_first : vector_first + VEC_ROWS]))
    spread = broadcast(layout, shard, sources)
    leftover = spread[:-VEC_ROWS]
    flat_vectors = spread[-VEC_ROWS:].reshape(-1).astype(F32)
    vectors = []
    offset = 0
    for length in VEC_LENGTHS:
        vectors.append(flat_vectors[offset : offset + length])
        offset += length
    (
        gain_one,
        shift_one,
        bias_query,
        bias_value,
        bias_out,
        gain_two,
        shift_two,
        bias_down,
        bias_up,
    ) = vectors

    residual = inputs[0].astype(F32)
    unit_one, inverse_one = norm_forward(residual)
    normed_round = (unit_one * gain_one + shift_one).astype(BF)
    qkv_weight = first_weights(layout, place, gathered_first, leftover)
    projected = dense(normed_round, qkv_weight)
    queries = ((projected[:, :D] + bias_query) * score_scale).astype(BF)
    keys = projected[:, D : 2 * D].astype(BF)
    values = (projected[:, 2 * D :] + bias_value).astype(BF)
    packed = to_heads(jnp.concatenate([queries, keys, values], -1), 3)
    out_weight, up_weight, down_weight = other_weights(layout, place, gathered_rest)
    mixed_heads, log_total = attend(counts, packed, chunk)
    mixed = from_heads(mixed_heads, 1)
    middle = residual + dense(mixed, out_weight) + bias_out
    unit_two, inverse_two = norm_forward(middle)
    normed_two_round = (unit_two * gain_two + shift_two).astype(BF)
    pre_gelu = dense(normed_two_round, up_weight) + bias_up
    activated = jax.nn.gelu(pre_gelu, approximate=True).astype(BF)
    output = (middle + dense(activated, down_weight) + bias_down).astype(BF)

    positions = lax.axis_index("ctx") * local_rows + jnp.arange(local_rows, dtype=jnp.int32)
    row_valid = (positions < counts[0])[:, None].astype(F32)
    grad_next = out_cotangent[0] * row_valid
    grad_bias_down = jnp.sum(grad_next, 0)
    grad_round = grad_next.astype(BF)
    grad_down = t_dot(activated, grad_round).astype(BF)
    grad_act = dot_t(grad_round, down_weight)
    gelu_back = jax.vjp(functools.partial(jax.nn.gelu, approximate=True), pre_gelu)[1]
    grad_pre = gelu_back(grad_act)[0]
    grad_bias_up = jnp.sum(grad_pre, 0)
    grad_pre_round = grad_pre.astype(BF)
    grad_up = t_dot(normed_two_round, grad_pre_round).astype(BF)
    middle_group = layout.columns // 2
    (terms,) = gradient_pieces(
        layout, place, (middle_group, layout.columns), {"up": grad_up, "down": grad_down}
    )
    sum_last = scatter(layout, terms)
    grad_normed_two = dot_t(grad_pre_round, up_weight)
    grad_gain_two = jnp.sum(grad_normed_two * unit_two, 0)
    grad_shift_two = jnp.sum(grad_normed_two, 0)
    grad_middle = grad_next + norm_back(grad_normed_two, unit_two, inverse_two, gain_two)
    grad_bias_out = jnp.sum(grad_middle, 0)
    middle_round = grad_middle.astype(BF)
    grad_out = t_dot(mixed, middle_round).astype(BF)
    grad_mixed = dot_t(middle_round, out_weight).astype(BF)
    grad_mixed_heads = to_heads(grad_mixed, 1)
    (terms,) = gradient_pieces(
        layout, place, (layout.first, middle_group), {"out": grad_out, "up": grad_up}
    )
    sum_middle = scatter(layout, terms)
    grad_packed, sums = attend_back(counts, packed, log_total, grad_mixed_heads, chunk)
    grad_projected = from_heads(grad_packed, 3)
    grad_qkv = t_dot(normed_round, grad_projected).astype(BF)
    terms, leftover_terms = gradient_pieces(
        layout, place, (0, layout.first), {"qkv": grad_qkv}, leftover=True
    )
    sum_first = scatter(layout, terms)
    grad_normed_one = dot_t(grad_projected, qkv_weight)
    grad_gain_one = jnp.sum(grad_normed_one * unit_one, 0)
    grad_shift_one = jnp.sum(grad_normed_one, 0)
    input_grad = grad_middle + norm_back(grad_normed_one, unit_one, inverse_one, gain_one)

    share = D // layout.ctx
    where = (lax.axis_index("ctx") * share,)
    sum_q, sum_v = (sums[:, 0].reshape(-1), sums[:, 1].reshape(-1))
    grad_bias_query = lax.dynamic_update_slice(jnp.zeros((D,), F32), sum_q, where)
    grad_bias_value = lax.dynamic_update_slice(jnp.zeros((D,), F32), sum_v, where)
    vector_terms = [
        grad_gain_one,
        grad_shift_one,
        grad_bias_query,
        grad_bias_value,
        grad_bias_out,
        grad_gain_two,
        grad_shift_two,
        grad_bias_down,
        grad_bias_up,
    ]
    padding = jnp.zeros((VEC_ROWS * LANES - sum(VEC_LENGTHS),), F32)
    vector_grads = jnp.concatenate(vector_terms + [padding]).reshape(VEC_ROWS, LANES)
    for axis, bit, _ in bits(layout):
        vector_grads = vector_grads + exchange(vector_grads, axis, bit)
    for axis, bit, _ in bits(layout):
        leftover_terms = add(leftover_terms, exchange(leftover_terms, axis, bit))

    summed = jnp.concatenate([sum_first, sum_middle, sum_last])
    held = lax.all_to_all(
        summed.reshape(layout.columns, layout.piece, LANES),
        "dp",
        split_axis=0,
        concat_axis=0,
        tiled=True,
        axis_index_groups=everyone,
    )
    chunk_sum = held.reshape(-1, LANES).astype(F32)
    extra = jnp.zeros_like(chunk_sum)
    used = 0
    for owner, rows in layout.leftover():
        placed = jnp.pad(
            leftover_terms[used : used + rows].astype(F32), ((0, chunk_sum.shape[0] - rows), (0, 0))
        )
        extra = jnp.where(shard == owner, placed, extra)
        used += rows
    after = chunk_sum.shape[0] - vector_first - VEC_ROWS
    placed = jnp.pad(vector_grads, ((vector_first, after), (0, 0)))
    chunk_sum = chunk_sum + jnp.where(shard == layout.devices - 1, placed, extra)
    offset = (shard * layout.rows) % TILE
    rows = lax.dynamic_slice(chunk_sum, (offset, 0), (layout.rows, LANES))
    param_grads = rows.reshape(params.shape)
    index = (shard * params.shape[1] + jnp.arange(params.shape[1], dtype=jnp.int32))[None, :]
    new_params, new_first, new_second = adam_update(
        params, param_grads, first_moment, second_moment, index
    )
    return (output[None], input_grad[None], param_grads, new_params, new_first, new_second)


def solution(mesh):
    placed = (
        P("dp", "ctx", None),
        P("dp"),
        P(None, ("dp", "ctx")),
        P(None, ("dp", "ctx")),
        P(None, ("dp", "ctx")),
        P("dp", "ctx", None),
    )
    dp, ctx = (mesh.shape["dp"], mesh.shape["ctx"])

    def program(inputs, counts, params, first_moment, second_moment, out_cotangent):
        layout = Layout(dp, ctx, params.shape[1] // (dp * ctx))
        return jax.shard_map(
            functools.partial(shards, layout),
            mesh=mesh,
            in_specs=placed,
            out_specs=(
                P("dp", "ctx", None),
                P("dp", "ctx", None),
                P(None, ("dp", "ctx")),
                P(None, ("dp", "ctx")),
                P(None, ("dp", "ctx")),
                P(None, ("dp", "ctx")),
            ),
            check_vma=False,
        )(inputs, counts, params, first_moment, second_moment, out_cotangent)

    return program
```

```python
import functools
import math

import jax
import jax.numpy as jnp
from jax import lax
from jax.experimental import pallas as pl
from jax.experimental.pallas import tpu as pltpu
from jax.sharding import PartitionSpec as P


D = 1152
HD = 72
FF = 4304
LANES = 128
TILE = 16

norm_epsilon = 1e-06
beta_one = 0.9
beta_two = 0.95
adam_epsilon = 1e-08
adam_step = 3
rate_matrix = 0.005
rate_vector = 0.1
weight_decay = 0.1
masked_score = -1e30

BF = jnp.bfloat16
F32 = jnp.float32

QKV_BLOCKS = 3 * D // LANES
D_BLOCKS = D // LANES
ROW_QKV = 0
ROW_OUT = D * QKV_BLOCKS
ROW_UP = ROW_OUT + D * D_BLOCKS
ROW_DOWN = ROW_UP + D * FF // LANES
ROW_VEC = ROW_DOWN + FF * D_BLOCKS
VEC_ROWS = 128
VEC_LENGTHS = [D] * 8 + [FF]

UP_GROUP = LANES // math.gcd(FF, LANES)
UP_STRIDE = UP_GROUP * FF // LANES
UP_BLOCKS = -(-FF // LANES)
UP_TAIL = FF - (UP_BLOCKS - 1) * LANES
STEPS = 9
BLOCK = D // STEPS
DOWN_BLOCK = -(-FF // (STEPS * TILE)) * TILE
VMEM_LIMIT = 60 * 1024 * 1024


class Layout:
    def __init__(self, dp, ctx, shard_length):
        self.dp, self.ctx = dp, ctx
        self.devices = dp * ctx
        self.columns = dp // 2
        self.rows = shard_length // LANES
        longest = (self.rows + TILE - 1) // TILE
        self.piece = -(-longest // self.columns) * TILE
        self.group_shards = 2 * ctx
        self.first = ROW_OUT // (self.group_shards * self.rows)
        self.last_piece = self.rows // TILE * TILE - (self.columns - 1) * self.piece
        assert self.first > 0 and self.last_piece > 0

    def start(self, shard):
        return shard * self.rows // TILE * TILE

    def group_start(self, group):
        return self.start(group * self.group_shards)

    def group_end(self, group):
        return self.start(group * self.group_shards - 1) + self.columns * self.piece

    def leftover(self):
        shard = self.first * self.group_shards
        found = []
        while self.start(shard) < ROW_OUT:
            found.append((shard, min(ROW_OUT, self.start(shard + 1)) - self.start(shard)))
            shard += 1
        return found


def lane_index(rows):
    return lax.broadcasted_iota(jnp.int32, (rows, LANES), 1)


def rows_to_matrix(flat, base, rows, blocks, wide, out):
    wide[pl.ds(0, rows * blocks), :] = flat[pl.ds(base, rows * blocks), :].astype(F32)
    for block in range(blocks):
        part = wide[pl.ds(block, rows, stride=blocks), :]
        out[:, block * LANES : (block + 1) * LANES] = part.astype(BF)


def matrix_to_rows(matrix, rows, blocks, wide, flat, base):
    for block in range(blocks):
        part = matrix[:, block * LANES : (block + 1) * LANES].astype(F32)
        wide[pl.ds(block, rows, stride=blocks), :] = part
    flat[pl.ds(base, rows * blocks), :] = wide[pl.ds(0, rows * blocks), :].astype(BF)


def rows_to_up(flat, base, wide, square, out):
    groups = BLOCK // UP_GROUP
    length = groups * UP_STRIDE
    wide[pl.ds(0, length), :] = flat[pl.ds(base, length), :].astype(F32)
    lanes = lane_index(groups)
    for row in range(UP_GROUP):
        first, shift = divmod(row * FF, LANES)
        held = None
        for block in range(UP_BLOCKS + 1):
            if block == UP_BLOCKS and shift + UP_TAIL <= LANES:
                piece = held
            else:
                piece = wide[pl.ds(first + block, groups, stride=UP_STRIDE), :]
                if shift:
                    piece = pltpu.roll(piece, LANES - shift, 1)
            if block:
                value = jnp.where(lanes < LANES - shift, held, piece) if shift else held
                square[block - 1, pl.ds(row, groups, stride=UP_GROUP), :] = value
            held = piece
    for block in range(UP_BLOCKS):
        first, last = (block * LANES, min(FF, (block + 1) * LANES))
        out[:, first:last] = square[block, :, : last - first].astype(BF)


def up_to_rows(matrix, square, wide, flat, base):
    groups = BLOCK // UP_GROUP
    length = groups * UP_STRIDE
    for block in range(UP_BLOCKS):
        first, last = (block * LANES, min(FF, (block + 1) * LANES))
        square[block, :, : last - first] = matrix[:, first:last].astype(F32)
    lanes = lane_index(groups)
    held = None
    for row in range(UP_GROUP):
        first, shift = divmod(row * FF, LANES)
        for block in range(UP_BLOCKS):
            piece = square[block, pl.ds(row, groups, stride=UP_GROUP), :]
            if shift:
                piece = pltpu.roll(piece, shift, 1)
                value = jnp.where(lanes < shift, held, piece)
            else:
                value = piece
            if block == UP_BLOCKS - 1 and shift + UP_TAIL < LANES:
                held = value
            else:
                wide[pl.ds(first + block, groups, stride=UP_STRIDE), :] = value
                held = piece
    flat[pl.ds(base, length), :] = wide[pl.ds(0, length), :].astype(BF)


def fetch(layout, place, groups, origin, sources, flat, sem):
    low, high = groups
    count = high - low
    for ref, (column, core, first_row, members) in sources:
        device_column = jnp.bitwise_xor(place[0], column)
        device_core = jnp.bitwise_xor(place[1], core)

        def body(index, _, ref=ref, first_row=first_row):
            row = jnp.bitwise_xor(place[2], first_row + index // count)
            group = low + index % count
            shard = group * layout.group_shards + device_core * layout.ctx + row
            start = shard * layout.rows // TILE * TILE
            target = pl.multiple_of(start + device_column * layout.piece - origin, TILE)
            source = pl.multiple_of(index * layout.piece, TILE)

            def copy(offset, rows):
                pltpu.make_async_copy(
                    ref.at[pl.ds(source + offset, rows), :],
                    flat.at[pl.ds(target + offset, rows), :],
                    sem,
                ).start()

            is_last = device_column == layout.columns - 1
            longer = shard * layout.rows % TILE + layout.rows % TILE >= TILE

            @pl.when(jnp.logical_not(is_last))
            def _():
                copy(0, layout.piece)

            @pl.when(is_last)
            def _():
                copy(0, layout.last_piece)

            @pl.when(jnp.logical_and(is_last, longer))
            def _():
                copy(layout.last_piece, TILE)

            return 0

        lax.fori_loop(0, members * count, body, 0)


def flat_of(gathered):
    return [array for array, _ in gathered]


def first_weights(layout, place, gathered, leftover):
    inside = layout.group_start(layout.first)
    length = inside + leftover.shape[0]
    assert length == ROW_OUT
    arrays = flat_of(gathered)

    def kernel(place_ref, *refs):
        sources, (extra, qkv, flat, wide, sem) = (refs[: len(arrays)], refs[len(arrays) :])
        step = pl.program_id(0)

        @pl.when(step == 0)
        def _():
            named = [(ref, entry) for ref, (_, entry) in zip(sources, gathered)]
            fetch(layout, place_ref, (0, layout.first), 0, named, flat, sem)
            pltpu.make_async_copy(
                extra, flat.at[pl.ds(inside, leftover.shape[0]), :], sem
            ).start()
            pltpu.make_async_copy(flat, flat, sem).wait()

        base = pl.multiple_of(step * (BLOCK * QKV_BLOCKS), TILE)
        rows_to_matrix(flat, base, BLOCK, QKV_BLOCKS, wide, qkv)

    return pl.pallas_call(
        kernel,
        name="first_weights",
        grid=(STEPS,),
        in_specs=[pl.BlockSpec(memory_space=pltpu.SMEM)]
        + [pl.BlockSpec(memory_space=pl.ANY)] * (len(arrays) + 1),
        out_specs=pl.BlockSpec((BLOCK, 3 * D), lambda i: (i, 0)),
        out_shape=jax.ShapeDtypeStruct((D, 3 * D), BF),
        scratch_shapes=[
            pltpu.VMEM((length, LANES), BF),
            pltpu.VMEM((BLOCK * QKV_BLOCKS, LANES), F32),
            pltpu.SemaphoreType.DMA,
        ],
        compiler_params=pltpu.CompilerParams(vmem_limit_bytes=VMEM_LIMIT),
    )(place, *arrays, leftover)


def other_weights(layout, place, gathered):
    origin = layout.group_start(layout.first)
    length = layout.start(layout.devices) - origin
    padded = max(length, ROW_DOWN - origin + STEPS * DOWN_BLOCK * D_BLOCKS)
    up_length = BLOCK // UP_GROUP * UP_STRIDE
    arrays = flat_of(gathered)

    def kernel(place_ref, *refs):
        sources = refs[: len(arrays)]
        out_w, up_w, down_w, flat, wide, square, sem = refs[len(arrays) :]
        step = pl.program_id(0)

        @pl.when(step == 0)
        def _():
            named = [(ref, entry) for ref, (_, entry) in zip(sources, gathered)]
            fetch(layout, place_ref, (layout.first, layout.columns), origin, named, flat, sem)
            whole = flat.at[pl.ds(0, length), :]
            pltpu.make_async_copy(whole, whole, sem).wait()

        base = pl.multiple_of(ROW_OUT - origin + step * (BLOCK * D_BLOCKS), TILE)
        rows_to_matrix(flat, base, BLOCK, D_BLOCKS, wide, out_w)
        base = pl.multiple_of(ROW_UP - origin + step * up_length, TILE)
        rows_to_up(flat, base, wide, square, up_w)
        base = pl.multiple_of(ROW_DOWN - origin + step * (DOWN_BLOCK * D_BLOCKS), TILE)
        rows_to_matrix(flat, base, DOWN_BLOCK, D_BLOCKS, wide, down_w)

    return pl.pallas_call(
        kernel,
        name="other_weights",
        grid=(STEPS,),
        in_specs=[pl.BlockSpec(memory_space=pltpu.SMEM)]
        + [pl.BlockSpec(memory_space=pl.ANY)] * len(arrays),
        out_specs=[
            pl.BlockSpec((BLOCK, D), lambda i: (i, 0)),
            pl.BlockSpec((BLOCK, FF), lambda i: (i, 0)),
            pl.BlockSpec((DOWN_BLOCK, D), lambda i: (i, 0)),
        ],
        out_shape=[
            jax.ShapeDtypeStruct((D, D), BF),
            jax.ShapeDtypeStruct((D, FF), BF),
            jax.ShapeDtypeStruct((FF, D), BF),
        ],
        scratch_shapes=[
            pltpu.VMEM((padded, LANES), BF),
            pltpu.VMEM((max(up_length + 8, DOWN_BLOCK * D_BLOCKS), LANES), F32),
            pltpu.VMEM((UP_BLOCKS, BLOCK, LANES), F32),
            pltpu.SemaphoreType.DMA,
        ],
        compiler_params=pltpu.CompilerParams(vmem_limit_bytes=VMEM_LIMIT),
    )(place, *arrays)


MATRICES = {
    "qkv": (ROW_QKV, BLOCK, BLOCK * QKV_BLOCKS, 3 * D),
    "out": (ROW_OUT, BLOCK, BLOCK * D_BLOCKS, D),
    "up": (ROW_UP, BLOCK, BLOCK // UP_GROUP * UP_STRIDE, FF),
    "down": (ROW_DOWN, DOWN_BLOCK, DOWN_BLOCK * D_BLOCKS, D),
}


def gradient_pieces(layout, place, groups, matrices, leftover=False):
    low, high = layout.group_start(groups[0]), layout.group_end(groups[1])
    count = groups[1] - groups[0]
    names = list(matrices)
    plan = {}
    for name in names:
        first, _, stride, _ = MATRICES[name]
        blocks = [
            block
            for block in range(STEPS)
            if leftover
            or (first + block * stride < high and first + (block + 1) * stride > low)
        ]
        plan[name] = (first, blocks[0], len(blocks), stride)
    origin = min([low] + [first + b * stride for first, b, _, stride in plan.values()])
    end = max([high] + [first + (b + n) * stride for first, b, n, stride in plan.values()])
    steps = max(n for _, _, n, _ in plan.values())
    covered = min(first + b * stride for first, b, _, stride in plan.values())
    rows = layout.devices * count * layout.piece
    extra = ROW_OUT - layout.group_start(layout.first)

    def kernel(place_ref, *refs):
        inputs, refs = (refs[: len(names)], refs[len(names) :])
        outputs, (flat, wide, square, sem) = (refs[:-4], refs[-4:])
        step = pl.program_id(0)
        if covered > low:

            @pl.when(step == 0)
            def _():
                flat[pl.ds(low - origin, covered - low), :] = jnp.zeros((covered - low, LANES), BF)

        for ref, name in zip(inputs, names):
            first, block, number, stride = plan[name]

            def convert(ref=ref, name=name, first=first, block=block, stride=stride):
                base = pl.multiple_of(first - origin + (block + step) * stride, TILE)
                if name == "up":
                    up_to_rows(ref, square, wide, flat, base)
                else:
                    blocks = QKV_BLOCKS if name == "qkv" else D_BLOCKS
                    matrix_to_rows(ref, stride // blocks, blocks, wide, flat, base)

            if number == steps:
                convert()
            else:
                pl.when(step < number)(convert)

        @pl.when(step == steps - 1)
        def _():
            if "down" in names:
                tail = end - ROW_VEC
                flat[pl.ds(ROW_VEC - origin, tail), :] = jnp.zeros((tail, LANES), BF)

            def body(index, _):
                group = groups[0] + index % count
                key = index // count
                row = jnp.bitwise_xor(place_ref[2], key % layout.ctx)
                key = key // layout.ctx
                column = jnp.bitwise_xor(place_ref[0], key % layout.columns)
                core = jnp.bitwise_xor(place_ref[1], key // layout.columns)
                shard = group * layout.group_shards + core * layout.ctx + row
                start = shard * layout.rows // TILE * TILE
                source = pl.multiple_of(start + column * layout.piece - origin, TILE)
                target = pl.multiple_of(index * layout.piece, TILE)
                pltpu.make_async_copy(
                    flat.at[pl.ds(source, layout.piece), :],
                    outputs[0].at[pl.ds(target, layout.piece), :],
                    sem,
                ).start()
                return 0

            lax.fori_loop(0, layout.devices * count, body, 0)
            pltpu.make_async_copy(outputs[0], outputs[0], sem).wait()
            if leftover:
                copy = pltpu.make_async_copy(
                    flat.at[pl.ds(ROW_OUT - extra - origin, extra), :], outputs[1], sem
                )
                copy.start()
                copy.wait()

    def spec(name):
        _, block, number, _ = plan[name]
        _, height, _, width = MATRICES[name]
        return pl.BlockSpec(
            (height, width), lambda i: (block + jnp.minimum(i, number - 1), 0)
        )

    shapes = [jax.ShapeDtypeStruct((rows, LANES), BF)]
    if leftover:
        shapes.append(jax.ShapeDtypeStruct((extra, LANES), BF))
    wide_rows = max(stride for _, _, _, stride in plan.values())
    return pl.pallas_call(
        kernel,
        grid=(steps,),
        in_specs=[pl.BlockSpec(memory_space=pltpu.SMEM)] + [spec(name) for name in names],
        out_specs=[pl.BlockSpec(memory_space=pl.ANY)] * len(shapes),
        out_shape=shapes,
        scratch_shapes=[
            pltpu.VMEM((end - origin, LANES), BF),
            pltpu.VMEM((wide_rows, LANES), F32),
            pltpu.VMEM((UP_BLOCKS if "up" in names else 1, BLOCK, LANES), F32),
            pltpu.SemaphoreType.DMA,
        ],
        compiler_params=pltpu.CompilerParams(vmem_limit_bytes=VMEM_LIMIT),
    )(place, *[matrices[name] for name in names])


def dot_t(left, right):
    return lax.dot_general(left, right, (((1,), (1,)), ((), ())), preferred_element_type=F32)


def t_dot(left, right):
    return lax.dot_general(left, right, (((0,), (0,)), ((), ())), preferred_element_type=F32)


def dense(left, right):
    return jnp.dot(left, right, preferred_element_type=F32)


def masked(scores, count):
    columns = lax.broadcasted_iota(jnp.int32, scores.shape, 1)
    return jnp.where(columns < count, scores, masked_score)


def unpack_heads(source, parts, heads, held):
    for part in range(parts):
        for head in range(heads):
            first = (part * heads + head) * HD
            held[part, head] = source[:, first : first + HD]


def attend(counts, packed, chunk):
    length, width = packed.shape
    heads = width // (3 * HD)

    def kernel(count, source, mixed, log_total, held, made):
        head = pl.program_id(0)

        @pl.when(head == 0)
        def _():
            unpack_heads(source, 3, heads, held)

        for first in range(0, length, chunk):
            queries = held[0, head, pl.ds(first, chunk), :]
            scores = masked(dot_t(queries, held[1, head]), count[0])
            top = jnp.max(scores, -1, keepdims=True)
            exponent = jnp.exp(scores - top)
            total = jnp.sum(exponent, -1, keepdims=True)
            probs = (exponent / total).astype(BF)
            made[head, pl.ds(first, chunk), :] = dense(probs, held[2, head]).astype(BF)
            log_total[0, first : first + chunk, :] = top + jnp.log(total)

        @pl.when(head == heads - 1)
        def _():
            mixed[...] = jnp.concatenate([made[index] for index in range(heads)], -1)

    return pl.pallas_call(
        kernel,
        name="attend",
        grid=(heads,),
        in_specs=[
            pl.BlockSpec(memory_space=pltpu.SMEM),
            pl.BlockSpec((length, width), lambda h: (0, 0)),
        ],
        out_specs=[
            pl.BlockSpec((length, heads * HD), lambda h: (0, 0)),
            pl.BlockSpec((1, length, 1), lambda h: (h, 0, 0)),
        ],
        out_shape=[
            jax.ShapeDtypeStruct((length, heads * HD), BF),
            jax.ShapeDtypeStruct((heads, length, 1), F32),
        ],
        scratch_shapes=[
            pltpu.VMEM((3, heads, length, HD), BF),
            pltpu.VMEM((heads, length, HD), BF),
        ],
        compiler_params=pltpu.CompilerParams(vmem_limit_bytes=VMEM_LIMIT),
    )(counts, packed)


def attend_back(counts, packed, log_total, grad_mixed, chunk):
    length, width = packed.shape
    heads = width // (3 * HD)
    scale = HD ** (-0.5)

    def kernel(count, source, logs, grad_source, made, sums, held, grad, results, acc_k, acc_v):
        head = pl.program_id(0)

        @pl.when(head == 0)
        def _():
            unpack_heads(source, 3, heads, held)
            unpack_heads(grad_source, 1, heads, grad)

        acc_k[...] = jnp.zeros_like(acc_k)
        acc_v[...] = jnp.zeros_like(acc_v)
        total_q = jnp.zeros((1, HD), F32)
        for first in range(0, length, chunk):
            part = pl.ds(first, chunk)
            queries = held[0, head, part, :]
            scores = masked(dot_t(queries, held[1, head]), count[0])
            probs = jnp.exp(scores - logs[0, part, :])
            grad_heads = grad[0, head, part, :]
            grad_probs = dot_t(grad_heads, held[2, head])
            delta = jnp.sum(probs * grad_probs, -1, keepdims=True)
            grad_scores = (probs * (grad_probs - delta)).astype(BF)
            grad_query = dense(grad_scores, held[1, head]) * scale
            total_q = total_q + jnp.sum(grad_query, 0, keepdims=True)
            results[0, head, part, :] = grad_query.astype(BF)
            acc_k[...] += t_dot(grad_scores, queries)
            acc_v[...] += t_dot(probs.astype(BF), grad_heads)
        results[1, head] = acc_k[...].astype(BF)
        results[2, head] = acc_v[...].astype(BF)
        sums[0, 0:1, :] = total_q
        sums[0, 1:2, :] = jnp.sum(acc_v[...], 0, keepdims=True)

        @pl.when(head == heads - 1)
        def _():
            made[...] = jnp.concatenate(
                [results[part, index] for part in range(3) for index in range(heads)], -1
            )

    return pl.pallas_call(
        kernel,
        name="attend_back",
        grid=(heads,),
        in_specs=[
            pl.BlockSpec(memory_space=pltpu.SMEM),
            pl.BlockSpec((length, width), lambda h: (0, 0)),
            pl.BlockSpec((1, length, 1), lambda h: (h, 0, 0)),
            pl.BlockSpec((length, heads * HD), lambda h: (0, 0)),
        ],
        out_specs=[
            pl.BlockSpec((length, width), lambda h: (0, 0)),
            pl.BlockSpec((1, 2, HD), lambda h: (h, 0, 0)),
        ],
        out_shape=[
            jax.ShapeDtypeStruct((length, width), BF),
            jax.ShapeDtypeStruct((heads, 2, HD), F32),
        ],
        scratch_shapes=[
            pltpu.VMEM((3, heads, length, HD), BF),
            pltpu.VMEM((1, heads, length, HD), BF),
            pltpu.VMEM((3, heads, length, HD), BF),
            pltpu.VMEM((length, HD), F32),
            pltpu.VMEM((length, HD), F32),
        ],
        compiler_params=pltpu.CompilerParams(vmem_limit_bytes=VMEM_LIMIT),
    )(counts, packed, log_total, grad_mixed)


def norm_forward(residual):
    centre = residual - jnp.mean(residual, -1, keepdims=True)
    inverse = lax.rsqrt(jnp.mean(centre * centre, -1, keepdims=True) + norm_epsilon)
    return (centre * inverse, inverse)


def norm_back(grad_normed, unit, inverse, gain):
    scaled = grad_normed * gain
    return inverse * (
        scaled
        - jnp.mean(scaled, -1, keepdims=True)
        - unit * jnp.mean(scaled * unit, -1, keepdims=True)
    )


def adam_update(master, grads, first, second, matrix_part):
    first_new = beta_one * first + (1.0 - beta_one) * grads
    second_new = beta_two * second + (1.0 - beta_two) * grads * grads
    first_hat = first_new / (1.0 - beta_one**adam_step)
    second_hat = second_new / (1.0 - beta_two**adam_step)
    rate = jnp.where(matrix_part, rate_matrix, rate_vector)
    decay = jnp.where(matrix_part, weight_decay, 0.0)
    updated = master - rate * (first_hat / (jnp.sqrt(second_hat) + adam_epsilon) + decay * master)
    return (updated, first_new, second_new)


def to_heads(array, parts):
    ctx = lax.axis_size("ctx")
    rows = array.shape[0]
    split = array.reshape(rows, parts, ctx, D // ctx).transpose(2, 0, 1, 3)
    split = split.reshape(ctx, rows, parts * D // ctx)
    held = lax.all_to_all(split, "ctx", split_axis=0, concat_axis=0, tiled=True)
    return held.reshape(rows * ctx, parts * D // ctx)


def from_heads(array, parts):
    ctx = lax.axis_size("ctx")
    length = array.shape[0]
    split = array.reshape(ctx, length // ctx, parts * D // ctx)
    held = lax.all_to_all(split, "ctx", split_axis=0, concat_axis=0, tiled=True)
    held = held.reshape(ctx, length // ctx, parts, D // ctx)
    return held.transpose(1, 2, 0, 3).reshape(length // ctx, parts * D)


def exchange(array, axis, bit):
    size = lax.axis_size(axis)
    return lax.ppermute(array, axis, [(index, index ^ bit) for index in range(size)])


def add(*arrays):
    return functools.reduce(jnp.add, [array.astype(F32) for array in arrays]).astype(BF)


def gather(layout, share, batches):
    held = {0: share}
    bit = 1
    while bit < layout.ctx:
        held.update({key ^ bit: exchange(held[key], "ctx", bit) for key in list(held)})
        bit *= 2
    arrays = []
    members = layout.ctx // batches
    for batch in range(batches):
        first = batch * members
        stack = jnp.concatenate([held[key] for key in range(first, first + members)])
        found = [(stack, (0, 0, first, members))]
        if layout.columns == 4:
            middle, half = (stack.shape[0] // 2, members // 2)
            by_x = exchange(stack, "dp", 2)
            by_y = exchange(stack, "dp", 4)
            found += [(by_x, (1, 0, first, members)), (by_y, (2, 0, first, members))]
            across = exchange(by_x[:middle], "dp", 4)
            found.append((across, (3, 0, first, half)))
            across = exchange(by_y[middle:], "dp", 2)
            found.append((across, (3, 0, first + half, half)))
        else:
            bit = 1
            while bit < layout.columns:
                found += [
                    (exchange(array, "dp", 2 * bit), (place[0] ^ bit,) + place[1:])
                    for array, place in found
                ]
                bit *= 2
        arrays += found
    arrays += [(exchange(array, "dp", 1), (place[0], 1) + place[2:]) for array, place in arrays]
    return arrays, held[layout.ctx - 1]


def scatter(layout, pieces):
    middle = pieces.shape[0] // 2
    kept = add(pieces[:middle], exchange(pieces[middle:], "dp", 1))
    size = middle // layout.columns
    parts = [kept[index * size : (index + 1) * size] for index in range(layout.columns)]
    half = size // 2
    if layout.columns == 4:
        low = add(parts[1][:half], exchange(parts[3][:half], "dp", 4))
        high = add(parts[2][half:], exchange(parts[3][half:], "dp", 2))
        summed = [
            add(parts[0][:half], exchange(low, "dp", 2), exchange(parts[2][:half], "dp", 4)),
            add(parts[0][half:], exchange(parts[1][half:], "dp", 2), exchange(high, "dp", 4)),
        ]
    else:
        bit = layout.columns // 2
        while bit:
            parts = [
                add(parts[index], exchange(parts[index ^ bit], "dp", 2 * bit))
                for index in range(bit)
            ]
            bit //= 2
        summed = [parts[0][:half], parts[0][half:]]
    each = layout.ctx // 2
    length = size // layout.ctx
    held = {
        key: summed[key // each][(key % each) * length : (key % each + 1) * length]
        for key in range(layout.ctx)
    }
    bit = 1
    while bit < layout.ctx:
        for key in [key for key in held if key & bit]:
            moved = exchange(held.pop(key), "ctx", bit)
            held[key ^ bit] = add(held[key ^ bit], moved)
        bit *= 2
    return held[0]


def bits(layout):
    found = []
    for unit, size in ((1, layout.ctx), (2 * layout.ctx, layout.columns), (layout.ctx, 2)):
        bit = 1
        while bit < size:
            found.append(bit * unit)
            bit *= 2
    return found


def broadcast(layout, shard, owner, held):
    have = [owner]
    for bit in bits(layout):
        other = lax.ppermute(held, ("dp", "ctx"), [(index, index ^ bit) for index in have])
        have += [index ^ bit for index in have]
        held = jnp.where((shard & bit) != (owner & bit), other, held)
    return held


def sum_to(layout, owner, held):
    have = list(range(layout.devices))
    for bit in reversed(bits(layout)):
        senders = [index for index in have if (index & bit) != (owner & bit)]
        other = lax.ppermute(held, ("dp", "ctx"), [(index, index ^ bit) for index in senders])
        have = [index for index in have if index not in senders]
        held = (held.astype(F32) + other.astype(F32)).astype(held.dtype)
    return held


def column_groups(layout):
    return [[column * 2 + core for column in range(layout.columns)] for core in range(2)]


SWEEP = 512


def align(layout, params, before, offset):
    length = layout.columns * layout.piece
    steps = pl.cdiv(layout.rows, SWEEP)
    held = max(TILE + steps * SWEEP, TILE + length)

    def kernel(offset_ref, rows, previous, chunk, wide):
        step = pl.program_id(0)

        @pl.when(step == 0)
        def _():
            wide[0:TILE, :] = previous[...]

        base = pl.multiple_of(TILE + step * SWEEP, TILE)
        wide[pl.ds(base, SWEEP), :] = rows[...].reshape(SWEEP, LANES)

        @pl.when(step == steps - 1)
        def _():
            chunk[...] = wide[pl.ds(TILE - offset_ref[0], length), :].astype(BF)

    return pl.pallas_call(
        kernel,
        name="align",
        grid=(steps,),
        in_specs=[
            pl.BlockSpec(memory_space=pltpu.SMEM),
            pl.BlockSpec((1, SWEEP * LANES), lambda i: (0, i)),
            pl.BlockSpec((TILE, LANES), lambda i: (0, 0)),
        ],
        out_specs=pl.BlockSpec((length, LANES), lambda i: (0, 0)),
        out_shape=jax.ShapeDtypeStruct((length, LANES), BF),
        scratch_shapes=[pltpu.VMEM((held, LANES), F32)],
        compiler_params=pltpu.CompilerParams(vmem_limit_bytes=VMEM_LIMIT),
    )(offset, params, before)


def finish(layout, where, chunk, leftover, vectors, params, first, second):
    length = layout.columns * layout.piece
    steps = pl.cdiv(layout.rows, SWEEP)
    held = max(length, TILE + steps * SWEEP)
    vector_first = ROW_VEC - layout.start(layout.devices - 1)

    def kernel(place, sums, rest, vector, master, one, two, grads, new, new_one, new_two, wide):
        step = pl.program_id(0)
        shard = place[0]

        @pl.when(step == 0)
        def _():
            wide[pl.ds(0, length), :] = sums[...].astype(F32)
            used = 0
            for owner, rows in layout.leftover():

                @pl.when(shard == owner)
                def _(used=used, rows=rows):
                    wide[pl.ds(0, rows), :] += rest[pl.ds(used, rows), :].astype(F32)

                used += rows

            @pl.when(shard == layout.devices - 1)
            def _():
                wide[pl.ds(vector_first, VEC_ROWS), :] += vector[...]

        grad = wide[pl.ds(place[1] + step * SWEEP, SWEEP), :]
        row = lax.broadcasted_iota(jnp.int32, (SWEEP, LANES), 0)
        matrix_part = row < ROW_VEC - shard * layout.rows - step * SWEEP
        value = master[...].reshape(SWEEP, LANES)
        results = adam_update(
            value,
            grad,
            one[...].reshape(SWEEP, LANES),
            two[...].reshape(SWEEP, LANES),
            matrix_part,
        )
        for ref, result in zip((grads, new, new_one, new_two), (grad,) + results):
            ref[...] = result.reshape(1, SWEEP * LANES)

    flat = pl.BlockSpec((1, SWEEP * LANES), lambda i: (0, i))

    def whole(array):
        return pl.BlockSpec(array.shape, lambda i: (0, 0))

    return pl.pallas_call(
        kernel,
        name="finish",
        grid=(steps,),
        in_specs=[
            pl.BlockSpec(memory_space=pltpu.SMEM),
            whole(chunk),
            whole(leftover),
            whole(vectors),
            flat,
            flat,
            flat,
        ],
        out_specs=[flat] * 4,
        out_shape=[jax.ShapeDtypeStruct(params.shape, F32)] * 4,
        scratch_shapes=[pltpu.VMEM((held, LANES), F32)],
        compiler_params=pltpu.CompilerParams(vmem_limit_bytes=VMEM_LIMIT),
    )(where, chunk, leftover, vectors, params, first, second)


def shards(layout, inputs, counts, params, first_moment, second_moment, out_cotangent):
    local_rows = inputs.shape[1]
    shard = lax.axis_index(("dp", "ctx"))
    score_scale = HD ** (-0.5)
    everyone = column_groups(layout)
    chunk = 256

    place = jnp.stack(
        [lax.axis_index("dp") // 2, lax.axis_index("dp") % 2, lax.axis_index("ctx")]
    ).astype(jnp.int32)
    last = layout.devices - 1
    ending = params[0, -TILE * LANES :].reshape(TILE, LANES)
    before = lax.ppermute(ending, ("dp", "ctx"), [(index, index + 1) for index in range(last)])
    offset = ((shard * layout.rows) % TILE).astype(jnp.int32)
    chunk_rows = align(layout, params, before, offset.reshape(1))
    pieces = lax.all_to_all(
        chunk_rows.reshape(layout.columns, layout.piece, LANES),
        "dp",
        split_axis=0,
        concat_axis=0,
        tiled=True,
        axis_index_groups=everyone,
    )
    shared_first = pieces[: layout.first].reshape(-1, LANES)
    gathered_first, along = gather(layout, shared_first, 2)
    shared_rest = pieces[layout.first :].reshape(-1, LANES)
    shared_rest = lax.optimization_barrier((shared_rest, along))[0]
    gathered_rest, _ = gather(layout, shared_rest, 1)
    vector_first = ROW_VEC - layout.start(last)
    assert 0 <= vector_first and vector_first + VEC_ROWS <= layout.columns * layout.piece
    leftover = jnp.concatenate(
        [broadcast(layout, shard, owner, chunk_rows[:rows]) for owner, rows in layout.leftover()]
    )
    spread = chunk_rows[vector_first : vector_first + VEC_ROWS]
    spread = broadcast(layout, shard, last, spread)
    flat_vectors = spread.reshape(-1).astype(F32)
    vectors = []
    used = 0
    for length in VEC_LENGTHS:
        vectors.append(flat_vectors[used : used + length])
        used += length
    (
        gain_one,
        shift_one,
        bias_query,
        bias_value,
        bias_out,
        gain_two,
        shift_two,
        bias_down,
        bias_up,
    ) = vectors

    residual = inputs[0].astype(F32)
    unit_one, inverse_one = norm_forward(residual)
    normed_round = (unit_one * gain_one + shift_one).astype(BF)
    qkv_weight = first_weights(layout, place, gathered_first, leftover)
    projected = dense(normed_round, qkv_weight)
    queries = ((projected[:, :D] + bias_query) * score_scale).astype(BF)
    keys = projected[:, D : 2 * D].astype(BF)
    values = (projected[:, 2 * D :] + bias_value).astype(BF)
    packed = to_heads(jnp.concatenate([queries, keys, values], -1), 3)
    out_weight, up_weight, down_weight = other_weights(layout, place, gathered_rest)
    mixed_heads, log_total = attend(counts, packed, chunk)
    mixed = from_heads(mixed_heads, 1)
    middle = residual + dense(mixed, out_weight) + bias_out
    unit_two, inverse_two = norm_forward(middle)
    normed_two_round = (unit_two * gain_two + shift_two).astype(BF)
    pre_gelu = dense(normed_two_round, up_weight) + bias_up
    activated = jax.nn.gelu(pre_gelu, approximate=True).astype(BF)
    output = (middle + dense(activated, down_weight) + bias_down).astype(BF)

    positions = lax.axis_index("ctx") * local_rows + jnp.arange(local_rows, dtype=jnp.int32)
    row_valid = (positions < counts[0])[:, None].astype(F32)
    grad_next = out_cotangent[0] * row_valid
    grad_bias_down = jnp.sum(grad_next, 0)
    grad_round = grad_next.astype(BF)
    grad_down = t_dot(activated, grad_round).astype(BF)
    grad_act = dot_t(grad_round, down_weight)
    gelu_back = jax.vjp(functools.partial(jax.nn.gelu, approximate=True), pre_gelu)[1]
    grad_pre = gelu_back(grad_act)[0]
    grad_bias_up = jnp.sum(grad_pre, 0)
    grad_pre_round = grad_pre.astype(BF)
    grad_up = t_dot(normed_two_round, grad_pre_round).astype(BF)
    middle_group = layout.columns // 2
    (terms,) = gradient_pieces(
        layout, place, (middle_group, layout.columns), {"up": grad_up, "down": grad_down}
    )
    grad_pre_round, terms = lax.optimization_barrier((grad_pre_round, terms))
    sum_last = scatter(layout, terms)
    grad_normed_two = dot_t(grad_pre_round, up_weight)
    grad_gain_two = jnp.sum(grad_normed_two * unit_two, 0)
    grad_shift_two = jnp.sum(grad_normed_two, 0)
    grad_middle = grad_next + norm_back(grad_normed_two, unit_two, inverse_two, gain_two)
    grad_bias_out = jnp.sum(grad_middle, 0)
    middle_round = grad_middle.astype(BF)
    grad_out = t_dot(mixed, middle_round).astype(BF)
    grad_mixed = dot_t(middle_round, out_weight).astype(BF)
    grad_mixed_heads = to_heads(grad_mixed, 1)
    (terms,) = gradient_pieces(
        layout, place, (layout.first, middle_group), {"out": grad_out, "up": grad_up}
    )
    sum_middle = scatter(layout, terms)
    grad_packed, sums = attend_back(counts, packed, log_total, grad_mixed_heads, chunk)
    grad_projected = from_heads(grad_packed, 3)
    grad_qkv = t_dot(normed_round, grad_projected).astype(BF)
    terms, leftover_terms = gradient_pieces(
        layout, place, (0, layout.first), {"qkv": grad_qkv}, leftover=True
    )
    sum_first = scatter(layout, terms)
    grad_normed_one = dot_t(grad_projected, qkv_weight)
    grad_gain_one = jnp.sum(grad_normed_one * unit_one, 0)
    grad_shift_one = jnp.sum(grad_normed_one, 0)
    input_grad = grad_middle + norm_back(grad_normed_one, unit_one, inverse_one, gain_one)

    share = D // layout.ctx
    where = (lax.axis_index("ctx") * share,)
    sum_q, sum_v = (sums[:, 0].reshape(-1), sums[:, 1].reshape(-1))
    grad_bias_query = lax.dynamic_update_slice(jnp.zeros((D,), F32), sum_q, where)
    grad_bias_value = lax.dynamic_update_slice(jnp.zeros((D,), F32), sum_v, where)
    vector_terms = [
        grad_gain_one,
        grad_shift_one,
        grad_bias_query,
        grad_bias_value,
        grad_bias_out,
        grad_gain_two,
        grad_shift_two,
        grad_bias_down,
        grad_bias_up,
    ]
    padding = jnp.zeros((VEC_ROWS * LANES - sum(VEC_LENGTHS),), F32)
    vector_grads = jnp.concatenate(vector_terms + [padding]).reshape(VEC_ROWS, LANES)
    vector_grads = sum_to(layout, last, vector_grads)
    used = 0
    sums_left = []
    for owner, rows in layout.leftover():
        part = leftover_terms[used : used + rows]
        sums_left.append(sum_to(layout, owner, part))
        used += rows
    leftover_sum = jnp.concatenate(sums_left)

    summed = jnp.concatenate([sum_first, sum_middle, sum_last])
    held = lax.all_to_all(
        summed.reshape(layout.columns, layout.piece, LANES),
        "dp",
        split_axis=0,
        concat_axis=0,
        tiled=True,
        axis_index_groups=everyone,
    )
    param_grads, new_params, new_first, new_second = finish(
        layout,
        jnp.stack([shard.astype(jnp.int32), offset]),
        held.reshape(-1, LANES),
        leftover_sum,
        vector_grads,
        params,
        first_moment,
        second_moment,
    )
    return (output[None], input_grad[None], param_grads, new_params, new_first, new_second)


def solution(mesh):
    placed = (
        P("dp", "ctx", None),
        P("dp"),
        P(None, ("dp", "ctx")),
        P(None, ("dp", "ctx")),
        P(None, ("dp", "ctx")),
        P("dp", "ctx", None),
    )
    dp, ctx = (mesh.shape["dp"], mesh.shape["ctx"])

    def program(inputs, counts, params, first_moment, second_moment, out_cotangent):
        layout = Layout(dp, ctx, params.shape[1] // (dp * ctx))

        def body(*arguments):
            return shards(layout, *arguments)

        return jax.shard_map(
            body,
            mesh=mesh,
            in_specs=placed,
            out_specs=(
                P("dp", "ctx", None),
                P("dp", "ctx", None),
                P(None, ("dp", "ctx")),
                P(None, ("dp", "ctx")),
                P(None, ("dp", "ctx")),
                P(None, ("dp", "ctx")),
            ),
            check_vma=False,
        )(inputs, counts, params, first_moment, second_moment, out_cotangent)

    return program
```

```python
import functools
import math

import jax
import jax.numpy as jnp
from jax import lax
from jax.experimental import pallas as pl
from jax.experimental.pallas import tpu as pltpu
from jax.sharding import PartitionSpec as P


D = 1152
HD = 72
FF = 4304
LANES = 128
TILE = 16

norm_epsilon = 1e-06
beta_one = 0.9
beta_two = 0.95
adam_epsilon = 1e-08
adam_step = 3
rate_matrix = 0.005
rate_vector = 0.1
weight_decay = 0.1
masked_score = -1e30

BF = jnp.bfloat16
F32 = jnp.float32

QKV_BLOCKS = 3 * D // LANES
D_BLOCKS = D // LANES
ROW_QKV = 0
ROW_OUT = D * QKV_BLOCKS
ROW_UP = ROW_OUT + D * D_BLOCKS
ROW_DOWN = ROW_UP + D * FF // LANES
ROW_VEC = ROW_DOWN + FF * D_BLOCKS
VEC_ROWS = 128
VEC_LENGTHS = [D] * 8 + [FF]

UP_GROUP = LANES // math.gcd(FF, LANES)
UP_STRIDE = UP_GROUP * FF // LANES
UP_BLOCKS = -(-FF // LANES)
UP_TAIL = FF - (UP_BLOCKS - 1) * LANES
STEPS = 9
BLOCK = D // STEPS
DOWN_BLOCK = -(-FF // (STEPS * TILE)) * TILE
VMEM_LIMIT = 60 * 1024 * 1024


class Layout:
    def __init__(self, dp, ctx, shard_length):
        self.dp, self.ctx = dp, ctx
        self.devices = dp * ctx
        self.columns = dp // 2
        self.rows = shard_length // LANES
        longest = (self.rows + TILE - 1) // TILE
        self.piece = -(-longest // self.columns) * TILE
        self.group_shards = 2 * ctx
        self.first = ROW_OUT // (self.group_shards * self.rows)
        self.last_piece = self.rows // TILE * TILE - (self.columns - 1) * self.piece
        assert self.first > 0 and self.last_piece > 0

    def start(self, shard):
        return shard * self.rows // TILE * TILE

    def group_start(self, group):
        return self.start(group * self.group_shards)

    def group_end(self, group):
        return self.start(group * self.group_shards - 1) + self.columns * self.piece

    def leftover(self):
        shard = self.first * self.group_shards
        found = []
        while self.start(shard) < ROW_OUT:
            found.append((shard, min(ROW_OUT, self.start(shard + 1)) - self.start(shard)))
            shard += 1
        return found


def lane_index(rows):
    return lax.broadcasted_iota(jnp.int32, (rows, LANES), 1)


def rows_to_matrix(flat, base, rows, blocks, wide, out):
    wide[pl.ds(0, rows * blocks), :] = flat[pl.ds(base, rows * blocks), :].astype(F32)
    for block in range(blocks):
        part = wide[pl.ds(block, rows, stride=blocks), :]
        out[:, block * LANES : (block + 1) * LANES] = part.astype(BF)


def matrix_to_rows(matrix, rows, blocks, wide, flat, base):
    for block in range(blocks):
        part = matrix[:, block * LANES : (block + 1) * LANES].astype(F32)
        wide[pl.ds(block, rows, stride=blocks), :] = part
    flat[pl.ds(base, rows * blocks), :] = wide[pl.ds(0, rows * blocks), :].astype(BF)


def rows_to_up(flat, base, wide, square, out):
    groups = BLOCK // UP_GROUP
    length = groups * UP_STRIDE
    wide[pl.ds(0, length), :] = flat[pl.ds(base, length), :].astype(F32)
    lanes = lane_index(groups)
    for row in range(UP_GROUP):
        first, shift = divmod(row * FF, LANES)
        held = None
        for block in range(UP_BLOCKS + 1):
            if block == UP_BLOCKS and shift + UP_TAIL <= LANES:
                piece = held
            else:
                piece = wide[pl.ds(first + block, groups, stride=UP_STRIDE), :]
                if shift:
                    piece = pltpu.roll(piece, LANES - shift, 1)
            if block:
                value = jnp.where(lanes < LANES - shift, held, piece) if shift else held
                square[block - 1, pl.ds(row, groups, stride=UP_GROUP), :] = value
            held = piece
    for block in range(UP_BLOCKS):
        first, last = (block * LANES, min(FF, (block + 1) * LANES))
        out[:, first:last] = square[block, :, : last - first].astype(BF)


def up_to_rows(matrix, square, wide, flat, base):
    groups = BLOCK // UP_GROUP
    length = groups * UP_STRIDE
    for block in range(UP_BLOCKS):
        first, last = (block * LANES, min(FF, (block + 1) * LANES))
        square[block, :, : last - first] = matrix[:, first:last].astype(F32)
    lanes = lane_index(groups)
    held = None
    for row in range(UP_GROUP):
        first, shift = divmod(row * FF, LANES)
        for block in range(UP_BLOCKS):
            piece = square[block, pl.ds(row, groups, stride=UP_GROUP), :]
            if shift:
                piece = pltpu.roll(piece, shift, 1)
                value = jnp.where(lanes < shift, held, piece)
            else:
                value = piece
            if block == UP_BLOCKS - 1 and shift + UP_TAIL < LANES:
                held = value
            else:
                wide[pl.ds(first + block, groups, stride=UP_STRIDE), :] = value
                held = piece
    flat[pl.ds(base, length), :] = wide[pl.ds(0, length), :].astype(BF)


def fetch(layout, place, groups, origin, sources, flat, sem):
    low, high = groups
    for ref, (column, core, key) in sources:
        device_column = jnp.bitwise_xor(place[0], column)
        device_core = jnp.bitwise_xor(place[1], core)
        row = jnp.bitwise_xor(place[2], key)

        def body(index, _, ref=ref, device_column=device_column, device_core=device_core, row=row):
            shard = (low + index) * layout.group_shards + device_core * layout.ctx + row
            start = shard * layout.rows // TILE * TILE
            target = pl.multiple_of(start + device_column * layout.piece - origin, TILE)
            source = pl.multiple_of(index * layout.piece, TILE)

            def copy(offset, rows):
                pltpu.make_async_copy(
                    ref.at[pl.ds(source + offset, rows), :],
                    flat.at[pl.ds(target + offset, rows), :],
                    sem,
                ).start()

            is_last = device_column == layout.columns - 1
            longer = shard * layout.rows % TILE + layout.rows % TILE >= TILE

            @pl.when(jnp.logical_not(is_last))
            def _():
                copy(0, layout.piece)

            @pl.when(is_last)
            def _():
                copy(0, layout.last_piece)

            @pl.when(jnp.logical_and(is_last, longer))
            def _():
                copy(layout.last_piece, TILE)

            return 0

        lax.fori_loop(0, high - low, body, 0)


def flat_of(gathered):
    return [array for array, _ in gathered]


def first_weights(layout, place, gathered, leftover):
    inside = layout.group_start(layout.first)
    length = inside + leftover.shape[0]
    assert length == ROW_OUT
    arrays = flat_of(gathered)

    def kernel(place_ref, *refs):
        sources, (extra, qkv, flat, wide, sem) = (refs[: len(arrays)], refs[len(arrays) :])
        step = pl.program_id(0)

        @pl.when(step == 0)
        def _():
            named = [(ref, entry) for ref, (_, entry) in zip(sources, gathered)]
            fetch(layout, place_ref, (0, layout.first), 0, named, flat, sem)
            pltpu.make_async_copy(
                extra, flat.at[pl.ds(inside, leftover.shape[0]), :], sem
            ).start()
            pltpu.make_async_copy(flat, flat, sem).wait()

        base = pl.multiple_of(step * (BLOCK * QKV_BLOCKS), TILE)
        rows_to_matrix(flat, base, BLOCK, QKV_BLOCKS, wide, qkv)

    return pl.pallas_call(
        kernel,
        name="first_weights",
        grid=(STEPS,),
        in_specs=[pl.BlockSpec(memory_space=pltpu.SMEM)]
        + [pl.BlockSpec(memory_space=pl.ANY)] * (len(arrays) + 1),
        out_specs=pl.BlockSpec((BLOCK, 3 * D), lambda i: (i, 0)),
        out_shape=jax.ShapeDtypeStruct((D, 3 * D), BF),
        scratch_shapes=[
            pltpu.VMEM((length, LANES), BF),
            pltpu.VMEM((BLOCK * QKV_BLOCKS, LANES), F32),
            pltpu.SemaphoreType.DMA,
        ],
        compiler_params=pltpu.CompilerParams(vmem_limit_bytes=VMEM_LIMIT),
    )(place, *arrays, leftover)


def other_weights(layout, place, gathered):
    origin = layout.group_start(layout.first)
    length = layout.start(layout.devices) - origin
    padded = max(length, ROW_DOWN - origin + STEPS * DOWN_BLOCK * D_BLOCKS)
    up_length = BLOCK // UP_GROUP * UP_STRIDE
    arrays = flat_of(gathered)

    def kernel(place_ref, *refs):
        sources = refs[: len(arrays)]
        out_w, up_w, down_w, flat, wide, square, sem = refs[len(arrays) :]
        step = pl.program_id(0)

        @pl.when(step == 0)
        def _():
            named = [(ref, entry) for ref, (_, entry) in zip(sources, gathered)]
            fetch(layout, place_ref, (layout.first, layout.columns), origin, named, flat, sem)
            whole = flat.at[pl.ds(0, length), :]
            pltpu.make_async_copy(whole, whole, sem).wait()

        base = pl.multiple_of(ROW_OUT - origin + step * (BLOCK * D_BLOCKS), TILE)
        rows_to_matrix(flat, base, BLOCK, D_BLOCKS, wide, out_w)
        base = pl.multiple_of(ROW_UP - origin + step * up_length, TILE)
        rows_to_up(flat, base, wide, square, up_w)
        base = pl.multiple_of(ROW_DOWN - origin + step * (DOWN_BLOCK * D_BLOCKS), TILE)
        rows_to_matrix(flat, base, DOWN_BLOCK, D_BLOCKS, wide, down_w)

    return pl.pallas_call(
        kernel,
        name="other_weights",
        grid=(STEPS,),
        in_specs=[pl.BlockSpec(memory_space=pltpu.SMEM)]
        + [pl.BlockSpec(memory_space=pl.ANY)] * len(arrays),
        out_specs=[
            pl.BlockSpec((BLOCK, D), lambda i: (i, 0)),
            pl.BlockSpec((BLOCK, FF), lambda i: (i, 0)),
            pl.BlockSpec((DOWN_BLOCK, D), lambda i: (i, 0)),
        ],
        out_shape=[
            jax.ShapeDtypeStruct((D, D), BF),
            jax.ShapeDtypeStruct((D, FF), BF),
            jax.ShapeDtypeStruct((FF, D), BF),
        ],
        scratch_shapes=[
            pltpu.VMEM((padded, LANES), BF),
            pltpu.VMEM((max(up_length + 8, DOWN_BLOCK * D_BLOCKS), LANES), F32),
            pltpu.VMEM((UP_BLOCKS, BLOCK, LANES), F32),
            pltpu.SemaphoreType.DMA,
        ],
        compiler_params=pltpu.CompilerParams(vmem_limit_bytes=VMEM_LIMIT),
    )(place, *arrays)


MATRICES = {
    "qkv": (ROW_QKV, BLOCK, BLOCK * QKV_BLOCKS, 3 * D),
    "out": (ROW_OUT, BLOCK, BLOCK * D_BLOCKS, D),
    "up": (ROW_UP, BLOCK, BLOCK // UP_GROUP * UP_STRIDE, FF),
    "down": (ROW_DOWN, DOWN_BLOCK, DOWN_BLOCK * D_BLOCKS, D),
}


def gradient_pieces(layout, place, groups, matrices, leftover=False):
    low, high = layout.group_start(groups[0]), layout.group_end(groups[1])
    count = groups[1] - groups[0]
    names = list(matrices)
    plan = {}
    for name in names:
        first, _, stride, _ = MATRICES[name]
        blocks = [
            block
            for block in range(STEPS)
            if leftover
            or (first + block * stride < high and first + (block + 1) * stride > low)
        ]
        plan[name] = (first, blocks[0], len(blocks), stride)
    origin = min([low] + [first + b * stride for first, b, _, stride in plan.values()])
    end = max([high] + [first + (b + n) * stride for first, b, n, stride in plan.values()])
    steps = max(n for _, _, n, _ in plan.values())
    covered = min(first + b * stride for first, b, _, stride in plan.values())
    rows = layout.devices // 2 * count * layout.piece
    extra = ROW_OUT - layout.group_start(layout.first)

    def kernel(place_ref, *refs):
        inputs, refs = (refs[: len(names)], refs[len(names) :])
        outputs, (flat, wide, square, sem) = (refs[:-4], refs[-4:])
        step = pl.program_id(0)
        if covered > low:

            @pl.when(step == 0)
            def _():
                flat[pl.ds(low - origin, covered - low), :] = jnp.zeros((covered - low, LANES), BF)

        for ref, name in zip(inputs, names):
            first, block, number, stride = plan[name]

            def convert(ref=ref, name=name, first=first, block=block, stride=stride):
                base = pl.multiple_of(first - origin + (block + step) * stride, TILE)
                if name == "up":
                    up_to_rows(ref, square, wide, flat, base)
                else:
                    blocks = QKV_BLOCKS if name == "qkv" else D_BLOCKS
                    matrix_to_rows(ref, stride // blocks, blocks, wide, flat, base)

            if number == steps:
                convert()
            else:
                pl.when(step < number)(convert)

        @pl.when(step == steps - 1)
        def _():
            if "down" in names:
                tail = end - ROW_VEC
                flat[pl.ds(ROW_VEC - origin, tail), :] = jnp.zeros((tail, LANES), BF)

            def body(index, _):
                group = groups[0] + index % count
                key = index // count
                row = jnp.bitwise_xor(place_ref[2], key % layout.ctx)
                column = jnp.bitwise_xor(place_ref[0], key // layout.ctx)
                for bit in range(2):
                    core = jnp.bitwise_xor(place_ref[1], bit)
                    shard = group * layout.group_shards + core * layout.ctx + row
                    start = shard * layout.rows // TILE * TILE
                    source = pl.multiple_of(start + column * layout.piece - origin, TILE)
                    target = pl.multiple_of(index * layout.piece, TILE)
                    pltpu.make_async_copy(
                        flat.at[pl.ds(source, layout.piece), :],
                        outputs[bit].at[pl.ds(target, layout.piece), :],
                        sem,
                    ).start()
                return 0

            lax.fori_loop(0, layout.devices // 2 * count, body, 0)
            pltpu.make_async_copy(outputs[0], outputs[0], sem).wait()
            pltpu.make_async_copy(outputs[1], outputs[1], sem).wait()
            if leftover:
                copy = pltpu.make_async_copy(
                    flat.at[pl.ds(ROW_OUT - extra - origin, extra), :], outputs[2], sem
                )
                copy.start()
                copy.wait()

    def spec(name):
        _, block, number, _ = plan[name]
        _, height, _, width = MATRICES[name]
        return pl.BlockSpec(
            (height, width), lambda i: (block + jnp.minimum(i, number - 1), 0)
        )

    shapes = [jax.ShapeDtypeStruct((rows, LANES), BF)] * 2
    if leftover:
        shapes.append(jax.ShapeDtypeStruct((extra, LANES), BF))
    wide_rows = max(stride for _, _, _, stride in plan.values())
    return pl.pallas_call(
        kernel,
        grid=(steps,),
        in_specs=[pl.BlockSpec(memory_space=pltpu.SMEM)] + [spec(name) for name in names],
        out_specs=[pl.BlockSpec(memory_space=pl.ANY)] * len(shapes),
        out_shape=shapes,
        scratch_shapes=[
            pltpu.VMEM((end - origin, LANES), BF),
            pltpu.VMEM((wide_rows, LANES), F32),
            pltpu.VMEM((UP_BLOCKS if "up" in names else 1, BLOCK, LANES), F32),
            pltpu.SemaphoreType.DMA,
        ],
        compiler_params=pltpu.CompilerParams(vmem_limit_bytes=VMEM_LIMIT),
    )(place, *[matrices[name] for name in names])


def dot_t(left, right):
    return lax.dot_general(left, right, (((1,), (1,)), ((), ())), preferred_element_type=F32)


def t_dot(left, right):
    return lax.dot_general(left, right, (((0,), (0,)), ((), ())), preferred_element_type=F32)


def dense(left, right):
    return jnp.dot(left, right, preferred_element_type=F32)


def masked(scores, count):
    columns = lax.broadcasted_iota(jnp.int32, scores.shape, 1)
    return jnp.where(columns < count, scores, masked_score)


def unpack_heads(place, blocks, parts, heads, held):
    for key, block in enumerate(blocks):
        rows = block.shape[0]
        row = pl.multiple_of(jnp.bitwise_xor(place[2], key) * rows, TILE)
        for part in range(parts):
            for head in range(heads):
                first = (part * heads + head) * HD
                held[part, head, pl.ds(row, rows), :] = block[:, first : first + HD]


def pack_heads(place, held, parts, heads, blocks):
    for key, block in enumerate(blocks):
        rows = block.shape[0]
        row = pl.multiple_of(jnp.bitwise_xor(place[2], key) * rows, TILE)
        block[...] = jnp.concatenate(
            [held[part, head, pl.ds(row, rows), :] for part in range(parts) for head in range(heads)],
            -1,
        )


def attend(counts, place, blocks, chunk):
    rows, width = blocks[0].shape
    heads, ctx = (width // (3 * HD), len(blocks))
    length = rows * ctx

    def kernel(count, place_ref, *refs):
        sources, mixed = (refs[:ctx], refs[ctx : 2 * ctx])
        log_total, held, made = refs[2 * ctx :]
        head = pl.program_id(0)

        @pl.when(head == 0)
        def _():
            unpack_heads(place_ref, sources, 3, heads, held)

        for first in range(0, length, chunk):
            queries = held[0, head, pl.ds(first, chunk), :]
            scores = masked(dot_t(queries, held[1, head]), count[0])
            top = jnp.max(scores, -1, keepdims=True)
            exponent = jnp.exp(scores - top)
            total = jnp.sum(exponent, -1, keepdims=True)
            probs = (exponent / total).astype(BF)
            made[0, head, pl.ds(first, chunk), :] = dense(probs, held[2, head]).astype(BF)
            log_total[0, first : first + chunk, :] = top + jnp.log(total)

        @pl.when(head == heads - 1)
        def _():
            pack_heads(place_ref, made, 1, heads, mixed)

    outputs = pl.pallas_call(
        kernel,
        name="attend",
        grid=(heads,),
        in_specs=[pl.BlockSpec(memory_space=pltpu.SMEM)] * 2
        + [pl.BlockSpec((rows, width), lambda h: (0, 0))] * ctx,
        out_specs=[pl.BlockSpec((rows, heads * HD), lambda h: (0, 0))] * ctx
        + [pl.BlockSpec((1, length, 1), lambda h: (h, 0, 0))],
        out_shape=[jax.ShapeDtypeStruct((rows, heads * HD), BF)] * ctx
        + [jax.ShapeDtypeStruct((heads, length, 1), F32)],
        scratch_shapes=[
            pltpu.VMEM((3, heads, length, HD), BF),
            pltpu.VMEM((1, heads, length, HD), BF),
        ],
        compiler_params=pltpu.CompilerParams(vmem_limit_bytes=VMEM_LIMIT),
    )(counts, place, *blocks)
    return outputs[:ctx], outputs[ctx]


def attend_back(counts, place, blocks, log_total, grad_blocks, chunk):
    rows, width = blocks[0].shape
    heads, ctx = (width // (3 * HD), len(blocks))
    length = rows * ctx
    scale = HD ** (-0.5)

    def kernel(count, place_ref, logs, *refs):
        sources, grads, made = (refs[:ctx], refs[ctx : 2 * ctx], refs[2 * ctx : 3 * ctx])
        sums, held, grad, results, acc_k, acc_v = refs[3 * ctx :]
        head = pl.program_id(0)

        @pl.when(head == 0)
        def _():
            unpack_heads(place_ref, sources, 3, heads, held)
            unpack_heads(place_ref, grads, 1, heads, grad)

        acc_k[...] = jnp.zeros_like(acc_k)
        acc_v[...] = jnp.zeros_like(acc_v)
        total_q = jnp.zeros((1, HD), F32)
        for first in range(0, length, chunk):
            part = pl.ds(first, chunk)
            queries = held[0, head, part, :]
            scores = masked(dot_t(queries, held[1, head]), count[0])
            probs = jnp.exp(scores - logs[0, part, :])
            grad_heads = grad[0, head, part, :]
            grad_probs = dot_t(grad_heads, held[2, head])
            delta = jnp.sum(probs * grad_probs, -1, keepdims=True)
            grad_scores = (probs * (grad_probs - delta)).astype(BF)
            grad_query = dense(grad_scores, held[1, head]) * scale
            total_q = total_q + jnp.sum(grad_query, 0, keepdims=True)
            results[0, head, part, :] = grad_query.astype(BF)
            acc_k[...] += t_dot(grad_scores, queries)
            acc_v[...] += t_dot(probs.astype(BF), grad_heads)
        results[1, head] = acc_k[...].astype(BF)
        results[2, head] = acc_v[...].astype(BF)
        sums[0, 0:1, :] = total_q
        sums[0, 1:2, :] = jnp.sum(acc_v[...], 0, keepdims=True)

        @pl.when(head == heads - 1)
        def _():
            pack_heads(place_ref, results, 3, heads, made)

    wide = pl.BlockSpec((rows, width), lambda h: (0, 0))
    outputs = pl.pallas_call(
        kernel,
        name="attend_back",
        grid=(heads,),
        in_specs=[pl.BlockSpec(memory_space=pltpu.SMEM)] * 2
        + [pl.BlockSpec((1, length, 1), lambda h: (h, 0, 0))]
        + [wide] * ctx
        + [pl.BlockSpec((rows, heads * HD), lambda h: (0, 0))] * ctx,
        out_specs=[wide] * ctx + [pl.BlockSpec((1, 2, HD), lambda h: (h, 0, 0))],
        out_shape=[jax.ShapeDtypeStruct((rows, width), BF)] * ctx
        + [jax.ShapeDtypeStruct((heads, 2, HD), F32)],
        scratch_shapes=[
            pltpu.VMEM((3, heads, length, HD), BF),
            pltpu.VMEM((1, heads, length, HD), BF),
            pltpu.VMEM((3, heads, length, HD), BF),
            pltpu.VMEM((length, HD), F32),
            pltpu.VMEM((length, HD), F32),
        ],
        compiler_params=pltpu.CompilerParams(vmem_limit_bytes=VMEM_LIMIT),
    )(counts, place, log_total, *blocks, *grad_blocks)
    return outputs[:ctx], outputs[ctx]


def norm_forward(residual):
    centre = residual - jnp.mean(residual, -1, keepdims=True)
    inverse = lax.rsqrt(jnp.mean(centre * centre, -1, keepdims=True) + norm_epsilon)
    return (centre * inverse, inverse)


def norm_back(grad_normed, unit, inverse, gain):
    scaled = grad_normed * gain
    return inverse * (
        scaled
        - jnp.mean(scaled, -1, keepdims=True)
        - unit * jnp.mean(scaled * unit, -1, keepdims=True)
    )


def adam_update(master, grads, first, second, matrix_part):
    first_new = beta_one * first + (1.0 - beta_one) * grads
    second_new = beta_two * second + (1.0 - beta_two) * grads * grads
    first_hat = first_new / (1.0 - beta_one**adam_step)
    second_hat = second_new / (1.0 - beta_two**adam_step)
    rate = jnp.where(matrix_part, rate_matrix, rate_vector)
    decay = jnp.where(matrix_part, weight_decay, 0.0)
    updated = master - rate * (first_hat / (jnp.sqrt(second_hat) + adam_epsilon) + decay * master)
    return (updated, first_new, second_new)


def exchange(array, axis, bit):
    size = lax.axis_size(axis)
    return lax.ppermute(array, axis, [(index, index ^ bit) for index in range(size)])


def pick(index, choices):
    picked = choices[0]
    for position, choice in enumerate(choices[1:], 1):
        picked = jnp.where(index == position, choice, picked)
    return picked


def to_heads(array, parts):
    ctx = lax.axis_size("ctx")
    rows = array.shape[0]
    split = array.reshape(rows, parts, ctx, D // ctx).transpose(2, 0, 1, 3)
    split = split.reshape(ctx, rows, parts * D // ctx)
    place = lax.axis_index("ctx")
    blocks = [
        lax.dynamic_index_in_dim(split, place ^ key, keepdims=False) for key in range(ctx)
    ]
    return blocks[:1] + [exchange(blocks[key], "ctx", key) for key in range(1, ctx)]


def from_heads(blocks, parts):
    ctx = len(blocks)
    held = list(blocks[:1]) + [exchange(blocks[key], "ctx", key) for key in range(1, ctx)]
    place = lax.axis_index("ctx")
    ordered = [
        pick(place, [held[index ^ position] for position in range(ctx)]) for index in range(ctx)
    ]
    share = D // ctx
    return jnp.concatenate(
        [block[:, part * share : (part + 1) * share] for part in range(parts) for block in ordered],
        -1,
    )


def add(*arrays):
    return functools.reduce(jnp.add, [array.astype(F32) for array in arrays]).astype(BF)


def gather(layout, share, behind=None):
    held = {0: share}
    bit = 1
    while bit < layout.ctx:
        held.update({key ^ bit: exchange(held[key], "ctx", bit) for key in list(held)})
        bit *= 2
    arrays = []
    for key in range(layout.ctx):
        own = held[key]
        if behind is not None:
            own = lax.optimization_barrier((own, behind))[0]
        found = [(own, (0, 0, key))]
        if layout.columns == 4:
            by_x = exchange(own, "dp", 2)
            by_y = exchange(own, "dp", 4)
            if key % 2:
                across = exchange(by_y, "dp", 2)
            else:
                across = exchange(by_x, "dp", 4)
            found += [(by_x, (1, 0, key)), (by_y, (2, 0, key)), (across, (3, 0, key))]
        else:
            bit = 1
            while bit < layout.columns:
                found += [
                    (exchange(array, "dp", 2 * bit), (place[0] ^ bit, 0, key))
                    for array, place in found
                ]
                bit *= 2
        arrays += found
    last = arrays[-2][0]
    arrays += [(exchange(array, "dp", 1), (place[0], 1, place[2])) for array, place in arrays]
    return arrays, held[layout.ctx - 1], last


def scatter(layout, kept, sent):
    received = exchange(sent, "dp", 1)
    half = kept.shape[0] // layout.columns // 2
    parts = lax.optimization_barrier(
        [
            add(kept[index * half : (index + 1) * half], received[index * half : (index + 1) * half])
            for index in range(2 * layout.columns)
        ]
    )
    if layout.columns == 4:
        low = add(parts[2], exchange(parts[6], "dp", 4))
        high = add(parts[5], exchange(parts[7], "dp", 2))
        over_x = exchange(parts[3], "dp", 2)
        over_y = exchange(parts[4], "dp", 4)
        low, high = (exchange(low, "dp", 2), exchange(high, "dp", 4))
        summed = [add(parts[0], low, over_y), add(parts[1], over_x, high)]
    else:
        bit = layout.columns
        while bit > 1:
            parts = [
                add(parts[index], exchange(parts[index ^ bit], "dp", bit))
                for index in range(bit)
            ]
            bit //= 2
        summed = parts
    each = layout.ctx // 2
    length = half // each
    held = {
        key: summed[key // each][(key % each) * length : (key % each + 1) * length]
        for key in range(layout.ctx)
    }
    bit = 1
    while bit < layout.ctx:
        for key in [key for key in held if key & bit]:
            moved = exchange(held.pop(key), "ctx", bit)
            held[key ^ bit] = add(held[key ^ bit], moved)
        bit *= 2
    return held[0]


def bits(layout):
    found = []
    for unit, size in ((1, layout.ctx), (2 * layout.ctx, layout.columns), (layout.ctx, 2)):
        bit = 1
        while bit < size:
            found.append(bit * unit)
            bit *= 2
    return found


def broadcast(layout, shard, owner, held):
    have = [owner]
    for bit in bits(layout):
        other = lax.ppermute(held, ("dp", "ctx"), [(index, index ^ bit) for index in have])
        have += [index ^ bit for index in have]
        held = jnp.where((shard & bit) != (owner & bit), other, held)
    return held


def sum_to(layout, owner, held):
    have = list(range(layout.devices))
    for bit in reversed(bits(layout)):
        senders = [index for index in have if (index & bit) != (owner & bit)]
        other = lax.ppermute(held, ("dp", "ctx"), [(index, index ^ bit) for index in senders])
        have = [index for index in have if index not in senders]
        held = (held.astype(F32) + other.astype(F32)).astype(held.dtype)
    return held


SWEEP = 512


def align(layout, place, params, before):
    length = layout.columns * layout.piece
    steps = pl.cdiv(layout.rows, SWEEP)
    held = max(TILE + steps * SWEEP, TILE + length)
    vector_first = ROW_VEC - layout.start(layout.devices - 1)
    assert 0 <= vector_first and vector_first + VEC_ROWS <= length
    starts = max(rows for _, rows in layout.leftover())

    def kernel(place_ref, rows, previous, *refs):
        outputs, wide = (refs[:-1], refs[-1])
        step = pl.program_id(0)

        @pl.when(step == 0)
        def _():
            wide[0:TILE, :] = previous[...]

        base = pl.multiple_of(TILE + step * SWEEP, TILE)
        wide[pl.ds(base, SWEEP), :] = rows[...].reshape(SWEEP, LANES)

        @pl.when(step == steps - 1)
        def _():
            first = TILE - place_ref[3]
            for key in range(layout.columns):
                row = first + jnp.bitwise_xor(place_ref[0], key) * layout.piece
                outputs[key][...] = wide[pl.ds(row, layout.piece), :].astype(BF)
            outputs[-2][...] = wide[pl.ds(first, starts), :].astype(BF)
            outputs[-1][...] = wide[pl.ds(first + vector_first, VEC_ROWS), :].astype(BF)

    heights = [layout.piece] * layout.columns + [starts, VEC_ROWS]
    return pl.pallas_call(
        kernel,
        name="align",
        grid=(steps,),
        in_specs=[
            pl.BlockSpec(memory_space=pltpu.SMEM),
            pl.BlockSpec((1, SWEEP * LANES), lambda i: (0, i)),
            pl.BlockSpec((TILE, LANES), lambda i: (0, 0)),
        ],
        out_specs=[pl.BlockSpec((height, LANES), lambda i: (0, 0)) for height in heights],
        out_shape=[jax.ShapeDtypeStruct((height, LANES), BF) for height in heights],
        scratch_shapes=[pltpu.VMEM((held, LANES), F32)],
        compiler_params=pltpu.CompilerParams(vmem_limit_bytes=VMEM_LIMIT),
    )(place, params, before)


def finish(layout, place, pieces, leftover, vectors, params, first, second):
    length = layout.columns * layout.piece
    steps = pl.cdiv(layout.rows, SWEEP)
    held = max(length, TILE + steps * SWEEP)
    vector_first = ROW_VEC - layout.start(layout.devices - 1)
    columns = layout.columns

    def kernel(place_ref, *refs):
        sums, refs = (refs[:columns], refs[columns:])
        rest, vector, master, one, two, grads, new, new_one, new_two, wide = refs
        step = pl.program_id(0)
        shard = place_ref[4]

        @pl.when(step == 0)
        def _():
            for key in range(columns):
                row = jnp.bitwise_xor(place_ref[0], key) * layout.piece
                row = pl.multiple_of(row, TILE)
                wide[pl.ds(row, layout.piece), :] = sums[key][...].astype(F32)
            used = 0
            for owner, rows in layout.leftover():

                @pl.when(shard == owner)
                def _(used=used, rows=rows):
                    wide[pl.ds(0, rows), :] += rest[pl.ds(used, rows), :].astype(F32)

                used += rows

            @pl.when(shard == layout.devices - 1)
            def _():
                wide[pl.ds(vector_first, VEC_ROWS), :] += vector[...]

        grad = wide[pl.ds(place_ref[3] + step * SWEEP, SWEEP), :]
        row = lax.broadcasted_iota(jnp.int32, (SWEEP, LANES), 0)
        matrix_part = row < ROW_VEC - shard * layout.rows - step * SWEEP
        results = adam_update(
            master[...].reshape(SWEEP, LANES),
            grad,
            one[...].reshape(SWEEP, LANES),
            two[...].reshape(SWEEP, LANES),
            matrix_part,
        )
        for ref, result in zip((grads, new, new_one, new_two), (grad,) + results):
            ref[...] = result.reshape(1, SWEEP * LANES)

    flat = pl.BlockSpec((1, SWEEP * LANES), lambda i: (0, i))

    def whole(array):
        return pl.BlockSpec(array.shape, lambda i: (0, 0))

    return pl.pallas_call(
        kernel,
        name="finish",
        grid=(steps,),
        in_specs=[pl.BlockSpec(memory_space=pltpu.SMEM)]
        + [whole(piece) for piece in pieces]
        + [whole(leftover), whole(vectors), flat, flat, flat],
        out_specs=[flat] * 4,
        out_shape=[jax.ShapeDtypeStruct(params.shape, F32)] * 4,
        scratch_shapes=[pltpu.VMEM((held, LANES), F32)],
        compiler_params=pltpu.CompilerParams(vmem_limit_bytes=VMEM_LIMIT),
    )(place, *pieces, leftover, vectors, params, first, second)


def shards(layout, inputs, counts, params, first_moment, second_moment, out_cotangent):
    local_rows = inputs.shape[1]
    shard = lax.axis_index(("dp", "ctx"))
    score_scale = HD ** (-0.5)
    chunk = 256

    column = lax.axis_index("dp") // 2
    offset = (shard * layout.rows) % TILE
    place = jnp.stack(
        [column, lax.axis_index("dp") % 2, lax.axis_index("ctx"), offset, shard]
    ).astype(jnp.int32)
    last = layout.devices - 1
    ending = params[0, -TILE * LANES :].reshape(TILE, LANES)
    before = lax.ppermute(ending, ("dp", "ctx"), [(index, index + 1) for index in range(last)])
    aligned = align(layout, place, params, before)
    shares = list(aligned[:1]) + [
        exchange(aligned[key], "dp", 2 * key) for key in range(1, layout.columns)
    ]
    groups = [
        pick(column, [shares[index ^ position] for position in range(layout.columns)])
        for index in range(layout.columns)
    ]
    gathered_first, along, behind = gather(layout, jnp.concatenate(groups[: layout.first]))
    shared_rest = jnp.concatenate(groups[layout.first :])
    shared_rest = lax.optimization_barrier((shared_rest, along))[0]
    gathered_rest, _, _ = gather(layout, shared_rest, behind)
    leftover = jnp.concatenate(
        [broadcast(layout, shard, owner, aligned[-2][:rows]) for owner, rows in layout.leftover()]
    )
    spread = broadcast(layout, shard, last, aligned[-1])
    flat_vectors = spread.reshape(-1).astype(F32)
    vectors = []
    used = 0
    for length in VEC_LENGTHS:
        vectors.append(flat_vectors[used : used + length])
        used += length
    (
        gain_one,
        shift_one,
        bias_query,
        bias_value,
        bias_out,
        gain_two,
        shift_two,
        bias_down,
        bias_up,
    ) = vectors

    residual = inputs[0].astype(F32)
    unit_one, inverse_one = norm_forward(residual)
    normed_round = (unit_one * gain_one + shift_one).astype(BF)
    qkv_weight = first_weights(layout, place, gathered_first, leftover)
    projected = dense(normed_round, qkv_weight)
    queries = ((projected[:, :D] + bias_query) * score_scale).astype(BF)
    keys = projected[:, D : 2 * D].astype(BF)
    values = (projected[:, 2 * D :] + bias_value).astype(BF)
    packed = to_heads(jnp.concatenate([queries, keys, values], -1), 3)
    out_weight, up_weight, down_weight = other_weights(layout, place, gathered_rest)
    mixed_heads, log_total = attend(counts, place, packed, chunk)
    mixed = from_heads(mixed_heads, 1)
    middle = residual + dense(mixed, out_weight) + bias_out
    unit_two, inverse_two = norm_forward(middle)
    normed_two_round = (unit_two * gain_two + shift_two).astype(BF)
    pre_gelu = dense(normed_two_round, up_weight) + bias_up
    activated = jax.nn.gelu(pre_gelu, approximate=True).astype(BF)
    output = (middle + dense(activated, down_weight) + bias_down).astype(BF)

    positions = lax.axis_index("ctx") * local_rows + jnp.arange(local_rows, dtype=jnp.int32)
    row_valid = (positions < counts[0])[:, None].astype(F32)
    grad_next = out_cotangent[0] * row_valid
    grad_bias_down = jnp.sum(grad_next, 0)
    grad_round = grad_next.astype(BF)
    grad_down = t_dot(activated, grad_round).astype(BF)
    grad_act = dot_t(grad_round, down_weight)
    gelu_back = jax.vjp(functools.partial(jax.nn.gelu, approximate=True), pre_gelu)[1]
    grad_pre = gelu_back(grad_act)[0]
    grad_bias_up = jnp.sum(grad_pre, 0)
    grad_pre_round = grad_pre.astype(BF)
    grad_up = t_dot(normed_two_round, grad_pre_round).astype(BF)
    middle_group = layout.columns // 2
    terms = gradient_pieces(
        layout, place, (middle_group, layout.columns), {"up": grad_up, "down": grad_down}
    )
    grad_pre_round, terms = lax.optimization_barrier((grad_pre_round, terms))
    sum_last = scatter(layout, *terms)
    grad_normed_two = dot_t(grad_pre_round, up_weight)
    grad_gain_two = jnp.sum(grad_normed_two * unit_two, 0)
    grad_shift_two = jnp.sum(grad_normed_two, 0)
    grad_middle = grad_next + norm_back(grad_normed_two, unit_two, inverse_two, gain_two)
    grad_bias_out = jnp.sum(grad_middle, 0)
    middle_round = grad_middle.astype(BF)
    grad_out = t_dot(mixed, middle_round).astype(BF)
    grad_mixed = dot_t(middle_round, out_weight).astype(BF)
    grad_mixed_heads = to_heads(grad_mixed, 1)
    terms = gradient_pieces(
        layout, place, (layout.first, middle_group), {"out": grad_out, "up": grad_up}
    )
    sum_middle = scatter(layout, *terms)
    grad_packed, sums = attend_back(
        counts, place, packed, log_total, grad_mixed_heads, chunk
    )
    grad_projected = from_heads(grad_packed, 3)
    grad_qkv = t_dot(normed_round, grad_projected).astype(BF)
    *terms, leftover_terms = gradient_pieces(
        layout, place, (0, layout.first), {"qkv": grad_qkv}, leftover=True
    )
    grad_projected, leftover_terms, *terms = lax.optimization_barrier(
        (grad_projected, leftover_terms, *terms)
    )
    sum_first = scatter(layout, *terms)
    grad_normed_one = dot_t(grad_projected, qkv_weight)
    grad_gain_one = jnp.sum(grad_normed_one * unit_one, 0)
    grad_shift_one = jnp.sum(grad_normed_one, 0)
    input_grad = grad_middle + norm_back(grad_normed_one, unit_one, inverse_one, gain_one)

    share = D // layout.ctx
    where = (lax.axis_index("ctx") * share,)
    sum_q, sum_v = (sums[:, 0].reshape(-1), sums[:, 1].reshape(-1))
    grad_bias_query = lax.dynamic_update_slice(jnp.zeros((D,), F32), sum_q, where)
    grad_bias_value = lax.dynamic_update_slice(jnp.zeros((D,), F32), sum_v, where)
    vector_terms = [
        grad_gain_one,
        grad_shift_one,
        grad_bias_query,
        grad_bias_value,
        grad_bias_out,
        grad_gain_two,
        grad_shift_two,
        grad_bias_down,
        grad_bias_up,
    ]
    padding = jnp.zeros((VEC_ROWS * LANES - sum(VEC_LENGTHS),), F32)
    vector_grads = jnp.concatenate(vector_terms + [padding]).reshape(VEC_ROWS, LANES)
    vector_grads = sum_to(layout, last, vector_grads)
    used = 0
    sums_left = []
    for owner, rows in layout.leftover():
        part = leftover_terms[used : used + rows]
        sums_left.append(sum_to(layout, owner, part))
        used += rows
    leftover_sum = jnp.concatenate(sums_left)

    summed = jnp.concatenate([sum_first, sum_middle, sum_last])
    summed = summed.reshape(layout.columns, layout.piece, LANES)
    pieces = [
        lax.dynamic_index_in_dim(summed, column ^ key, keepdims=False)
        for key in range(layout.columns)
    ]
    pieces = pieces[:1] + [exchange(pieces[key], "dp", 2 * key) for key in range(1, layout.columns)]
    param_grads, new_params, new_first, new_second = finish(
        layout, place, pieces, leftover_sum, vector_grads, params, first_moment, second_moment
    )
    return (output[None], input_grad[None], param_grads, new_params, new_first, new_second)


def solution(mesh):
    placed = (
        P("dp", "ctx", None),
        P("dp"),
        P(None, ("dp", "ctx")),
        P(None, ("dp", "ctx")),
        P(None, ("dp", "ctx")),
        P("dp", "ctx", None),
    )
    dp, ctx = (mesh.shape["dp"], mesh.shape["ctx"])

    def program(inputs, counts, params, first_moment, second_moment, out_cotangent):
        layout = Layout(dp, ctx, params.shape[1] // (dp * ctx))

        def body(*arguments):
            return shards(layout, *arguments)

        return jax.shard_map(
            body,
            mesh=mesh,
            in_specs=placed,
            out_specs=(
                P("dp", "ctx", None),
                P("dp", "ctx", None),
                P(None, ("dp", "ctx")),
                P(None, ("dp", "ctx")),
                P(None, ("dp", "ctx")),
                P(None, ("dp", "ctx")),
            ),
            check_vma=False,
        )(inputs, counts, params, first_moment, second_moment, out_cotangent)

    return program
```

```python
import functools
import math

import jax
import jax.numpy as jnp
from jax import lax
from jax.experimental import pallas as pl
from jax.experimental.pallas import tpu as pltpu
from jax.sharding import PartitionSpec as P


D = 1152
HD = 72
FF = 4304
LANES = 128
TILE = 16

norm_epsilon = 1e-06
beta_one = 0.9
beta_two = 0.95
adam_epsilon = 1e-08
adam_step = 3
rate_matrix = 0.005
rate_vector = 0.1
weight_decay = 0.1
masked_score = -1e30

BF = jnp.bfloat16
F32 = jnp.float32

QKV_BLOCKS = 3 * D // LANES
D_BLOCKS = D // LANES
ROW_QKV = 0
ROW_OUT = D * QKV_BLOCKS
ROW_UP = ROW_OUT + D * D_BLOCKS
ROW_DOWN = ROW_UP + D * FF // LANES
ROW_VEC = ROW_DOWN + FF * D_BLOCKS
VEC_ROWS = 128
VEC_LENGTHS = [D] * 8 + [FF]

UP_GROUP = LANES // math.gcd(FF, LANES)
UP_STRIDE = UP_GROUP * FF // LANES
UP_BLOCKS = -(-FF // LANES)
UP_TAIL = FF - (UP_BLOCKS - 1) * LANES
STEPS = 9
BLOCK = D // STEPS
DOWN_BLOCK = -(-FF // (STEPS * TILE)) * TILE
VMEM_LIMIT = 60 * 1024 * 1024


class Layout:
    def __init__(self, dp, ctx, shard_length):
        self.dp, self.ctx = dp, ctx
        self.devices = dp * ctx
        self.columns = dp // 2
        self.rows = shard_length // LANES
        longest = (self.rows + TILE - 1) // TILE
        self.piece = -(-longest // self.columns) * TILE
        self.group_shards = 2 * ctx
        self.first = ROW_OUT // (self.group_shards * self.rows)
        self.last_piece = self.rows // TILE * TILE - (self.columns - 1) * self.piece
        assert self.first > 0 and self.last_piece > 0

    def start(self, shard):
        return shard * self.rows // TILE * TILE

    def group_start(self, group):
        return self.start(group * self.group_shards)

    def group_end(self, group):
        return self.start(group * self.group_shards - 1) + self.columns * self.piece

    def leftover(self):
        shard = self.first * self.group_shards
        found = []
        while self.start(shard) < ROW_OUT:
            found.append((shard, min(ROW_OUT, self.start(shard + 1)) - self.start(shard)))
            shard += 1
        return found


def lane_index(rows):
    return lax.broadcasted_iota(jnp.int32, (rows, LANES), 1)


def rows_to_matrix(flat, base, rows, blocks, wide, out):
    wide[pl.ds(0, rows * blocks), :] = flat[pl.ds(base, rows * blocks), :].astype(F32)
    for block in range(blocks):
        part = wide[pl.ds(block, rows, stride=blocks), :]
        out[:, block * LANES : (block + 1) * LANES] = part.astype(BF)


def matrix_to_rows(matrix, rows, blocks, wide, flat, base):
    for block in range(blocks):
        part = matrix[:, block * LANES : (block + 1) * LANES].astype(F32)
        wide[pl.ds(block, rows, stride=blocks), :] = part
    flat[pl.ds(base, rows * blocks), :] = wide[pl.ds(0, rows * blocks), :].astype(BF)


def rows_to_up(flat, base, wide, square, out):
    groups = BLOCK // UP_GROUP
    length = groups * UP_STRIDE
    wide[pl.ds(0, length), :] = flat[pl.ds(base, length), :].astype(F32)
    lanes = lane_index(groups)
    for row in range(UP_GROUP):
        first, shift = divmod(row * FF, LANES)
        held = None
        for block in range(UP_BLOCKS + 1):
            if block == UP_BLOCKS and shift + UP_TAIL <= LANES:
                piece = held
            else:
                piece = wide[pl.ds(first + block, groups, stride=UP_STRIDE), :]
                if shift:
                    piece = pltpu.roll(piece, LANES - shift, 1)
            if block:
                value = jnp.where(lanes < LANES - shift, held, piece) if shift else held
                square[block - 1, pl.ds(row, groups, stride=UP_GROUP), :] = value
            held = piece
    for block in range(UP_BLOCKS):
        first, last = (block * LANES, min(FF, (block + 1) * LANES))
        out[:, first:last] = square[block, :, : last - first].astype(BF)


def up_to_rows(matrix, square, wide, flat, base):
    groups = BLOCK // UP_GROUP
    length = groups * UP_STRIDE
    for block in range(UP_BLOCKS):
        first, last = (block * LANES, min(FF, (block + 1) * LANES))
        square[block, :, : last - first] = matrix[:, first:last].astype(F32)
    lanes = lane_index(groups)
    held = None
    for row in range(UP_GROUP):
        first, shift = divmod(row * FF, LANES)
        for block in range(UP_BLOCKS):
            piece = square[block, pl.ds(row, groups, stride=UP_GROUP), :]
            if shift:
                piece = pltpu.roll(piece, shift, 1)
                value = jnp.where(lanes < shift, held, piece)
            else:
                value = piece
            if block == UP_BLOCKS - 1 and shift + UP_TAIL < LANES:
                held = value
            else:
                wide[pl.ds(first + block, groups, stride=UP_STRIDE), :] = value
                held = piece
    flat[pl.ds(base, length), :] = wide[pl.ds(0, length), :].astype(BF)


def fetch(layout, place, groups, origin, sources, flat, sem):
    low, high = groups
    for ref, (column, core, key) in sources:
        device_column = jnp.bitwise_xor(place[0], column)
        device_core = jnp.bitwise_xor(place[1], core)
        row = jnp.bitwise_xor(place[2], key)

        def body(index, _, ref=ref, device_column=device_column, device_core=device_core, row=row):
            shard = (low + index) * layout.group_shards + device_core * layout.ctx + row
            start = shard * layout.rows // TILE * TILE
            target = pl.multiple_of(start + device_column * layout.piece - origin, TILE)
            source = pl.multiple_of(index * layout.piece, TILE)

            def copy(offset, rows):
                pltpu.make_async_copy(
                    ref.at[pl.ds(source + offset, rows), :],
                    flat.at[pl.ds(target + offset, rows), :],
                    sem,
                ).start()

            is_last = device_column == layout.columns - 1
            longer = shard * layout.rows % TILE + layout.rows % TILE >= TILE

            @pl.when(jnp.logical_not(is_last))
            def _():
                copy(0, layout.piece)

            @pl.when(is_last)
            def _():
                copy(0, layout.last_piece)

            @pl.when(jnp.logical_and(is_last, longer))
            def _():
                copy(layout.last_piece, TILE)

            return 0

        lax.fori_loop(0, high - low, body, 0)


def flat_of(gathered):
    return [array for array, _ in gathered]


def first_weights(layout, place, gathered, leftover):
    inside = layout.group_start(layout.first)
    length = inside + leftover.shape[0]
    assert length == ROW_OUT
    arrays = flat_of(gathered)

    def kernel(place_ref, *refs):
        sources, (extra, qkv, flat, wide, sem) = (refs[: len(arrays)], refs[len(arrays) :])
        step = pl.program_id(0)

        @pl.when(step == 0)
        def _():
            named = [(ref, entry) for ref, (_, entry) in zip(sources, gathered)]
            fetch(layout, place_ref, (0, layout.first), 0, named, flat, sem)
            pltpu.make_async_copy(
                extra, flat.at[pl.ds(inside, leftover.shape[0]), :], sem
            ).start()
            pltpu.make_async_copy(flat, flat, sem).wait()

        base = pl.multiple_of(step * (BLOCK * QKV_BLOCKS), TILE)
        rows_to_matrix(flat, base, BLOCK, QKV_BLOCKS, wide, qkv)

    return pl.pallas_call(
        kernel,
        name="first_weights",
        grid=(STEPS,),
        in_specs=[pl.BlockSpec(memory_space=pltpu.SMEM)]
        + [pl.BlockSpec(memory_space=pl.ANY)] * (len(arrays) + 1),
        out_specs=pl.BlockSpec((BLOCK, 3 * D), lambda i: (i, 0)),
        out_shape=jax.ShapeDtypeStruct((D, 3 * D), BF),
        scratch_shapes=[
            pltpu.VMEM((length, LANES), BF),
            pltpu.VMEM((BLOCK * QKV_BLOCKS, LANES), F32),
            pltpu.SemaphoreType.DMA,
        ],
        compiler_params=pltpu.CompilerParams(vmem_limit_bytes=VMEM_LIMIT),
    )(place, *arrays, leftover)


def other_weights(layout, place, gathered):
    origin = layout.group_start(layout.first)
    length = layout.start(layout.devices) - origin
    padded = max(length, ROW_DOWN - origin + STEPS * DOWN_BLOCK * D_BLOCKS)
    up_length = BLOCK // UP_GROUP * UP_STRIDE
    arrays = flat_of(gathered)

    def kernel(place_ref, *refs):
        sources = refs[: len(arrays)]
        out_w, up_w, down_w, flat, wide, square, sem = refs[len(arrays) :]
        step = pl.program_id(0)

        @pl.when(step == 0)
        def _():
            named = [(ref, entry) for ref, (_, entry) in zip(sources, gathered)]
            fetch(layout, place_ref, (layout.first, layout.columns), origin, named, flat, sem)
            whole = flat.at[pl.ds(0, length), :]
            pltpu.make_async_copy(whole, whole, sem).wait()

        base = pl.multiple_of(ROW_OUT - origin + step * (BLOCK * D_BLOCKS), TILE)
        rows_to_matrix(flat, base, BLOCK, D_BLOCKS, wide, out_w)
        base = pl.multiple_of(ROW_UP - origin + step * up_length, TILE)
        rows_to_up(flat, base, wide, square, up_w)
        base = pl.multiple_of(ROW_DOWN - origin + step * (DOWN_BLOCK * D_BLOCKS), TILE)
        rows_to_matrix(flat, base, DOWN_BLOCK, D_BLOCKS, wide, down_w)

    return pl.pallas_call(
        kernel,
        name="other_weights",
        grid=(STEPS,),
        in_specs=[pl.BlockSpec(memory_space=pltpu.SMEM)]
        + [pl.BlockSpec(memory_space=pl.ANY)] * len(arrays),
        out_specs=[
            pl.BlockSpec((BLOCK, D), lambda i: (i, 0)),
            pl.BlockSpec((BLOCK, FF), lambda i: (i, 0)),
            pl.BlockSpec((DOWN_BLOCK, D), lambda i: (i, 0)),
        ],
        out_shape=[
            jax.ShapeDtypeStruct((D, D), BF),
            jax.ShapeDtypeStruct((D, FF), BF),
            jax.ShapeDtypeStruct((FF, D), BF),
        ],
        scratch_shapes=[
            pltpu.VMEM((padded, LANES), BF),
            pltpu.VMEM((max(up_length + 8, DOWN_BLOCK * D_BLOCKS), LANES), F32),
            pltpu.VMEM((UP_BLOCKS, BLOCK, LANES), F32),
            pltpu.SemaphoreType.DMA,
        ],
        compiler_params=pltpu.CompilerParams(vmem_limit_bytes=VMEM_LIMIT),
    )(place, *arrays)


MATRICES = {
    "qkv": (ROW_QKV, BLOCK, BLOCK * QKV_BLOCKS, 3 * D),
    "out": (ROW_OUT, BLOCK, BLOCK * D_BLOCKS, D),
    "up": (ROW_UP, BLOCK, BLOCK // UP_GROUP * UP_STRIDE, FF),
    "down": (ROW_DOWN, DOWN_BLOCK, DOWN_BLOCK * D_BLOCKS, D),
}


def gradient_pieces(layout, place, groups, matrices, leftover=False):
    low, high = layout.group_start(groups[0]), layout.group_end(groups[1])
    count = groups[1] - groups[0]
    names = list(matrices)
    plan = {}
    for name in names:
        first, _, stride, _ = MATRICES[name]
        blocks = [
            block
            for block in range(STEPS)
            if leftover
            or (first + block * stride < high and first + (block + 1) * stride > low)
        ]
        plan[name] = (first, blocks[0], len(blocks), stride)
    origin = min([low] + [first + b * stride for first, b, _, stride in plan.values()])
    end = max([high] + [first + (b + n) * stride for first, b, n, stride in plan.values()])
    steps = max(n for _, _, n, _ in plan.values())
    covered = min(first + b * stride for first, b, _, stride in plan.values())
    rows = layout.devices // 2 * count * layout.piece
    extra = ROW_OUT - layout.group_start(layout.first)

    def kernel(place_ref, *refs):
        inputs, refs = (refs[: len(names)], refs[len(names) :])
        outputs, (flat, wide, square, sem) = (refs[:-4], refs[-4:])
        step = pl.program_id(0)
        if covered > low:

            @pl.when(step == 0)
            def _():
                flat[pl.ds(low - origin, covered - low), :] = jnp.zeros((covered - low, LANES), BF)

        for ref, name in zip(inputs, names):
            first, block, number, stride = plan[name]

            def convert(ref=ref, name=name, first=first, block=block, stride=stride):
                base = pl.multiple_of(first - origin + (block + step) * stride, TILE)
                if name == "up":
                    up_to_rows(ref, square, wide, flat, base)
                else:
                    blocks = QKV_BLOCKS if name == "qkv" else D_BLOCKS
                    matrix_to_rows(ref, stride // blocks, blocks, wide, flat, base)

            if number == steps:
                convert()
            else:
                pl.when(step < number)(convert)

        @pl.when(step == steps - 1)
        def _():
            if "down" in names:
                tail = end - ROW_VEC
                flat[pl.ds(ROW_VEC - origin, tail), :] = jnp.zeros((tail, LANES), BF)

            def body(index, _):
                group = groups[0] + index % count
                key = index // count
                row = jnp.bitwise_xor(place_ref[2], key % layout.ctx)
                column = jnp.bitwise_xor(place_ref[0], key // layout.ctx)
                for bit in range(2):
                    core = jnp.bitwise_xor(place_ref[1], bit)
                    shard = group * layout.group_shards + core * layout.ctx + row
                    start = shard * layout.rows // TILE * TILE
                    source = pl.multiple_of(start + column * layout.piece - origin, TILE)
                    target = pl.multiple_of(index * layout.piece, TILE)
                    pltpu.make_async_copy(
                        flat.at[pl.ds(source, layout.piece), :],
                        outputs[bit].at[pl.ds(target, layout.piece), :],
                        sem,
                    ).start()
                return 0

            lax.fori_loop(0, layout.devices // 2 * count, body, 0)
            pltpu.make_async_copy(outputs[0], outputs[0], sem).wait()
            pltpu.make_async_copy(outputs[1], outputs[1], sem).wait()
            if leftover:
                copy = pltpu.make_async_copy(
                    flat.at[pl.ds(ROW_OUT - extra - origin, extra), :], outputs[2], sem
                )
                copy.start()
                copy.wait()

    def spec(name):
        _, block, number, _ = plan[name]
        _, height, _, width = MATRICES[name]
        return pl.BlockSpec(
            (height, width), lambda i: (block + jnp.minimum(i, number - 1), 0)
        )

    shapes = [jax.ShapeDtypeStruct((rows, LANES), BF)] * 2
    if leftover:
        shapes.append(jax.ShapeDtypeStruct((extra, LANES), BF))
    wide_rows = max(stride for _, _, _, stride in plan.values())
    return pl.pallas_call(
        kernel,
        grid=(steps,),
        in_specs=[pl.BlockSpec(memory_space=pltpu.SMEM)] + [spec(name) for name in names],
        out_specs=[pl.BlockSpec(memory_space=pl.ANY)] * len(shapes),
        out_shape=shapes,
        scratch_shapes=[
            pltpu.VMEM((end - origin, LANES), BF),
            pltpu.VMEM((wide_rows, LANES), F32),
            pltpu.VMEM((UP_BLOCKS if "up" in names else 1, BLOCK, LANES), F32),
            pltpu.SemaphoreType.DMA,
        ],
        compiler_params=pltpu.CompilerParams(vmem_limit_bytes=VMEM_LIMIT),
    )(place, *[matrices[name] for name in names])


def dot_t(left, right):
    return lax.dot_general(left, right, (((1,), (1,)), ((), ())), preferred_element_type=F32)


def t_dot(left, right):
    return lax.dot_general(left, right, (((0,), (0,)), ((), ())), preferred_element_type=F32)


def dense(left, right):
    return jnp.dot(left, right, preferred_element_type=F32)


def masked(scores, count):
    columns = lax.broadcasted_iota(jnp.int32, scores.shape, 1)
    return jnp.where(columns < count, scores, masked_score)


def unpack_heads(place, blocks, parts, heads, held):
    for key, block in enumerate(blocks):
        rows = block.shape[0]
        row = pl.multiple_of(jnp.bitwise_xor(place[2], key) * rows, TILE)
        for part in range(parts):
            for head in range(heads):
                first = (part * heads + head) * HD
                held[part, head, pl.ds(row, rows), :] = block[:, first : first + HD]


def pack_heads(place, held, parts, heads, blocks):
    for key, block in enumerate(blocks):
        rows = block.shape[0]
        row = pl.multiple_of(jnp.bitwise_xor(place[2], key) * rows, TILE)
        block[...] = jnp.concatenate(
            [held[part, head, pl.ds(row, rows), :] for part in range(parts) for head in range(heads)],
            -1,
        )


def attend(counts, place, blocks, chunk):
    rows, width = blocks[0].shape
    heads, ctx = (width // (3 * HD), len(blocks))
    length = rows * ctx

    def kernel(count, place_ref, *refs):
        sources, mixed = (refs[:ctx], refs[ctx : 2 * ctx])
        log_total, held, made = refs[2 * ctx :]
        head = pl.program_id(0)

        @pl.when(head == 0)
        def _():
            unpack_heads(place_ref, sources, 3, heads, held)

        for first in range(0, length, chunk):
            queries = held[0, head, pl.ds(first, chunk), :]
            scores = masked(dot_t(queries, held[1, head]), count[0])
            top = jnp.max(scores, -1, keepdims=True)
            exponent = jnp.exp(scores - top)
            total = jnp.sum(exponent, -1, keepdims=True)
            probs = (exponent / total).astype(BF)
            made[0, head, pl.ds(first, chunk), :] = dense(probs, held[2, head]).astype(BF)
            log_total[0, first : first + chunk, :] = top + jnp.log(total)

        @pl.when(head == heads - 1)
        def _():
            pack_heads(place_ref, made, 1, heads, mixed)

    outputs = pl.pallas_call(
        kernel,
        name="attend",
        grid=(heads,),
        in_specs=[pl.BlockSpec(memory_space=pltpu.SMEM)] * 2
        + [pl.BlockSpec((rows, width), lambda h: (0, 0))] * ctx,
        out_specs=[pl.BlockSpec((rows, heads * HD), lambda h: (0, 0))] * ctx
        + [pl.BlockSpec((1, length, 1), lambda h: (h, 0, 0))],
        out_shape=[jax.ShapeDtypeStruct((rows, heads * HD), BF)] * ctx
        + [jax.ShapeDtypeStruct((heads, length, 1), F32)],
        scratch_shapes=[
            pltpu.VMEM((3, heads, length, HD), BF),
            pltpu.VMEM((1, heads, length, HD), BF),
        ],
        compiler_params=pltpu.CompilerParams(vmem_limit_bytes=VMEM_LIMIT),
    )(counts, place, *blocks)
    return outputs[:ctx], outputs[ctx]


def attend_back(counts, place, blocks, log_total, grad_blocks, chunk):
    rows, width = blocks[0].shape
    heads, ctx = (width // (3 * HD), len(blocks))
    length = rows * ctx
    scale = HD ** (-0.5)

    def kernel(count, place_ref, logs, *refs):
        sources, grads, made = (refs[:ctx], refs[ctx : 2 * ctx], refs[2 * ctx : 3 * ctx])
        sums, held, grad, results, acc_k, acc_v = refs[3 * ctx :]
        head = pl.program_id(0)

        @pl.when(head == 0)
        def _():
            unpack_heads(place_ref, sources, 3, heads, held)
            unpack_heads(place_ref, grads, 1, heads, grad)

        acc_k[...] = jnp.zeros_like(acc_k)
        acc_v[...] = jnp.zeros_like(acc_v)
        total_q = jnp.zeros((1, HD), F32)
        for first in range(0, length, chunk):
            part = pl.ds(first, chunk)
            queries = held[0, head, part, :]
            scores = masked(dot_t(queries, held[1, head]), count[0])
            probs = jnp.exp(scores - logs[0, part, :])
            grad_heads = grad[0, head, part, :]
            grad_probs = dot_t(grad_heads, held[2, head])
            delta = jnp.sum(probs * grad_probs, -1, keepdims=True)
            grad_scores = (probs * (grad_probs - delta)).astype(BF)
            grad_query = dense(grad_scores, held[1, head]) * scale
            total_q = total_q + jnp.sum(grad_query, 0, keepdims=True)
            results[0, head, part, :] = grad_query.astype(BF)
            acc_k[...] += t_dot(grad_scores, queries)
            acc_v[...] += t_dot(probs.astype(BF), grad_heads)
        results[1, head] = acc_k[...].astype(BF)
        results[2, head] = acc_v[...].astype(BF)
        sums[0, 0:1, :] = total_q
        sums[0, 1:2, :] = jnp.sum(acc_v[...], 0, keepdims=True)

        @pl.when(head == heads - 1)
        def _():
            pack_heads(place_ref, results, 3, heads, made)

    wide = pl.BlockSpec((rows, width), lambda h: (0, 0))
    outputs = pl.pallas_call(
        kernel,
        name="attend_back",
        grid=(heads,),
        in_specs=[pl.BlockSpec(memory_space=pltpu.SMEM)] * 2
        + [pl.BlockSpec((1, length, 1), lambda h: (h, 0, 0))]
        + [wide] * ctx
        + [pl.BlockSpec((rows, heads * HD), lambda h: (0, 0))] * ctx,
        out_specs=[wide] * ctx + [pl.BlockSpec((1, 2, HD), lambda h: (h, 0, 0))],
        out_shape=[jax.ShapeDtypeStruct((rows, width), BF)] * ctx
        + [jax.ShapeDtypeStruct((heads, 2, HD), F32)],
        scratch_shapes=[
            pltpu.VMEM((3, heads, length, HD), BF),
            pltpu.VMEM((1, heads, length, HD), BF),
            pltpu.VMEM((3, heads, length, HD), BF),
            pltpu.VMEM((length, HD), F32),
            pltpu.VMEM((length, HD), F32),
        ],
        compiler_params=pltpu.CompilerParams(vmem_limit_bytes=VMEM_LIMIT),
    )(counts, place, log_total, *blocks, *grad_blocks)
    return outputs[:ctx], outputs[ctx]


def norm_forward(residual):
    centre = residual - jnp.mean(residual, -1, keepdims=True)
    inverse = lax.rsqrt(jnp.mean(centre * centre, -1, keepdims=True) + norm_epsilon)
    return (centre * inverse, inverse)


def norm_back(grad_normed, unit, inverse, gain):
    scaled = grad_normed * gain
    return inverse * (
        scaled
        - jnp.mean(scaled, -1, keepdims=True)
        - unit * jnp.mean(scaled * unit, -1, keepdims=True)
    )


def adam_update(master, grads, first, second, matrix_part):
    first_new = beta_one * first + (1.0 - beta_one) * grads
    second_new = beta_two * second + (1.0 - beta_two) * grads * grads
    first_hat = first_new / (1.0 - beta_one**adam_step)
    second_hat = second_new / (1.0 - beta_two**adam_step)
    rate = jnp.where(matrix_part, rate_matrix, rate_vector)
    decay = jnp.where(matrix_part, weight_decay, 0.0)
    updated = master - rate * (first_hat / (jnp.sqrt(second_hat) + adam_epsilon) + decay * master)
    return (updated, first_new, second_new)


def exchange(array, axis, bit):
    size = lax.axis_size(axis)
    return lax.ppermute(array, axis, [(index, index ^ bit) for index in range(size)])


def pick(index, choices):
    picked = choices[0]
    for position, choice in enumerate(choices[1:], 1):
        picked = jnp.where(index == position, choice, picked)
    return picked


def to_heads(array, parts):
    ctx = lax.axis_size("ctx")
    rows = array.shape[0]
    split = array.reshape(rows, parts, ctx, D // ctx).transpose(2, 0, 1, 3)
    split = split.reshape(ctx, rows, parts * D // ctx)
    place = lax.axis_index("ctx")
    blocks = [
        lax.dynamic_index_in_dim(split, place ^ key, keepdims=False) for key in range(ctx)
    ]
    return blocks[:1] + [exchange(blocks[key], "ctx", key) for key in range(1, ctx)]


def from_heads(blocks, parts):
    ctx = len(blocks)
    held = list(blocks[:1]) + [exchange(blocks[key], "ctx", key) for key in range(1, ctx)]
    place = lax.axis_index("ctx")
    ordered = [
        pick(place, [held[index ^ position] for position in range(ctx)]) for index in range(ctx)
    ]
    share = D // ctx
    return jnp.concatenate(
        [block[:, part * share : (part + 1) * share] for part in range(parts) for block in ordered],
        -1,
    )


def add(*arrays):
    return functools.reduce(jnp.add, [array.astype(F32) for array in arrays]).astype(BF)


def gather(layout, share, behind=None):
    held = {0: share}
    bit = layout.ctx // 2
    while bit:
        held.update({key ^ bit: exchange(held[key], "ctx", bit) for key in list(held)})
        bit //= 2
    arrays = []
    for key in range(layout.ctx):
        own = held[key]
        if behind is not None:
            own = lax.optimization_barrier((own, behind))[0]
        found = [(own, (0, 0, key))]
        if layout.columns == 4:
            by_x = exchange(own, "dp", 2)
            by_y = exchange(own, "dp", 4)
            if key % 2:
                across = exchange(by_y, "dp", 2)
            else:
                across = exchange(by_x, "dp", 4)
            found += [(by_x, (1, 0, key)), (by_y, (2, 0, key)), (across, (3, 0, key))]
        else:
            bit = 1
            while bit < layout.columns:
                found += [
                    (exchange(array, "dp", 2 * bit), (place[0] ^ bit, 0, key))
                    for array, place in found
                ]
                bit *= 2
        arrays += found
    last = arrays[-2][0]
    arrays += [(exchange(array, "dp", 1), (place[0], 1, place[2])) for array, place in arrays]
    return arrays, held[layout.ctx - 1], last


def scatter(layout, kept, sent):
    received = exchange(sent, "dp", 1)
    half = kept.shape[0] // layout.columns // 2
    parts = lax.optimization_barrier(
        [
            add(kept[index * half : (index + 1) * half], received[index * half : (index + 1) * half])
            for index in range(2 * layout.columns)
        ]
    )
    if layout.columns == 4:
        low = add(parts[2], exchange(parts[6], "dp", 4))
        high = add(parts[5], exchange(parts[7], "dp", 2))
        over_x = exchange(parts[3], "dp", 2)
        over_y = exchange(parts[4], "dp", 4)
        low, high = (exchange(low, "dp", 2), exchange(high, "dp", 4))
        summed = [add(parts[0], low, over_y), add(parts[1], over_x, high)]
    else:
        bit = layout.columns
        while bit > 1:
            parts = [
                add(parts[index], exchange(parts[index ^ bit], "dp", bit))
                for index in range(bit)
            ]
            bit //= 2
        summed = parts
    each = layout.ctx // 2
    length = half // each
    held = {
        key: summed[key // each][(key % each) * length : (key % each + 1) * length]
        for key in range(layout.ctx)
    }
    bit = 1
    while bit < layout.ctx:
        for key in [key for key in held if key & bit]:
            moved = exchange(held.pop(key), "ctx", bit)
            held[key ^ bit] = add(held[key ^ bit], moved)
        bit *= 2
    return held[0]


def bits(layout):
    found = []
    for unit, size in ((1, layout.ctx), (2 * layout.ctx, layout.columns), (layout.ctx, 2)):
        bit = 1
        while bit < size:
            found.append(bit * unit)
            bit *= 2
    return found


def everywhere(layout, array, bit):
    if bit < layout.ctx:
        return exchange(array, "ctx", bit)
    return exchange(array, "dp", bit // layout.ctx)


def broadcast(layout, shard, sources):
    held = jnp.concatenate([rows for _, rows in sources])
    owner = jnp.concatenate(
        [jnp.full((rows.shape[0], 1), source, jnp.int32) for source, rows in sources]
    )
    for bit in bits(layout):
        other = everywhere(layout, held, bit)
        held = jnp.where(((owner ^ shard) & bit) == 0, held, other)
    return held


def sum_all(layout, held):
    for bit in reversed(bits(layout)):
        held = add(held, everywhere(layout, held, bit))
    return held


SWEEP = 512


def align(layout, place, params, before):
    length = layout.columns * layout.piece
    steps = pl.cdiv(layout.rows, SWEEP)
    held = max(TILE + steps * SWEEP, TILE + length)
    vector_first = ROW_VEC - layout.start(layout.devices - 1)
    assert 0 <= vector_first and vector_first + VEC_ROWS <= length
    starts = max(rows for _, rows in layout.leftover())

    def kernel(place_ref, rows, previous, *refs):
        outputs, wide = (refs[:-1], refs[-1])
        step = pl.program_id(0)

        @pl.when(step == 0)
        def _():
            wide[0:TILE, :] = previous[...]

        base = pl.multiple_of(TILE + step * SWEEP, TILE)
        wide[pl.ds(base, SWEEP), :] = rows[...].reshape(SWEEP, LANES)

        @pl.when(step == steps - 1)
        def _():
            first = TILE - place_ref[3]
            for key in range(layout.columns):
                row = first + jnp.bitwise_xor(place_ref[0], key) * layout.piece
                outputs[key][...] = wide[pl.ds(row, layout.piece), :].astype(BF)
            outputs[-2][...] = wide[pl.ds(first, starts), :].astype(BF)
            outputs[-1][...] = wide[pl.ds(first + vector_first, VEC_ROWS), :].astype(BF)

    heights = [layout.piece] * layout.columns + [starts, VEC_ROWS]
    return pl.pallas_call(
        kernel,
        name="align",
        grid=(steps,),
        in_specs=[
            pl.BlockSpec(memory_space=pltpu.SMEM),
            pl.BlockSpec((1, SWEEP * LANES), lambda i: (0, i)),
            pl.BlockSpec((TILE, LANES), lambda i: (0, 0)),
        ],
        out_specs=[pl.BlockSpec((height, LANES), lambda i: (0, 0)) for height in heights],
        out_shape=[jax.ShapeDtypeStruct((height, LANES), BF) for height in heights],
        scratch_shapes=[pltpu.VMEM((held, LANES), F32)],
        compiler_params=pltpu.CompilerParams(vmem_limit_bytes=VMEM_LIMIT),
    )(place, params, before)


def finish(layout, place, pieces, small, params, first, second):
    length = layout.columns * layout.piece
    steps = pl.cdiv(layout.rows, SWEEP)
    held = max(length, TILE + steps * SWEEP)
    vector_first = ROW_VEC - layout.start(layout.devices - 1)
    columns = layout.columns
    extra = sum(rows for _, rows in layout.leftover())

    def kernel(place_ref, *refs):
        sums, refs = (refs[:columns], refs[columns:])
        rest, master, one, two, grads, new, new_one, new_two, wide = refs
        step = pl.program_id(0)
        shard = place_ref[4]

        @pl.when(step == 0)
        def _():
            for key in range(columns):
                row = jnp.bitwise_xor(place_ref[0], key) * layout.piece
                row = pl.multiple_of(row, TILE)
                wide[pl.ds(row, layout.piece), :] = sums[key][...].astype(F32)
            used = 0
            for owner, rows in layout.leftover():

                @pl.when(shard == owner)
                def _(used=used, rows=rows):
                    wide[pl.ds(0, rows), :] += rest[pl.ds(used, rows), :].astype(F32)

                used += rows

            @pl.when(shard == layout.devices - 1)
            def _():
                wide[pl.ds(vector_first, VEC_ROWS), :] += rest[pl.ds(extra, VEC_ROWS), :].astype(F32)

        grad = wide[pl.ds(place_ref[3] + step * SWEEP, SWEEP), :]
        row = lax.broadcasted_iota(jnp.int32, (SWEEP, LANES), 0)
        matrix_part = row < ROW_VEC - shard * layout.rows - step * SWEEP
        results = adam_update(
            master[...].reshape(SWEEP, LANES),
            grad,
            one[...].reshape(SWEEP, LANES),
            two[...].reshape(SWEEP, LANES),
            matrix_part,
        )
        for ref, result in zip((grads, new, new_one, new_two), (grad,) + results):
            ref[...] = result.reshape(1, SWEEP * LANES)

    flat = pl.BlockSpec((1, SWEEP * LANES), lambda i: (0, i))

    def whole(array):
        return pl.BlockSpec(array.shape, lambda i: (0, 0))

    return pl.pallas_call(
        kernel,
        name="finish",
        grid=(steps,),
        in_specs=[pl.BlockSpec(memory_space=pltpu.SMEM)]
        + [whole(piece) for piece in pieces]
        + [whole(small), flat, flat, flat],
        out_specs=[flat] * 4,
        out_shape=[jax.ShapeDtypeStruct(params.shape, F32)] * 4,
        scratch_shapes=[pltpu.VMEM((held, LANES), F32)],
        compiler_params=pltpu.CompilerParams(vmem_limit_bytes=VMEM_LIMIT),
    )(place, *pieces, small, params, first, second)


def shards(layout, inputs, counts, params, first_moment, second_moment, out_cotangent):
    local_rows = inputs.shape[1]
    shard = lax.axis_index(("dp", "ctx"))
    score_scale = HD ** (-0.5)
    chunk = 256

    column = lax.axis_index("dp") // 2
    offset = (shard * layout.rows) % TILE
    place = jnp.stack(
        [column, lax.axis_index("dp") % 2, lax.axis_index("ctx"), offset, shard]
    ).astype(jnp.int32)
    last = layout.devices - 1
    ending = params[0, -TILE * LANES :].reshape(TILE, LANES)
    before = lax.ppermute(ending, ("dp", "ctx"), [(index, index + 1) for index in range(last)])
    aligned = align(layout, place, params, before)
    shares = list(aligned[:1]) + [
        exchange(aligned[key], "dp", 2 * key) for key in range(1, layout.columns)
    ]
    groups = [
        pick(column, [shares[index ^ position] for position in range(layout.columns)])
        for index in range(layout.columns)
    ]
    gathered_first, along, behind = gather(layout, jnp.concatenate(groups[: layout.first]))
    shared_rest = jnp.concatenate(groups[layout.first :])
    shared_rest = lax.optimization_barrier((shared_rest, along))[0]
    gathered_rest, _, _ = gather(layout, shared_rest, behind)
    sources = [(owner, aligned[-2][:rows]) for owner, rows in layout.leftover()]
    spread = broadcast(layout, shard, sources + [(last, aligned[-1])])
    leftover, spread = (spread[:-VEC_ROWS], spread[-VEC_ROWS:])
    flat_vectors = spread.reshape(-1).astype(F32)
    vectors = []
    used = 0
    for length in VEC_LENGTHS:
        vectors.append(flat_vectors[used : used + length])
        used += length
    (
        gain_one,
        shift_one,
        bias_query,
        bias_value,
        bias_out,
        gain_two,
        shift_two,
        bias_down,
        bias_up,
    ) = vectors

    residual = inputs[0].astype(F32)
    unit_one, inverse_one = norm_forward(residual)
    normed_round = (unit_one * gain_one + shift_one).astype(BF)
    qkv_weight = first_weights(layout, place, gathered_first, leftover)
    projected = dense(normed_round, qkv_weight)
    queries = ((projected[:, :D] + bias_query) * score_scale).astype(BF)
    keys = projected[:, D : 2 * D].astype(BF)
    values = (projected[:, 2 * D :] + bias_value).astype(BF)
    packed = to_heads(jnp.concatenate([queries, keys, values], -1), 3)
    out_weight, up_weight, down_weight = other_weights(layout, place, gathered_rest)
    mixed_heads, log_total = attend(counts, place, packed, chunk)
    mixed = from_heads(mixed_heads, 1)
    middle = residual + dense(mixed, out_weight) + bias_out
    unit_two, inverse_two = norm_forward(middle)
    normed_two_round = (unit_two * gain_two + shift_two).astype(BF)
    pre_gelu = dense(normed_two_round, up_weight) + bias_up
    activated = jax.nn.gelu(pre_gelu, approximate=True).astype(BF)
    output = (middle + dense(activated, down_weight) + bias_down).astype(BF)

    positions = lax.axis_index("ctx") * local_rows + jnp.arange(local_rows, dtype=jnp.int32)
    row_valid = (positions < counts[0])[:, None].astype(F32)
    grad_next = out_cotangent[0] * row_valid
    grad_bias_down = jnp.sum(grad_next, 0)
    grad_round = grad_next.astype(BF)
    grad_down = t_dot(activated, grad_round).astype(BF)
    grad_act = dot_t(grad_round, down_weight)
    gelu_back = jax.vjp(functools.partial(jax.nn.gelu, approximate=True), pre_gelu)[1]
    grad_pre = gelu_back(grad_act)[0]
    grad_bias_up = jnp.sum(grad_pre, 0)
    grad_pre_round = grad_pre.astype(BF)
    grad_up = t_dot(normed_two_round, grad_pre_round).astype(BF)
    middle_group = layout.columns // 2
    terms = gradient_pieces(
        layout, place, (middle_group, layout.columns), {"up": grad_up, "down": grad_down}
    )
    grad_pre_round, terms = lax.optimization_barrier((grad_pre_round, terms))
    sum_last = scatter(layout, *terms)
    grad_normed_two = dot_t(grad_pre_round, up_weight)
    grad_gain_two = jnp.sum(grad_normed_two * unit_two, 0)
    grad_shift_two = jnp.sum(grad_normed_two, 0)
    grad_middle = grad_next + norm_back(grad_normed_two, unit_two, inverse_two, gain_two)
    grad_bias_out = jnp.sum(grad_middle, 0)
    middle_round = grad_middle.astype(BF)
    grad_out = t_dot(mixed, middle_round).astype(BF)
    grad_mixed = dot_t(middle_round, out_weight).astype(BF)
    grad_mixed_heads = to_heads(grad_mixed, 1)
    terms = gradient_pieces(
        layout, place, (layout.first, middle_group), {"out": grad_out, "up": grad_up}
    )
    sum_middle = scatter(layout, *terms)
    grad_packed, sums = attend_back(
        counts, place, packed, log_total, grad_mixed_heads, chunk
    )
    grad_projected = from_heads(grad_packed, 3)
    grad_qkv = t_dot(normed_round, grad_projected).astype(BF)
    *terms, leftover_terms = gradient_pieces(
        layout, place, (0, layout.first), {"qkv": grad_qkv}, leftover=True
    )
    grad_projected, leftover_terms, *terms = lax.optimization_barrier(
        (grad_projected, leftover_terms, *terms)
    )
    sum_first = scatter(layout, *terms)
    grad_normed_one = dot_t(grad_projected, qkv_weight)
    grad_gain_one = jnp.sum(grad_normed_one * unit_one, 0)
    grad_shift_one = jnp.sum(grad_normed_one, 0)
    input_grad = grad_middle + norm_back(grad_normed_one, unit_one, inverse_one, gain_one)

    share = D // layout.ctx
    where = (lax.axis_index("ctx") * share,)
    sum_q, sum_v = (sums[:, 0].reshape(-1), sums[:, 1].reshape(-1))
    grad_bias_query = lax.dynamic_update_slice(jnp.zeros((D,), F32), sum_q, where)
    grad_bias_value = lax.dynamic_update_slice(jnp.zeros((D,), F32), sum_v, where)
    vector_terms = [
        grad_gain_one,
        grad_shift_one,
        grad_bias_query,
        grad_bias_value,
        grad_bias_out,
        grad_gain_two,
        grad_shift_two,
        grad_bias_down,
        grad_bias_up,
    ]
    padding = jnp.zeros((VEC_ROWS * LANES - sum(VEC_LENGTHS),), F32)
    vector_grads = jnp.concatenate(vector_terms + [padding]).reshape(VEC_ROWS, LANES)
    small_terms = jnp.concatenate([leftover_terms, vector_grads.astype(BF)])
    small_sum = sum_all(layout, small_terms)

    summed = jnp.concatenate([sum_first, sum_middle, sum_last])
    summed = summed.reshape(layout.columns, layout.piece, LANES)
    pieces = [
        lax.dynamic_index_in_dim(summed, column ^ key, keepdims=False)
        for key in range(layout.columns)
    ]
    pieces = pieces[:1] + [exchange(pieces[key], "dp", 2 * key) for key in range(1, layout.columns)]
    param_grads, new_params, new_first, new_second = finish(
        layout, place, pieces, small_sum, params, first_moment, second_moment
    )
    return (output[None], input_grad[None], param_grads, new_params, new_first, new_second)


def solution(mesh):
    placed = (
        P("dp", "ctx", None),
        P("dp"),
        P(None, ("dp", "ctx")),
        P(None, ("dp", "ctx")),
        P(None, ("dp", "ctx")),
        P("dp", "ctx", None),
    )
    dp, ctx = (mesh.shape["dp"], mesh.shape["ctx"])

    def program(inputs, counts, params, first_moment, second_moment, out_cotangent):
        layout = Layout(dp, ctx, params.shape[1] // (dp * ctx))

        def body(*arguments):
            return shards(layout, *arguments)

        return jax.shard_map(
            body,
            mesh=mesh,
            in_specs=placed,
            out_specs=(
                P("dp", "ctx", None),
                P("dp", "ctx", None),
                P(None, ("dp", "ctx")),
                P(None, ("dp", "ctx")),
                P(None, ("dp", "ctx")),
                P(None, ("dp", "ctx")),
            ),
            check_vma=False,
        )(inputs, counts, params, first_moment, second_moment, out_cotangent)

    return program
```

```python
import functools
import math

import jax
import jax.numpy as jnp
from jax import lax
from jax.experimental import pallas as pl
from jax.experimental.pallas import tpu as pltpu
from jax.sharding import PartitionSpec as P


D = 1152
HD = 72
FF = 4304
LANES = 128
TILE = 16

norm_epsilon = 1e-06
beta_one = 0.9
beta_two = 0.95
adam_epsilon = 1e-08
adam_step = 3
rate_matrix = 0.005
rate_vector = 0.1
weight_decay = 0.1
masked_score = -1e30

BF = jnp.bfloat16
F32 = jnp.float32

QKV_BLOCKS = 3 * D // LANES
D_BLOCKS = D // LANES
ROW_QKV = 0
ROW_OUT = D * QKV_BLOCKS
ROW_UP = ROW_OUT + D * D_BLOCKS
ROW_DOWN = ROW_UP + D * FF // LANES
ROW_VEC = ROW_DOWN + FF * D_BLOCKS
VEC_ROWS = 128
VEC_LENGTHS = [D] * 8 + [FF]

UP_GROUP = LANES // math.gcd(FF, LANES)
UP_STRIDE = UP_GROUP * FF // LANES
UP_BLOCKS = -(-FF // LANES)
UP_TAIL = FF - (UP_BLOCKS - 1) * LANES
STEPS = 9
BLOCK = D // STEPS
DOWN_BLOCK = -(-FF // (STEPS * TILE)) * TILE
VMEM_LIMIT = 60 * 1024 * 1024


class Layout:
    def __init__(self, dp, ctx, shard_length):
        self.dp, self.ctx = dp, ctx
        self.devices = dp * ctx
        self.columns = dp // 2
        self.rows = shard_length // LANES
        longest = (self.rows + TILE - 1) // TILE
        self.piece = -(-longest // self.columns) * TILE
        self.group_shards = 2 * ctx
        self.first = ROW_OUT // (self.group_shards * self.rows)
        self.last_piece = self.rows // TILE * TILE - (self.columns - 1) * self.piece
        assert self.first > 0 and self.last_piece > 0

    def start(self, shard):
        return shard * self.rows // TILE * TILE

    def group_start(self, group):
        return self.start(group * self.group_shards)

    def group_end(self, group):
        return self.start(group * self.group_shards - 1) + self.columns * self.piece

    def leftover(self):
        shard = self.first * self.group_shards
        found = []
        while self.start(shard) < ROW_OUT:
            found.append((shard, min(ROW_OUT, self.start(shard + 1)) - self.start(shard)))
            shard += 1
        return found


def lane_index(rows):
    return lax.broadcasted_iota(jnp.int32, (rows, LANES), 1)


def rows_to_matrix(flat, base, rows, blocks, wide, out):
    wide[pl.ds(0, rows * blocks), :] = flat[pl.ds(base, rows * blocks), :].astype(F32)
    for block in range(blocks):
        part = wide[pl.ds(block, rows, stride=blocks), :]
        out[:, block * LANES : (block + 1) * LANES] = part.astype(BF)


def matrix_to_rows(matrix, rows, blocks, wide, flat, base):
    for block in range(blocks):
        part = matrix[:, block * LANES : (block + 1) * LANES].astype(F32)
        wide[pl.ds(block, rows, stride=blocks), :] = part
    flat[pl.ds(base, rows * blocks), :] = wide[pl.ds(0, rows * blocks), :].astype(BF)


def rows_to_up(flat, base, wide, square, out):
    groups = BLOCK // UP_GROUP
    length = groups * UP_STRIDE
    wide[pl.ds(0, length), :] = flat[pl.ds(base, length), :].astype(F32)
    lanes = lane_index(groups)
    for row in range(UP_GROUP):
        first, shift = divmod(row * FF, LANES)
        held = None
        for block in range(UP_BLOCKS + 1):
            if block == UP_BLOCKS and shift + UP_TAIL <= LANES:
                piece = held
            else:
                piece = wide[pl.ds(first + block, groups, stride=UP_STRIDE), :]
                if shift:
                    piece = pltpu.roll(piece, LANES - shift, 1)
            if block:
                value = jnp.where(lanes < LANES - shift, held, piece) if shift else held
                square[block - 1, pl.ds(row, groups, stride=UP_GROUP), :] = value
            held = piece
    for block in range(UP_BLOCKS):
        first, last = (block * LANES, min(FF, (block + 1) * LANES))
        out[:, first:last] = square[block, :, : last - first].astype(BF)


def up_to_rows(matrix, square, wide, flat, base):
    groups = BLOCK // UP_GROUP
    length = groups * UP_STRIDE
    for block in range(UP_BLOCKS):
        first, last = (block * LANES, min(FF, (block + 1) * LANES))
        square[block, :, : last - first] = matrix[:, first:last].astype(F32)
    lanes = lane_index(groups)
    held = None
    for row in range(UP_GROUP):
        first, shift = divmod(row * FF, LANES)
        for block in range(UP_BLOCKS):
            piece = square[block, pl.ds(row, groups, stride=UP_GROUP), :]
            if shift:
                piece = pltpu.roll(piece, shift, 1)
                value = jnp.where(lanes < shift, held, piece)
            else:
                value = piece
            if block == UP_BLOCKS - 1 and shift + UP_TAIL < LANES:
                held = value
            else:
                wide[pl.ds(first + block, groups, stride=UP_STRIDE), :] = value
                held = piece
    flat[pl.ds(base, length), :] = wide[pl.ds(0, length), :].astype(BF)


def fetch(layout, place, groups, origin, sources, flat, sem):
    low, high = groups
    for ref, (column, core, key) in sources:
        device_column = jnp.bitwise_xor(place[0], column)
        device_core = jnp.bitwise_xor(place[1], core)
        row = jnp.bitwise_xor(place[2], key)

        def body(index, _, ref=ref, device_column=device_column, device_core=device_core, row=row):
            shard = (low + index) * layout.group_shards + device_core * layout.ctx + row
            start = shard * layout.rows // TILE * TILE
            target = pl.multiple_of(start + device_column * layout.piece - origin, TILE)
            source = pl.multiple_of(index * layout.piece, TILE)

            def copy(offset, rows):
                pltpu.make_async_copy(
                    ref.at[pl.ds(source + offset, rows), :],
                    flat.at[pl.ds(target + offset, rows), :],
                    sem,
                ).start()

            is_last = device_column == layout.columns - 1
            longer = shard * layout.rows % TILE + layout.rows % TILE >= TILE

            @pl.when(jnp.logical_not(is_last))
            def _():
                copy(0, layout.piece)

            @pl.when(is_last)
            def _():
                copy(0, layout.last_piece)

            @pl.when(jnp.logical_and(is_last, longer))
            def _():
                copy(layout.last_piece, TILE)

            return 0

        lax.fori_loop(0, high - low, body, 0)


def flat_of(gathered):
    return [array for array, _ in gathered]


def first_weights(layout, place, gathered, leftover):
    inside = layout.group_start(layout.first)
    length = inside + leftover.shape[0]
    assert length == ROW_OUT
    arrays = flat_of(gathered)

    def kernel(place_ref, *refs):
        sources, (extra, qkv, flat, wide, sem) = (refs[: len(arrays)], refs[len(arrays) :])
        step = pl.program_id(0)

        @pl.when(step == 0)
        def _():
            named = [(ref, entry) for ref, (_, entry) in zip(sources, gathered)]
            fetch(layout, place_ref, (0, layout.first), 0, named, flat, sem)
            pltpu.make_async_copy(
                extra, flat.at[pl.ds(inside, leftover.shape[0]), :], sem
            ).start()
            pltpu.make_async_copy(flat, flat, sem).wait()

        base = pl.multiple_of(step * (BLOCK * QKV_BLOCKS), TILE)
        rows_to_matrix(flat, base, BLOCK, QKV_BLOCKS, wide, qkv)

    return pl.pallas_call(
        kernel,
        name="first_weights",
        grid=(STEPS,),
        in_specs=[pl.BlockSpec(memory_space=pltpu.SMEM)]
        + [pl.BlockSpec(memory_space=pl.ANY)] * (len(arrays) + 1),
        out_specs=pl.BlockSpec((BLOCK, 3 * D), lambda i: (i, 0)),
        out_shape=jax.ShapeDtypeStruct((D, 3 * D), BF),
        scratch_shapes=[
            pltpu.VMEM((length, LANES), BF),
            pltpu.VMEM((BLOCK * QKV_BLOCKS, LANES), F32),
            pltpu.SemaphoreType.DMA,
        ],
        compiler_params=pltpu.CompilerParams(vmem_limit_bytes=VMEM_LIMIT),
    )(place, *arrays, leftover)


def other_weights(layout, place, gathered):
    origin = layout.group_start(layout.first)
    length = layout.start(layout.devices) - origin
    padded = max(length, ROW_DOWN - origin + STEPS * DOWN_BLOCK * D_BLOCKS)
    up_length = BLOCK // UP_GROUP * UP_STRIDE
    arrays = flat_of(gathered)

    def kernel(place_ref, *refs):
        sources = refs[: len(arrays)]
        out_w, up_w, down_w, flat, wide, square, sem = refs[len(arrays) :]
        step = pl.program_id(0)

        @pl.when(step == 0)
        def _():
            named = [(ref, entry) for ref, (_, entry) in zip(sources, gathered)]
            fetch(layout, place_ref, (layout.first, layout.columns), origin, named, flat, sem)
            whole = flat.at[pl.ds(0, length), :]
            pltpu.make_async_copy(whole, whole, sem).wait()

        base = pl.multiple_of(ROW_OUT - origin + step * (BLOCK * D_BLOCKS), TILE)
        rows_to_matrix(flat, base, BLOCK, D_BLOCKS, wide, out_w)
        base = pl.multiple_of(ROW_UP - origin + step * up_length, TILE)
        rows_to_up(flat, base, wide, square, up_w)
        base = pl.multiple_of(ROW_DOWN - origin + step * (DOWN_BLOCK * D_BLOCKS), TILE)
        rows_to_matrix(flat, base, DOWN_BLOCK, D_BLOCKS, wide, down_w)

    return pl.pallas_call(
        kernel,
        name="other_weights",
        grid=(STEPS,),
        in_specs=[pl.BlockSpec(memory_space=pltpu.SMEM)]
        + [pl.BlockSpec(memory_space=pl.ANY)] * len(arrays),
        out_specs=[
            pl.BlockSpec((BLOCK, D), lambda i: (i, 0)),
            pl.BlockSpec((BLOCK, FF), lambda i: (i, 0)),
            pl.BlockSpec((DOWN_BLOCK, D), lambda i: (i, 0)),
        ],
        out_shape=[
            jax.ShapeDtypeStruct((D, D), BF),
            jax.ShapeDtypeStruct((D, FF), BF),
            jax.ShapeDtypeStruct((FF, D), BF),
        ],
        scratch_shapes=[
            pltpu.VMEM((padded, LANES), BF),
            pltpu.VMEM((max(up_length + 8, DOWN_BLOCK * D_BLOCKS), LANES), F32),
            pltpu.VMEM((UP_BLOCKS, BLOCK, LANES), F32),
            pltpu.SemaphoreType.DMA,
        ],
        compiler_params=pltpu.CompilerParams(vmem_limit_bytes=VMEM_LIMIT),
    )(place, *arrays)


MATRICES = {
    "qkv": (ROW_QKV, BLOCK, BLOCK * QKV_BLOCKS, 3 * D),
    "out": (ROW_OUT, BLOCK, BLOCK * D_BLOCKS, D),
    "up": (ROW_UP, BLOCK, BLOCK // UP_GROUP * UP_STRIDE, FF),
    "down": (ROW_DOWN, DOWN_BLOCK, DOWN_BLOCK * D_BLOCKS, D),
}


def gradient_pieces(layout, place, groups, matrices, leftover=False):
    low, high = layout.group_start(groups[0]), layout.group_end(groups[1])
    count = groups[1] - groups[0]
    names = list(matrices)
    plan = {}
    for name in names:
        first, _, stride, _ = MATRICES[name]
        blocks = [
            block
            for block in range(STEPS)
            if leftover
            or (first + block * stride < high and first + (block + 1) * stride > low)
        ]
        plan[name] = (first, blocks[0], len(blocks), stride)
    origin = min([low] + [first + b * stride for first, b, _, stride in plan.values()])
    end = max([high] + [first + (b + n) * stride for first, b, n, stride in plan.values()])
    steps = max(n for _, _, n, _ in plan.values())
    covered = min(first + b * stride for first, b, _, stride in plan.values())
    rows = layout.devices // 2 * count * layout.piece
    extra = ROW_OUT - layout.group_start(layout.first)

    def kernel(place_ref, *refs):
        inputs, refs = (refs[: len(names)], refs[len(names) :])
        outputs, (flat, wide, square, sem) = (refs[:-4], refs[-4:])
        step = pl.program_id(0)
        if covered > low:

            @pl.when(step == 0)
            def _():
                flat[pl.ds(low - origin, covered - low), :] = jnp.zeros((covered - low, LANES), BF)

        for ref, name in zip(inputs, names):
            first, block, number, stride = plan[name]

            def convert(ref=ref, name=name, first=first, block=block, stride=stride):
                base = pl.multiple_of(first - origin + (block + step) * stride, TILE)
                if name == "up":
                    up_to_rows(ref, square, wide, flat, base)
                else:
                    blocks = QKV_BLOCKS if name == "qkv" else D_BLOCKS
                    matrix_to_rows(ref, stride // blocks, blocks, wide, flat, base)

            if number == steps:
                convert()
            else:
                pl.when(step < number)(convert)

        @pl.when(step == steps - 1)
        def _():
            if "down" in names:
                tail = end - ROW_VEC
                flat[pl.ds(ROW_VEC - origin, tail), :] = jnp.zeros((tail, LANES), BF)

            def body(index, _):
                group = groups[0] + index % count
                key = index // count
                row = jnp.bitwise_xor(place_ref[2], key % layout.ctx)
                column = jnp.bitwise_xor(place_ref[0], key // layout.ctx)
                for bit in range(2):
                    core = jnp.bitwise_xor(place_ref[1], bit)
                    shard = group * layout.group_shards + core * layout.ctx + row
                    start = shard * layout.rows // TILE * TILE
                    source = pl.multiple_of(start + column * layout.piece - origin, TILE)
                    target = pl.multiple_of(index * layout.piece, TILE)
                    pltpu.make_async_copy(
                        flat.at[pl.ds(source, layout.piece), :],
                        outputs[bit].at[pl.ds(target, layout.piece), :],
                        sem,
                    ).start()
                return 0

            lax.fori_loop(0, layout.devices // 2 * count, body, 0)
            pltpu.make_async_copy(outputs[0], outputs[0], sem).wait()
            pltpu.make_async_copy(outputs[1], outputs[1], sem).wait()
            if leftover:
                copy = pltpu.make_async_copy(
                    flat.at[pl.ds(ROW_OUT - extra - origin, extra), :], outputs[2], sem
                )
                copy.start()
                copy.wait()

    def spec(name):
        _, block, number, _ = plan[name]
        _, height, _, width = MATRICES[name]
        return pl.BlockSpec(
            (height, width), lambda i: (block + jnp.minimum(i, number - 1), 0)
        )

    shapes = [jax.ShapeDtypeStruct((rows, LANES), BF)] * 2
    if leftover:
        shapes.append(jax.ShapeDtypeStruct((extra, LANES), BF))
    wide_rows = max(stride for _, _, _, stride in plan.values())
    return pl.pallas_call(
        kernel,
        grid=(steps,),
        in_specs=[pl.BlockSpec(memory_space=pltpu.SMEM)] + [spec(name) for name in names],
        out_specs=[pl.BlockSpec(memory_space=pl.ANY)] * len(shapes),
        out_shape=shapes,
        scratch_shapes=[
            pltpu.VMEM((end - origin, LANES), BF),
            pltpu.VMEM((wide_rows, LANES), F32),
            pltpu.VMEM((UP_BLOCKS if "up" in names else 1, BLOCK, LANES), F32),
            pltpu.SemaphoreType.DMA,
        ],
        compiler_params=pltpu.CompilerParams(vmem_limit_bytes=VMEM_LIMIT),
    )(place, *[matrices[name] for name in names])


def dot_t(left, right):
    return lax.dot_general(left, right, (((1,), (1,)), ((), ())), preferred_element_type=F32)


def t_dot(left, right):
    return lax.dot_general(left, right, (((0,), (0,)), ((), ())), preferred_element_type=F32)


def dense(left, right):
    return jnp.dot(left, right, preferred_element_type=F32)


def masked(scores, count):
    columns = lax.broadcasted_iota(jnp.int32, scores.shape, 1)
    return jnp.where(columns < count, scores, masked_score)


def unpack_heads(place, blocks, parts, heads, held):
    for key, block in enumerate(blocks):
        rows = block.shape[0]
        row = pl.multiple_of(jnp.bitwise_xor(place[2], key) * rows, TILE)
        for part in range(parts):
            for head in range(heads):
                first = (part * heads + head) * HD
                held[part, head, pl.ds(row, rows), :] = block[:, first : first + HD]


def pack_heads(place, held, parts, heads, blocks):
    for key, block in enumerate(blocks):
        rows = block.shape[0]
        row = pl.multiple_of(jnp.bitwise_xor(place[2], key) * rows, TILE)
        block[...] = jnp.concatenate(
            [held[part, head, pl.ds(row, rows), :] for part in range(parts) for head in range(heads)],
            -1,
        )


def attend(counts, place, blocks, chunk):
    rows, width = blocks[0].shape
    heads, ctx = (width // (3 * HD), len(blocks))
    length = rows * ctx

    def kernel(count, place_ref, *refs):
        sources, mixed = (refs[:ctx], refs[ctx : 2 * ctx])
        log_total, held, made = refs[2 * ctx :]
        head = pl.program_id(0)

        @pl.when(head == 0)
        def _():
            unpack_heads(place_ref, sources, 3, heads, held)

        for first in range(0, length, chunk):
            queries = held[0, head, pl.ds(first, chunk), :]
            scores = masked(dot_t(queries, held[1, head]), count[0])
            top = jnp.max(scores, -1, keepdims=True)
            exponent = jnp.exp(scores - top)
            total = jnp.sum(exponent, -1, keepdims=True)
            probs = (exponent / total).astype(BF)
            made[0, head, pl.ds(first, chunk), :] = dense(probs, held[2, head]).astype(BF)
            log_total[0, first : first + chunk, :] = top + jnp.log(total)

        @pl.when(head == heads - 1)
        def _():
            pack_heads(place_ref, made, 1, heads, mixed)

    outputs = pl.pallas_call(
        kernel,
        name="attend",
        grid=(heads,),
        in_specs=[pl.BlockSpec(memory_space=pltpu.SMEM)] * 2
        + [pl.BlockSpec((rows, width), lambda h: (0, 0))] * ctx,
        out_specs=[pl.BlockSpec((rows, heads * HD), lambda h: (0, 0))] * ctx
        + [pl.BlockSpec((1, length, 1), lambda h: (h, 0, 0))],
        out_shape=[jax.ShapeDtypeStruct((rows, heads * HD), BF)] * ctx
        + [jax.ShapeDtypeStruct((heads, length, 1), F32)],
        scratch_shapes=[
            pltpu.VMEM((3, heads, length, HD), BF),
            pltpu.VMEM((1, heads, length, HD), BF),
        ],
        compiler_params=pltpu.CompilerParams(vmem_limit_bytes=VMEM_LIMIT),
    )(counts, place, *blocks)
    return outputs[:ctx], outputs[ctx]


def attend_back(counts, place, blocks, log_total, grad_blocks, chunk):
    rows, width = blocks[0].shape
    heads, ctx = (width // (3 * HD), len(blocks))
    length = rows * ctx
    scale = HD ** (-0.5)

    def kernel(count, place_ref, logs, *refs):
        sources, grads, made = (refs[:ctx], refs[ctx : 2 * ctx], refs[2 * ctx : 3 * ctx])
        sums, held, grad, results, acc_k, acc_v = refs[3 * ctx :]
        head = pl.program_id(0)

        @pl.when(head == 0)
        def _():
            unpack_heads(place_ref, sources, 3, heads, held)
            unpack_heads(place_ref, grads, 1, heads, grad)

        acc_k[...] = jnp.zeros_like(acc_k)
        acc_v[...] = jnp.zeros_like(acc_v)
        total_q = jnp.zeros((1, HD), F32)
        for first in range(0, length, chunk):
            part = pl.ds(first, chunk)
            queries = held[0, head, part, :]
            scores = masked(dot_t(queries, held[1, head]), count[0])
            probs = jnp.exp(scores - logs[0, part, :])
            grad_heads = grad[0, head, part, :]
            grad_probs = dot_t(grad_heads, held[2, head])
            delta = jnp.sum(probs * grad_probs, -1, keepdims=True)
            grad_scores = (probs * (grad_probs - delta)).astype(BF)
            grad_query = dense(grad_scores, held[1, head]) * scale
            total_q = total_q + jnp.sum(grad_query, 0, keepdims=True)
            results[0, head, part, :] = grad_query.astype(BF)
            acc_k[...] += t_dot(grad_scores, queries)
            acc_v[...] += t_dot(probs.astype(BF), grad_heads)
        results[1, head] = acc_k[...].astype(BF)
        results[2, head] = acc_v[...].astype(BF)
        sums[0, 0:1, :] = total_q
        sums[0, 1:2, :] = jnp.sum(acc_v[...], 0, keepdims=True)

        @pl.when(head == heads - 1)
        def _():
            pack_heads(place_ref, results, 3, heads, made)

    wide = pl.BlockSpec((rows, width), lambda h: (0, 0))
    outputs = pl.pallas_call(
        kernel,
        name="attend_back",
        grid=(heads,),
        in_specs=[pl.BlockSpec(memory_space=pltpu.SMEM)] * 2
        + [pl.BlockSpec((1, length, 1), lambda h: (h, 0, 0))]
        + [wide] * ctx
        + [pl.BlockSpec((rows, heads * HD), lambda h: (0, 0))] * ctx,
        out_specs=[wide] * ctx + [pl.BlockSpec((1, 2, HD), lambda h: (h, 0, 0))],
        out_shape=[jax.ShapeDtypeStruct((rows, width), BF)] * ctx
        + [jax.ShapeDtypeStruct((heads, 2, HD), F32)],
        scratch_shapes=[
            pltpu.VMEM((3, heads, length, HD), BF),
            pltpu.VMEM((1, heads, length, HD), BF),
            pltpu.VMEM((3, heads, length, HD), BF),
            pltpu.VMEM((length, HD), F32),
            pltpu.VMEM((length, HD), F32),
        ],
        compiler_params=pltpu.CompilerParams(vmem_limit_bytes=VMEM_LIMIT),
    )(counts, place, log_total, *blocks, *grad_blocks)
    return outputs[:ctx], outputs[ctx]


def norm_forward(residual):
    centre = residual - jnp.mean(residual, -1, keepdims=True)
    inverse = lax.rsqrt(jnp.mean(centre * centre, -1, keepdims=True) + norm_epsilon)
    return (centre * inverse, inverse)


def norm_back(grad_normed, unit, inverse, gain):
    scaled = grad_normed * gain
    return inverse * (
        scaled
        - jnp.mean(scaled, -1, keepdims=True)
        - unit * jnp.mean(scaled * unit, -1, keepdims=True)
    )


def adam_update(master, grads, first, second, matrix_part):
    first_new = beta_one * first + (1.0 - beta_one) * grads
    second_new = beta_two * second + (1.0 - beta_two) * grads * grads
    first_hat = first_new / (1.0 - beta_one**adam_step)
    second_hat = second_new / (1.0 - beta_two**adam_step)
    rate = jnp.where(matrix_part, rate_matrix, rate_vector)
    decay = jnp.where(matrix_part, weight_decay, 0.0)
    updated = master - rate * (first_hat / (jnp.sqrt(second_hat) + adam_epsilon) + decay * master)
    return (updated, first_new, second_new)


def exchange(array, axis, bit):
    size = lax.axis_size(axis)
    return lax.ppermute(array, axis, [(index, index ^ bit) for index in range(size)])


def pick(index, choices):
    picked = choices[0]
    for position, choice in enumerate(choices[1:], 1):
        picked = jnp.where(index == position, choice, picked)
    return picked


def to_heads(array, parts):
    ctx = lax.axis_size("ctx")
    rows = array.shape[0]
    split = array.reshape(rows, parts, ctx, D // ctx).transpose(2, 0, 1, 3)
    split = split.reshape(ctx, rows, parts * D // ctx)
    place = lax.axis_index("ctx")
    blocks = [
        lax.dynamic_index_in_dim(split, place ^ key, keepdims=False) for key in range(ctx)
    ]
    return blocks[:1] + [exchange(blocks[key], "ctx", key) for key in range(1, ctx)]


def from_heads(blocks, parts):
    ctx = len(blocks)
    held = list(blocks[:1]) + [exchange(blocks[key], "ctx", key) for key in range(1, ctx)]
    place = lax.axis_index("ctx")
    ordered = [
        pick(place, [held[index ^ position] for position in range(ctx)]) for index in range(ctx)
    ]
    share = D // ctx
    return jnp.concatenate(
        [block[:, part * share : (part + 1) * share] for part in range(parts) for block in ordered],
        -1,
    )


def add(*arrays):
    return functools.reduce(jnp.add, [array.astype(F32) for array in arrays]).astype(BF)


def gather(layout, share, behind=None):
    held = {0: share}
    bit = layout.ctx // 2
    while bit:
        held.update({key ^ bit: exchange(held[key], "ctx", bit) for key in list(held)})
        bit //= 2
    arrays = []
    for key in range(layout.ctx):
        own = held[key]
        if behind is not None:
            own = lax.optimization_barrier((own, behind))[0]
        found = [(own, (0, 0, key))]
        if layout.columns == 4:
            by_x = exchange(own, "dp", 2)
            by_y = exchange(own, "dp", 4)
            if key % 2:
                across = exchange(by_y, "dp", 2)
            else:
                across = exchange(by_x, "dp", 4)
            found += [(by_x, (1, 0, key)), (by_y, (2, 0, key)), (across, (3, 0, key))]
        else:
            bit = 1
            while bit < layout.columns:
                found += [
                    (exchange(array, "dp", 2 * bit), (place[0] ^ bit, 0, key))
                    for array, place in found
                ]
                bit *= 2
        arrays += found
    last = arrays[-2][0]
    arrays += [(exchange(array, "dp", 1), (place[0], 1, place[2])) for array, place in arrays]
    return arrays, held[layout.ctx - 1], last


def scatter(layout, kept, sent):
    received = exchange(sent, "dp", 1)
    half = kept.shape[0] // layout.columns // 2
    parts = lax.optimization_barrier(
        [
            add(kept[index * half : (index + 1) * half], received[index * half : (index + 1) * half])
            for index in range(2 * layout.columns)
        ]
    )
    first_parts = parts
    if layout.columns == 4:
        low = add(parts[2], exchange(parts[6], "dp", 4))
        high = add(parts[5], exchange(parts[7], "dp", 2))
        over_x = exchange(parts[3], "dp", 2)
        over_y = exchange(parts[4], "dp", 4)
        low, high = (exchange(low, "dp", 2), exchange(high, "dp", 4))
        summed = [add(parts[0], low, over_y), add(parts[1], over_x, high)]
    else:
        bit = layout.columns
        while bit > 1:
            parts = [
                add(parts[index], exchange(parts[index ^ bit], "dp", bit))
                for index in range(bit)
            ]
            bit //= 2
        summed = parts
    each = layout.ctx // 2
    length = half // each
    held = {
        key: summed[key // each][(key % each) * length : (key % each + 1) * length]
        for key in range(layout.ctx)
    }
    bit = 1
    while bit < layout.ctx:
        for key in [key for key in held if key & bit]:
            moved = exchange(held.pop(key), "ctx", bit)
            held[key ^ bit] = add(held[key ^ bit], moved)
        bit *= 2
    return held[0], first_parts


def bits(layout):
    found = []
    for unit, size in ((1, layout.ctx), (2 * layout.ctx, layout.columns), (layout.ctx, 2)):
        bit = 1
        while bit < size:
            found.append(bit * unit)
            bit *= 2
    return found


def everywhere(layout, array, bit):
    if bit < layout.ctx:
        return exchange(array, "ctx", bit)
    return exchange(array, "dp", bit // layout.ctx)


def broadcast(layout, shard, sources):
    held = jnp.concatenate([rows for _, rows in sources])
    owner = jnp.concatenate(
        [jnp.full((rows.shape[0], 1), source, jnp.int32) for source, rows in sources]
    )
    for bit in reversed(bits(layout)):
        other = everywhere(layout, held, bit)
        held = jnp.where(((owner ^ shard) & bit) == 0, held, other)
    return held


def sum_all(layout, held):
    for bit in reversed(bits(layout)):
        held = add(held, everywhere(layout, held, bit))
    return held


SWEEP = 512


def align(layout, place, params, before):
    length = layout.columns * layout.piece
    steps = pl.cdiv(layout.rows, SWEEP)
    held = max(TILE + steps * SWEEP, TILE + length)
    vector_first = ROW_VEC - layout.start(layout.devices - 1)
    assert 0 <= vector_first and vector_first + VEC_ROWS <= length
    starts = max(rows for _, rows in layout.leftover())

    def kernel(place_ref, rows, previous, *refs):
        outputs, wide = (refs[:-1], refs[-1])
        step = pl.program_id(0)

        @pl.when(step == 0)
        def _():
            wide[0:TILE, :] = previous[...]

        base = pl.multiple_of(TILE + step * SWEEP, TILE)
        wide[pl.ds(base, SWEEP), :] = rows[...].reshape(SWEEP, LANES)

        @pl.when(step == steps - 1)
        def _():
            first = TILE - place_ref[3]
            for key in range(layout.columns):
                row = first + jnp.bitwise_xor(place_ref[0], key) * layout.piece
                outputs[key][...] = wide[pl.ds(row, layout.piece), :].astype(BF)
            outputs[-2][...] = wide[pl.ds(first, starts), :].astype(BF)
            outputs[-1][...] = wide[pl.ds(first + vector_first, VEC_ROWS), :].astype(BF)

    heights = [layout.piece] * layout.columns + [starts, VEC_ROWS]
    return pl.pallas_call(
        kernel,
        name="align",
        grid=(steps,),
        in_specs=[
            pl.BlockSpec(memory_space=pltpu.SMEM),
            pl.BlockSpec((1, SWEEP * LANES), lambda i: (0, i)),
            pl.BlockSpec((TILE, LANES), lambda i: (0, 0)),
        ],
        out_specs=[pl.BlockSpec((height, LANES), lambda i: (0, 0)) for height in heights],
        out_shape=[jax.ShapeDtypeStruct((height, LANES), BF) for height in heights],
        scratch_shapes=[pltpu.VMEM((held, LANES), F32)],
        compiler_params=pltpu.CompilerParams(vmem_limit_bytes=VMEM_LIMIT),
    )(place, params, before)


def finish(layout, place, pieces, small, params, first, second):
    length = layout.columns * layout.piece
    steps = pl.cdiv(layout.rows, SWEEP)
    held = max(length, TILE + steps * SWEEP)
    vector_first = ROW_VEC - layout.start(layout.devices - 1)
    columns = layout.columns
    extra = sum(rows for _, rows in layout.leftover())

    def kernel(place_ref, *refs):
        sums, refs = (refs[:columns], refs[columns:])
        rest, master, one, two, grads, new, new_one, new_two, wide = refs
        step = pl.program_id(0)
        shard = place_ref[4]

        @pl.when(step == 0)
        def _():
            for key in range(columns):
                row = jnp.bitwise_xor(place_ref[0], key) * layout.piece
                row = pl.multiple_of(row, TILE)
                wide[pl.ds(row, layout.piece), :] = sums[key][...].astype(F32)
            used = 0
            for owner, rows in layout.leftover():

                @pl.when(shard == owner)
                def _(used=used, rows=rows):
                    wide[pl.ds(0, rows), :] += rest[pl.ds(used, rows), :].astype(F32)

                used += rows

            @pl.when(shard == layout.devices - 1)
            def _():
                wide[pl.ds(vector_first, VEC_ROWS), :] += rest[pl.ds(extra, VEC_ROWS), :].astype(F32)

        grad = wide[pl.ds(place_ref[3] + step * SWEEP, SWEEP), :]
        row = lax.broadcasted_iota(jnp.int32, (SWEEP, LANES), 0)
        matrix_part = row < ROW_VEC - shard * layout.rows - step * SWEEP
        results = adam_update(
            master[...].reshape(SWEEP, LANES),
            grad,
            one[...].reshape(SWEEP, LANES),
            two[...].reshape(SWEEP, LANES),
            matrix_part,
        )
        for ref, result in zip((grads, new, new_one, new_two), (grad,) + results):
            ref[...] = result.reshape(1, SWEEP * LANES)

    flat = pl.BlockSpec((1, SWEEP * LANES), lambda i: (0, i))

    def whole(array):
        return pl.BlockSpec(array.shape, lambda i: (0, 0))

    return pl.pallas_call(
        kernel,
        name="finish",
        grid=(steps,),
        in_specs=[pl.BlockSpec(memory_space=pltpu.SMEM)]
        + [whole(piece) for piece in pieces]
        + [whole(small), flat, flat, flat],
        out_specs=[flat] * 4,
        out_shape=[jax.ShapeDtypeStruct(params.shape, F32)] * 4,
        scratch_shapes=[pltpu.VMEM((held, LANES), F32)],
        compiler_params=pltpu.CompilerParams(vmem_limit_bytes=VMEM_LIMIT),
    )(place, *pieces, small, params, first, second)


def shards(layout, inputs, counts, params, first_moment, second_moment, out_cotangent):
    local_rows = inputs.shape[1]
    shard = lax.axis_index(("dp", "ctx"))
    score_scale = HD ** (-0.5)
    chunk = 256

    column = lax.axis_index("dp") // 2
    offset = (shard * layout.rows) % TILE
    place = jnp.stack(
        [column, lax.axis_index("dp") % 2, lax.axis_index("ctx"), offset, shard]
    ).astype(jnp.int32)
    last = layout.devices - 1
    ending = params[0, -TILE * LANES :].reshape(TILE, LANES)
    before = lax.ppermute(ending, ("dp", "ctx"), [(index, index + 1) for index in range(last)])
    aligned = align(layout, place, params, before)
    shares = list(aligned[:1]) + [
        exchange(aligned[key], "dp", 2 * key) for key in range(1, layout.columns)
    ]
    groups = [
        pick(column, [shares[index ^ position] for position in range(layout.columns)])
        for index in range(layout.columns)
    ]
    gathered_first, along, behind = gather(layout, jnp.concatenate(groups[: layout.first]))
    shared_rest = jnp.concatenate(groups[layout.first :])
    shared_rest = lax.optimization_barrier((shared_rest, along))[0]
    gathered_rest, _, _ = gather(layout, shared_rest, behind)
    sources = [(owner, aligned[-2][:rows]) for owner, rows in layout.leftover()]
    spread = broadcast(layout, shard, sources + [(last, aligned[-1])])
    leftover, spread = (spread[:-VEC_ROWS], spread[-VEC_ROWS:])
    flat_vectors = spread.reshape(-1).astype(F32)
    vectors = []
    used = 0
    for length in VEC_LENGTHS:
        vectors.append(flat_vectors[used : used + length])
        used += length
    (
        gain_one,
        shift_one,
        bias_query,
        bias_value,
        bias_out,
        gain_two,
        shift_two,
        bias_down,
        bias_up,
    ) = vectors

    residual = inputs[0].astype(F32)
    unit_one, inverse_one = norm_forward(residual)
    normed_round = (unit_one * gain_one + shift_one).astype(BF)
    qkv_weight = first_weights(layout, place, gathered_first, leftover)
    projected = dense(normed_round, qkv_weight)
    queries = ((projected[:, :D] + bias_query) * score_scale).astype(BF)
    keys = projected[:, D : 2 * D].astype(BF)
    values = (projected[:, 2 * D :] + bias_value).astype(BF)
    packed = to_heads(jnp.concatenate([queries, keys, values], -1), 3)
    out_weight, up_weight, down_weight = other_weights(layout, place, gathered_rest)
    mixed_heads, log_total = attend(counts, place, packed, chunk)
    mixed = from_heads(mixed_heads, 1)
    middle = residual + dense(mixed, out_weight) + bias_out
    unit_two, inverse_two = norm_forward(middle)
    normed_two_round = (unit_two * gain_two + shift_two).astype(BF)
    pre_gelu = dense(normed_two_round, up_weight) + bias_up
    activated = jax.nn.gelu(pre_gelu, approximate=True).astype(BF)

    positions = lax.axis_index("ctx") * local_rows + jnp.arange(local_rows, dtype=jnp.int32)
    row_valid = (positions < counts[0])[:, None].astype(F32)
    grad_next = out_cotangent[0] * row_valid
    grad_bias_down = jnp.sum(grad_next, 0)
    grad_round = grad_next.astype(BF)
    grad_down = t_dot(activated, grad_round).astype(BF)
    grad_act = dot_t(grad_round, down_weight)
    gelu_back = jax.vjp(functools.partial(jax.nn.gelu, approximate=True), pre_gelu)[1]
    grad_pre = gelu_back(grad_act)[0]
    grad_bias_up = jnp.sum(grad_pre, 0)
    grad_pre_round = grad_pre.astype(BF)
    grad_up = t_dot(normed_two_round, grad_pre_round).astype(BF)
    middle_group = layout.columns // 2
    terms = gradient_pieces(
        layout, place, (middle_group, layout.columns), {"up": grad_up, "down": grad_down}
    )
    grad_pre_round, terms = lax.optimization_barrier((grad_pre_round, terms))
    sum_last, _ = scatter(layout, *terms)
    grad_normed_two = dot_t(grad_pre_round, up_weight)
    grad_gain_two = jnp.sum(grad_normed_two * unit_two, 0)
    grad_shift_two = jnp.sum(grad_normed_two, 0)
    grad_middle = grad_next + norm_back(grad_normed_two, unit_two, inverse_two, gain_two)
    grad_bias_out = jnp.sum(grad_middle, 0)
    middle_round = grad_middle.astype(BF)
    grad_out = t_dot(mixed, middle_round).astype(BF)
    grad_mixed = dot_t(middle_round, out_weight).astype(BF)
    grad_mixed_heads = to_heads(grad_mixed, 1)
    terms = gradient_pieces(
        layout, place, (layout.first, middle_group), {"out": grad_out, "up": grad_up}
    )
    sum_middle, _ = scatter(layout, *terms)
    grad_packed, sums = attend_back(
        counts, place, packed, log_total, grad_mixed_heads, chunk
    )
    grad_projected = from_heads(grad_packed, 3)
    grad_qkv = t_dot(normed_round, grad_projected).astype(BF)
    *terms, leftover_terms = gradient_pieces(
        layout, place, (0, layout.first), {"qkv": grad_qkv}, leftover=True
    )
    grad_projected, leftover_terms, *terms = lax.optimization_barrier(
        (grad_projected, leftover_terms, *terms)
    )
    sum_first, kept_first = scatter(layout, *terms)
    grad_projected, activated, _ = lax.optimization_barrier(
        (grad_projected, activated, kept_first)
    )
    output = (middle + dense(activated, down_weight) + bias_down).astype(BF)
    grad_normed_one = dot_t(grad_projected, qkv_weight)
    grad_gain_one = jnp.sum(grad_normed_one * unit_one, 0)
    grad_shift_one = jnp.sum(grad_normed_one, 0)
    input_grad = grad_middle + norm_back(grad_normed_one, unit_one, inverse_one, gain_one)

    share = D // layout.ctx
    where = (lax.axis_index("ctx") * share,)
    sum_q, sum_v = (sums[:, 0].reshape(-1), sums[:, 1].reshape(-1))
    grad_bias_query = lax.dynamic_update_slice(jnp.zeros((D,), F32), sum_q, where)
    grad_bias_value = lax.dynamic_update_slice(jnp.zeros((D,), F32), sum_v, where)
    vector_terms = [
        grad_gain_one,
        grad_shift_one,
        grad_bias_query,
        grad_bias_value,
        grad_bias_out,
        grad_gain_two,
        grad_shift_two,
        grad_bias_down,
        grad_bias_up,
    ]
    padding = jnp.zeros((VEC_ROWS * LANES - sum(VEC_LENGTHS),), F32)
    vector_grads = jnp.concatenate(vector_terms + [padding]).reshape(VEC_ROWS, LANES)
    small_terms = jnp.concatenate([leftover_terms, vector_grads.astype(BF)])
    small_sum = sum_all(layout, small_terms)

    summed = jnp.concatenate([sum_first, sum_middle, sum_last])
    summed = summed.reshape(layout.columns, layout.piece, LANES)
    pieces = [
        lax.dynamic_index_in_dim(summed, column ^ key, keepdims=False)
        for key in range(layout.columns)
    ]
    pieces = pieces[:1] + [exchange(pieces[key], "dp", 2 * key) for key in range(1, layout.columns)]
    param_grads, new_params, new_first, new_second = finish(
        layout, place, pieces, small_sum, params, first_moment, second_moment
    )
    return (output[None], input_grad[None], param_grads, new_params, new_first, new_second)


def solution(mesh):
    placed = (
        P("dp", "ctx", None),
        P("dp"),
        P(None, ("dp", "ctx")),
        P(None, ("dp", "ctx")),
        P(None, ("dp", "ctx")),
        P("dp", "ctx", None),
    )
    dp, ctx = (mesh.shape["dp"], mesh.shape["ctx"])

    def program(inputs, counts, params, first_moment, second_moment, out_cotangent):
        layout = Layout(dp, ctx, params.shape[1] // (dp * ctx))

        def body(*arguments):
            return shards(layout, *arguments)

        return jax.shard_map(
            body,
            mesh=mesh,
            in_specs=placed,
            out_specs=(
                P("dp", "ctx", None),
                P("dp", "ctx", None),
                P(None, ("dp", "ctx")),
                P(None, ("dp", "ctx")),
                P(None, ("dp", "ctx")),
                P(None, ("dp", "ctx")),
            ),
            check_vma=False,
        )(inputs, counts, params, first_moment, second_moment, out_cotangent)

    return program
```
